32 devices in a mesh: dp: 16 (over z, y, core), tp: 2 (over x).
Axes of the slice: x: 2, y: 2, z: 4, core: 2. Of those that a mesh axis runs over, the one named last changes fastest.
Arguments:
- layer_in: bfloat16 [16, 1024, 2048], P('dp', 'tp'), may hold values from -6 to 6
- cotangent: bfloat16 [16, 1024, 2048], P('dp', 'tp'), may hold values from -6 to 6
- resets: int32 [16, 1024], P('dp', 'tp'), may hold values 0 or 1
- norm_gains: float32 [2, 2048], replicated, may hold values from 0.5 to 1.5
- w_x: bfloat16 [2048, 2560], P(None, 'tp'), may hold values from -0.125 to 0.125
- w_y: bfloat16 [2048, 2560], P(None, 'tp'), may hold values from -0.125 to 0.125
- conv_w: float32 [4, 2560], replicated, may hold values from -3 to 3
- lru_bias: float32 [3, 2560], replicated, may hold values from -3 to 3
- a_param: float32 [2560], replicated, may hold values from -10.4 to -5.3
- gate_blocks: bfloat16 [2, 10, 256, 256], replicated, may hold values from -0.375 to 0.375
- w_out: bfloat16 [2560, 2048], P('tp'), may hold values from -0.25 to 0.25
- w_gate: bfloat16 [2048, 6144], P(None, 'tp'), may hold values from -0.125 to 0.125
- w_up: bfloat16 [2048, 6144], P(None, 'tp'), may hold values from -0.125 to 0.125
- w_down: bfloat16 [6144, 2048], P('tp'), may hold values from -0.078125 to 0.078125
Outputs:
- layer_out: bfloat16 [16, 1024, 2048], P('dp', 'tp')
- input_grad: float32 [16, 1024, 2048], P('dp', 'tp')
- norm_gains_grad: float32 [2, 2048], P(None, 'dp')
- w_x_grad: float32 [2048, 2560], P('dp', 'tp')
- w_y_grad: float32 [2048, 2560], P('dp', 'tp')
- conv_w_grad: float32 [4, 2560], P(None, 'dp')
- lru_bias_grad: float32 [3, 2560], P(None, 'dp')
- a_param_grad: float32 [2560], P('dp')
- gate_blocks_grad: float32 [2, 10, 256, 256], P(None, None, 'dp')
- w_out_grad: float32 [2560, 2048], P('tp', 'dp')
- w_gate_grad: float32 [2048, 6144], P('dp', 'tp')
- w_up_grad: float32 [2048, 6144], P('dp', 'tp')
- w_down_grad: float32 [6144, 2048], P('tp', 'dp')
The draws below stay inside these ranges and needn't reach their ends.
All inputs are finite; a program needn't handle non-finite values. No bound on the sum of `resets` on one device may be relied on, other than what follows from the above.
Results may differ from the reference program's by a relative error of at most 0.02.
Values may be sent and summed in bfloat16 or wider, within the bound.
A program may use at most 448 MiB of HBM per device.

```python
import math
import jax
import jax.numpy as jnp
from jax import lax

D = 2048
H = 10
B = 256
FF = 6144
K = 4
W = 2560
LEN = 1024
SEQS = 16


def set_ends(values, stream_key, smallest, high):
    index_at = [jax.random.randint(jax.random.fold_in(stream_key, axis), (), 0, length) for axis, length in enumerate(values.shape)]
    widest = values.shape.index(max(values.shape))
    next_to = index_at[:widest] + [(index_at[widest] + 1) % values.shape[widest]] + index_at[widest + 1:]
    return values.at[tuple(index_at)].set(smallest).at[tuple(next_to)].set(high)


def steps_of(key, dims, shards, smallest, high):
    loudness = 1.0
    for axis_at, blocks in shards:
        draws = jax.random.uniform(jax.random.fold_in(jax.random.fold_in(key, 6), axis_at), (blocks,), jnp.float32, smallest / len(shards), high / len(shards))
        loudness = loudness * jnp.repeat(jnp.exp(draws), dims[axis_at] // blocks).reshape((-1,) + (1,) * (len(dims) - 1 - axis_at))
    return loudness


def scatter_about(stream_key, shape, width, limit, cuts=(), dtype=jnp.bfloat16):
    entries = width * jax.random.normal(stream_key, shape, jnp.float32)
    if cuts:
        entries = entries * steps_of(stream_key, shape, cuts, -0.22, 0.18)
    return jnp.clip(entries, -limit, limit).astype(dtype)


def setup_inputs(seed: int = 0) -> dict:
    arg_keys = jax.random.split(jax.random.key(seed), 15)
    return {
        "layer_in": scatter_about(arg_keys[0], (SEQS, LEN, D), 1.0, 6.0, ((0, 16), (1, 2))),
        "cotangent": scatter_about(arg_keys[1], (SEQS, LEN, D), 1.0, 6.0, ((0, 16), (1, 2))),
        "resets": set_ends((jax.random.randint(arg_keys[2], (SEQS, LEN), 0, LEN // 4) < 1).astype(jnp.int32), jax.random.fold_in(arg_keys[2], 1), 0, 1),
        "norm_gains": jnp.clip(1.0 + 0.1 * jax.random.normal(arg_keys[3], (2, D), jnp.float32), 0.5, 1.5),
        "w_x": scatter_about(arg_keys[4], (D, W), D ** -0.5, 0.125, ((1, 2),)),
        "w_y": scatter_about(arg_keys[5], (D, W), D ** -0.5, 0.125, ((1, 2),)),
        "conv_w": scatter_about(arg_keys[6], (K, W), 0.5, 3.0, (), jnp.float32),
        "lru_bias": scatter_about(arg_keys[7], (3, W), 0.5, 3.0, (), jnp.float32),
        "a_param": jnp.clip(jax.random.uniform(arg_keys[8], (W,), jnp.float32, -10.4, -5.3), -10.4, -5.3),
        "gate_blocks": scatter_about(arg_keys[9], (2, H, B, B), B ** -0.5, 0.375),
        "w_out": scatter_about(arg_keys[10], (W, D), (W // 4) ** -0.5, 0.25, ((0, 2),)),
        "w_gate": scatter_about(arg_keys[11], (D, FF), D ** -0.5, 0.125, ((1, 2),)),
        "w_up": scatter_about(arg_keys[12], (D, FF), D ** -0.5, 0.125, ((1, 2),)),
        "w_down": scatter_about(arg_keys[13], (FF, D), FF ** -0.5, 0.078125, ((0, 2),)),
    }


@jax.custom_vjp
def low(v):
    return lax.optimization_barrier(v.astype(jnp.bfloat16)).astype(jnp.float32)

@jax.custom_vjp
def low_back(v):
    return v

def low_keep(v):
    return (low(v), None)

def low_pass(kept, grad):
    return (grad,)

def back_keep(v):
    return (v, None)

def back_low(kept, grad):
    return (low(grad),)
low.defvjp(low_keep, low_pass)
low_back.defvjp(back_keep, back_low)
EPS = 1e-06
HIGHEST = lax.Precision.HIGHEST

def matmul(first_mat, second_mat):
    return jnp.dot(first_mat, second_mat, precision=HIGHEST, preferred_element_type=jnp.float32)

def rms_scale(values, gain_vec):
    return values * lax.rsqrt(lax.optimization_barrier(jnp.mean(values * values, axis=-1, keepdims=True)) + EPS) * gain_vec

def lru_terms(conv_out, gate_in, gate_rate, a_param, starts):
    keep_mask = 1.0 - starts
    input_gate = jax.nn.sigmoid(gate_in)
    rate_gate = jax.nn.sigmoid(gate_rate)
    log_decay = -8.0 * rate_gate * jax.nn.softplus(a_param)
    scaling = starts + keep_mask * jnp.sqrt(-jnp.expm1(2.0 * log_decay))
    return (jnp.exp(log_decay) * keep_mask, conv_out * input_gate * scaling)

def delayed(values, offset):
    padding = [(0, 0)] * values.ndim
    padding[1] = (offset, 0)
    return jnp.pad(values, padding)[:, :values.shape[1]]

def layer(inputs, norm_gains, w_x, w_y, conv_w, lru_bias, a_param, gate_blocks, w_out, w_gate, w_up, w_down, starts):
    groups, length, model_width = inputs.shape
    keep_mask = 1.0 - starts
    normed = low(rms_scale(inputs, norm_gains[0])).reshape(groups * length, model_width)
    branch_x = low(low_back(matmul(normed, w_x))).reshape(groups, length, -1)
    branch_y = low_back(matmul(normed, w_y)).reshape(groups, length, -1)
    conv_sum = conv_w[0] * branch_x
    valid_mask = keep_mask
    for offset in range(1, K):
        conv_sum = conv_sum + valid_mask[..., None] * conv_w[offset] * delayed(branch_x, offset)
        valid_mask = valid_mask * delayed(keep_mask, offset)
    conv_out = low(conv_sum + lru_bias[0])
    blocks = conv_out.reshape(groups, length, H, B)
    gate_in = low_back(jnp.einsum('gshb,hbc->gshc', blocks, gate_blocks[0], precision=HIGHEST).reshape(groups, length, -1) + lru_bias[1])
    gate_rate = low_back(jnp.einsum('gshb,hbc->gshc', blocks, gate_blocks[1], precision=HIGHEST).reshape(groups, length, -1) + lru_bias[2])
    decay_rate, pushed = lru_terms(conv_out, gate_in, gate_rate, a_param, starts[..., None])

    def advance(carried, step_item):
        carried = step_item[0] * carried + step_item[1]
        return (carried, carried)
    start_state = jnp.zeros((groups, decay_rate.shape[2]), jnp.float32)
    _, states = lax.scan(advance, start_state, (jnp.swapaxes(decay_rate, 0, 1), jnp.swapaxes(pushed, 0, 1)))
    states = jnp.swapaxes(states, 0, 1)
    gated_out = low(states * jax.nn.gelu(branch_y, approximate=True)).reshape(groups * length, -1)
    recurrent = low_back(matmul(gated_out, w_out)).reshape(groups, length, model_width)
    middle = inputs + recurrent
    normed_two = low(rms_scale(middle, norm_gains[1])).reshape(groups * length, model_width)
    gate_val = low_back(matmul(normed_two, w_gate))
    up_val = low_back(matmul(normed_two, w_up))
    hidden = low(jax.nn.gelu(gate_val, approximate=True) * up_val)
    mlp_out = low_back(matmul(hidden, w_down)).reshape(groups, length, model_width)
    return middle + mlp_out

def reference(layer_in, cotangent, resets, norm_gains, w_x, w_y, conv_w, lru_bias, a_param, gate_blocks, w_out, w_gate, w_up, w_down):
    params = tuple((weight.astype(jnp.float32) for weight in (norm_gains, w_x, w_y, conv_w, lru_bias, a_param, gate_blocks, w_out, w_gate, w_up, w_down)))
    per_block = math.gcd(SEQS, max(1, 4096 // LEN))
    count_blocks = SEQS // per_block
    layer_blocks = layer_in.astype(jnp.float32).reshape(count_blocks, per_block, LEN, D)
    cot_blocks = cotangent.astype(jnp.float32).reshape(count_blocks, per_block, LEN, D)
    flag_blocks = resets.astype(jnp.float32).reshape(count_blocks, per_block, LEN)

    def block_step(totals, block_item):
        block_x, block_cot, block_flags = block_item

        def forward(inputs, *weights):
            return layer(inputs, *weights, block_flags)
        result, pullback = jax.vjp(forward, block_x, *params)
        grad_list = pullback(block_cot)
        totals = tuple((total_val + grad_val for total_val, grad_val in zip(totals, grad_list[1:])))
        return (totals, (result.astype(jnp.bfloat16), grad_list[0]))
    zero_grads = tuple((jnp.zeros_like(weight) for weight in params))
    totals, (out_blocks, grad_blocks) = lax.scan(block_step, zero_grads, (layer_blocks, cot_blocks, flag_blocks))
    return (out_blocks.reshape(SEQS, LEN, D), grad_blocks.reshape(SEQS, LEN, D), totals[0], totals[1], totals[2], totals[3], totals[4], totals[5], totals[6], totals[7], totals[8], totals[9], totals[10])
```

```python
import functools

import jax
import jax.numpy as jnp
from jax import lax
from jax.experimental import pallas as pl
from jax.experimental.pallas import tpu as pltpu
from jax.sharding import PartitionSpec as P

EPS = 1e-06
F32, BF16 = jnp.float32, jnp.bfloat16
STEP = 64
GELU_A, GELU_B = 0.7978845608028654, 0.044715


def one_minus_exp(value, exp_neg):
    series = 1.0 / 5040.0
    for term in (-1.0 / 720.0, 1.0 / 120.0, -1.0 / 24.0, 1.0 / 6.0, -0.5, 1.0):
        series = series * value + term
    return jnp.where(value < 0.25, series * value, 1.0 - exp_neg)


def group_scan(coef, term, carry, reverse):
    rows, lanes = coef.shape
    groups = rows // 8
    coef = coef.reshape(groups, 8, lanes)
    term = term.reshape(groups, 8, lanes)
    row = lax.broadcasted_iota(jnp.int32, (1, 8, lanes), 1)
    for dist in (1, 2, 4):
        shift = 8 - dist if reverse else dist
        inside = row < 8 - dist if reverse else row >= dist
        coef_by = jnp.where(inside, pltpu.roll(coef, shift, 1), 1.0)
        term_by = jnp.where(inside, pltpu.roll(term, shift, 1), 0.0)
        term = term + coef * term_by
        coef = coef * coef_by
    parts = [None] * groups
    for group in reversed(range(groups)) if reverse else range(groups):
        parts[group] = term[group] + coef[group] * carry
        carry = parts[group][0:1] if reverse else parts[group][7:8]
    return jnp.concatenate(parts, axis=0), carry


def gate_setup(place, bx_own, bx_oth, mask_ref, prm_ref, gate_ref, xs, cs, pre):
    half = bx_own.shape[0]
    length = 2 * half
    lanes = bx_own.shape[1]
    xs[0:8, :] = jnp.zeros((8, lanes), F32)
    xs[pl.ds(pl.multiple_of(8 + place * half, 8), half), :] = bx_own[...].astype(F32)
    xs[pl.ds(pl.multiple_of(8 + (1 - place) * half, 8), half), :] = bx_oth[...].astype(F32)
    taps = [prm_ref[k : k + 1, :] for k in range(4)]
    bias = prm_ref[4:5, :]

    def conv_step(index, _):
        at = pl.multiple_of(index * STEP, STEP)
        window = xs[pl.ds(at, STEP + 8), :]
        mask = mask_ref[pl.ds(at, STEP), :]
        total = taps[0] * window[8 : 8 + STEP] + bias
        for k in (1, 2, 3):
            total = total + (mask[:, k : k + 1] * taps[k]) * window[8 - k : 8 - k + STEP]
        cs[pl.ds(at, STEP), :] = total.astype(BF16)
        return 0

    lax.fori_loop(0, length // STEP, conv_step, 0)

    def gate_step(index, _):
        rows = pl.ds(pl.multiple_of(index * 256, 256), 256)
        conv = cs[rows, :]
        pre[rows, 0:lanes] = jnp.dot(conv, gate_ref[0, 0], preferred_element_type=F32)
        pre[rows, lanes:] = jnp.dot(conv, gate_ref[1, 0], preferred_element_type=F32)
        return 0

    lax.fori_loop(0, length // 256, gate_step, 0)


def gate_terms(pre_rows, prm_ref, keep):
    lanes = pre_rows.shape[1] // 2
    in_gate = jax.nn.sigmoid(pre_rows[:, :lanes] + prm_ref[5:6, :])
    rate_gate = jax.nn.sigmoid(pre_rows[:, lanes:] + prm_ref[6:7, :])
    log_decay = prm_ref[7:8, :] * rate_gate
    decay = jnp.exp(log_decay)
    squared = decay * decay
    gap = one_minus_exp(-2.0 * log_decay, squared)
    return in_gate, rate_gate, decay, squared, gap


def own_rows(place, half):
    return pl.ds(pl.multiple_of(place * half, half), half), pl.ds(pl.multiple_of((1 - place) * half, half), half)


def rec_fwd_kernel(
    bx_own, bx_oth, by_own, by_oth, mask_ref, prm_ref, gate_ref, gated_own, gated_oth, state_ref, xs, cs, pre, ys, gated,
):
    place = lax.axis_index("tp")
    half, lanes = bx_own.shape
    own, oth = own_rows(place, half)
    gate_setup(place, bx_own, bx_oth, mask_ref, prm_ref, gate_ref, xs, cs, pre)
    ys[own, :] = by_own[...]
    ys[oth, :] = by_oth[...]

    def step(index, carry):
        rows = pl.ds(pl.multiple_of(index * STEP, STEP), STEP)
        keep = mask_ref[rows, :][:, 0:1]
        in_gate, _, decay, _, gap = gate_terms(pre[rows, :], prm_ref, keep)
        scaling = (1.0 - keep) + keep * jnp.sqrt(gap)
        pushed = cs[rows, :].astype(F32) * in_gate * scaling
        state, carry = group_scan(decay * keep, pushed, carry, False)
        state_ref[rows, :] = state
        y = ys[rows, :]
        tanh = jnp.tanh(GELU_A * (y + GELU_B * (y * y * y)))
        gated[rows, :] = (state * (0.5 * y * (1.0 + tanh))).astype(BF16)
        return carry

    lax.fori_loop(0, 2 * half // STEP, step, jnp.zeros((1, lanes), F32))
    gated_own[...] = gated[own, :]
    gated_oth[...] = gated[oth, :]


def fold(value):
    return jnp.sum(value.reshape(value.shape[0] // 8, 8, value.shape[1]), axis=0)


def rec_bwd_kernel(
    count, bits, bx_own, bx_oth, by_own, by_oth, state_ref, up_own, up_oth, mask_ref, prm_ref, gate_ref,
    gx_own, gx_oth, gy_own, gy_oth, gw_ref, sum_ref, xs, cs, pre, ys, up_ref, gx_ref, gy_ref, gw, dg, gc,
):
    place = lax.axis_index("tp")
    half, lanes = bx_own.shape
    length = 2 * half
    steps = length // STEP
    own, oth = own_rows(place, half)
    gate_setup(place, bx_own, bx_oth, mask_ref, prm_ref, gate_ref, xs, cs, pre)
    ys[own, :] = by_own[...]
    ys[oth, :] = by_oth[...]
    up_ref[own, :] = up_own[...]
    up_ref[oth, :] = up_oth[...]
    zero8 = jnp.zeros((8, lanes), F32)

    def step(index, carried):
        carry, sum_in, sum_rate, sum_log = carried
        rows = pl.ds(pl.multiple_of((steps - 1 - index) * STEP, STEP), STEP)
        keep = mask_ref[rows, :][:, 0:1]
        in_gate, rate_gate, decay, squared, gap = gate_terms(pre[rows, :], prm_ref, keep)
        inverse = lax.rsqrt(gap)
        scaling = (1.0 - keep) + keep * (gap * inverse)
        y = ys[rows, :]
        y2 = y * y
        tanh = jnp.tanh(GELU_A * y * (1.0 + GELU_B * y2))
        lift = 0.5 * (1.0 + tanh)
        slope = lift + (0.5 * GELU_A) * y * (1.0 - tanh * tanh) * (1.0 + (3.0 * GELU_B) * y2)
        up = up_ref[rows, :]
        state = state_ref[rows, :]
        gy_ref[rows, :] = (up * state * slope).astype(BF16)
        direct = up * (y * lift)
        coef = decay * keep
        sent, below = group_scan(coef, coef * direct, carry, True)
        shifted = jnp.concatenate([sent[1:], carry], axis=0)
        grad_state = direct + shifted
        entered = cs[rows, :].astype(F32) * in_gate
        pushed = entered * scaling
        grad_log = grad_state * ((state - pushed) - entered * (keep * squared * inverse))
        grad_in = (grad_state * pushed * (1.0 - in_gate)).astype(BF16)
        through = grad_log * rate_gate
        grad_rate = (through * (1.0 - rate_gate) * prm_ref[7:8, :]).astype(BF16)
        dg[rows, 0:lanes] = grad_in
        dg[rows, lanes:] = grad_rate
        gc[rows, :] = grad_state * in_gate * scaling
        return (
            below,
            sum_in + fold(grad_in.astype(F32)),
            sum_rate + fold(grad_rate.astype(F32)),
            sum_log + fold(through),
        )

    _, sum_in, sum_rate, sum_log = lax.fori_loop(
        0, steps, step, (jnp.zeros((1, lanes), F32), zero8, zero8, zero8)
    )
    gc[length : length + 8, :] = zero8

    def back_step(index, _):
        rows = pl.ds(pl.multiple_of(index * 256, 256), 256)
        gc[rows, :] += matmul_right(dg[rows, 0:lanes], gate_ref[0, 0]) + matmul_right(
            dg[rows, lanes:], gate_ref[1, 0]
        )
        return 0

    lax.fori_loop(0, length // 256, back_step, 0)
    gw[0:lanes, :] = matmul_left(cs[...], dg[:, 0:lanes]).astype(BF16)
    gw[lanes:, :] = matmul_left(cs[...], dg[:, lanes:]).astype(BF16)
    rows_each = lanes // count
    me = lax.axis_index("dp")
    for spot in range(count):
        block = block_from(me, spot, bits)
        for gate in (0, 1):
            source = pl.ds(pl.multiple_of(gate * lanes + block * rows_each, rows_each), rows_each)
            gw_ref[spot, 0, gate * rows_each : (gate + 1) * rows_each, :] = gw[source, :]
    taps = [prm_ref[k : k + 1, :] for k in range(4)]

    def conv_step(index, sums):
        at = pl.multiple_of(index * STEP, STEP)
        grad = gc[pl.ds(at, STEP + 8), :]
        window = xs[pl.ds(at, STEP + 8), :]
        mask = mask_ref[pl.ds(at, STEP + 8), :]
        here = grad[0:STEP]
        total = taps[0] * here
        sums = [sums[0] + fold(here), sums[1] + fold(here * window[8 : 8 + STEP])] + list(sums[2:])
        for k in (1, 2, 3):
            masked = grad * mask[:, k : k + 1]
            total = total + taps[k] * masked[k : k + STEP]
            sums[k + 1] = sums[k + 1] + fold(masked[0:STEP] * window[8 - k : 8 - k + STEP])
        gx_ref[pl.ds(at, STEP), :] = total.astype(BF16)
        return tuple(sums)

    sums = lax.fori_loop(0, steps, conv_step, (zero8,) * 5)
    for index, value in enumerate(sums[1:5] + (sums[0], sum_in, sum_rate, sum_log)):
        sum_ref[index : index + 1, :] = jnp.sum(value, axis=0, keepdims=True)
    for source, first, second in ((gx_ref, gx_own, gx_oth), (gy_ref, gy_own, gy_oth)):
        first[...] = source[own, :]
        second[...] = source[oth, :]


def rec_specs(half, lanes, length):
    piece = pl.BlockSpec((half, lanes), lambda h: (0, h))
    whole = pl.BlockSpec((length, lanes), lambda h: (0, h))
    mask = pl.BlockSpec((length + 8, 8), lambda h: (0, 0))
    prm = pl.BlockSpec((8, lanes), lambda h: (0, h))
    gate = pl.BlockSpec((2, 1, lanes, lanes), lambda h: (0, h, 0, 0))
    return piece, whole, mask, prm, gate


def rec_scratch(length, lanes):
    return [
        pltpu.VMEM((length + 8, lanes), F32),
        pltpu.VMEM((length, lanes), BF16),
        pltpu.VMEM((length, 2 * lanes), F32),
        pltpu.VMEM((length, lanes), F32),
    ]


def rec_fwd(bx_own, bx_oth, by_own, by_oth, mask, prm, gates):
    half, width = bx_own.shape
    length, lanes, heads = 2 * half, gates.shape[2], gates.shape[1]
    piece, whole, mask_spec, prm_spec, gate_spec = rec_specs(half, lanes, length)
    return pl.pallas_call(
        rec_fwd_kernel,
        grid=(heads,),
        in_specs=[piece] * 4 + [mask_spec, prm_spec, gate_spec],
        out_specs=[piece, piece, whole],
        out_shape=[
            jax.ShapeDtypeStruct((half, width), BF16),
            jax.ShapeDtypeStruct((half, width), BF16),
            jax.ShapeDtypeStruct((length, width), F32),
        ],
        scratch_shapes=rec_scratch(length, lanes) + [pltpu.VMEM((length, lanes), BF16)],
        compiler_params=pltpu.CompilerParams(vmem_limit_bytes=40 << 20),
        cost_estimate=pl.CostEstimate(
            flops=4 * length * width * lanes + 100 * length * width,
            bytes_accessed=16 * length * width,
            transcendentals=6 * length * width,
        ),
        name="rec_fwd",
    )(bx_own, bx_oth, by_own, by_oth, mask, prm, gates)


def rec_bwd(bx_own, bx_oth, by_own, by_oth, states, up_own, up_oth, mask, prm, gates, count):
    half, width = bx_own.shape
    length, lanes, heads = 2 * half, gates.shape[2], gates.shape[1]
    piece, whole, mask_spec, prm_spec, gate_spec = rec_specs(half, lanes, length)
    return pl.pallas_call(
        functools.partial(rec_bwd_kernel, count, stage_bits(count)),
        grid=(heads,),
        in_specs=[piece] * 4 + [whole, piece, piece, mask_spec, prm_spec, gate_spec],
        out_specs=[piece] * 4 + [pl.BlockSpec((count, 1, 2 * lanes // count, lanes), lambda h: (0, h, 0, 0)), prm_spec],
        out_shape=[jax.ShapeDtypeStruct((half, width), BF16)] * 4
        + [
            jax.ShapeDtypeStruct((count, heads, 2 * lanes // count, lanes), BF16),
            jax.ShapeDtypeStruct((8, width), F32),
        ],
        scratch_shapes=rec_scratch(length, lanes)
        + [
            pltpu.VMEM((length, lanes), F32),
            pltpu.VMEM((length, lanes), BF16),
            pltpu.VMEM((length, lanes), BF16),
            pltpu.VMEM((2 * lanes, lanes), BF16),
            pltpu.VMEM((length, 2 * lanes), BF16),
            pltpu.VMEM((length + 8, lanes), F32),
        ],
        compiler_params=pltpu.CompilerParams(vmem_limit_bytes=48 << 20),
        cost_estimate=pl.CostEstimate(
            flops=12 * length * width * lanes + 250 * length * width,
            bytes_accessed=24 * length * width,
            transcendentals=8 * length * width,
        ),
        name="rec_bwd",
    )(bx_own, bx_oth, by_own, by_oth, states, up_own, up_oth, mask, prm, gates)


def stage_bits(count):
    bits = count.bit_length() - 1
    return [1 << bit for bit in ([0, 1] + list(reversed(range(2, bits))))[:bits]]


def block_at(place, bits):
    return sum(bit for step, bit in enumerate(bits) if (place >> (len(bits) - 1 - step)) & 1)


def block_from(me, place, bits):
    relative = block_at(place, bits)
    block = 0
    for bit in bits:
        mine = lax.rem(me // bit, 2)
        block = block + bit * (1 - mine if relative & bit else mine)
    return block


def arrange_kernel(count, bits, steps, first, second, keep, send):
    me = lax.axis_index("dp")
    cols = first.shape[1] // count

    def move(piece):
        for place in range(count):
            source = pl.ds(pl.multiple_of(block_from(me, place, bits) * cols, cols), cols)
            into, spot = (keep, place) if place < count // 2 else (send, place - count // 2)
            into[:, spot * cols : (spot + 1) * cols] = piece[:, source]

    @pl.when(pl.program_id(0) < steps)
    def _():
        move(first)

    @pl.when(pl.program_id(0) >= steps)
    def _():
        move(second)


def arrange(first, second, count):
    half, width = first.shape
    steps = 2
    block = half // steps
    shape = jax.ShapeDtypeStruct((2 * half, width // 2), first.dtype)
    return pl.pallas_call(
        functools.partial(arrange_kernel, count, stage_bits(count), steps),
        grid=(2 * steps,),
        in_specs=[
            pl.BlockSpec((block, width), lambda i: (jnp.minimum(i, steps - 1), 0)),
            pl.BlockSpec((block, width), lambda i: (jnp.maximum(i - steps, 0), 0)),
        ],
        out_specs=[pl.BlockSpec((block, width // 2), lambda i: (i, 0))] * 2,
        out_shape=[shape, shape],
        cost_estimate=pl.CostEstimate(flops=0, bytes_accessed=8 * half * width, transcendentals=0),
        name="arrange",
    )(first, second)


def swap(value):
    return lax.ppermute(value, "tp", [(0, 1), (1, 0)])


def flip(value, bit):
    count = lax.axis_size("dp")
    return lax.ppermute(value, "dp", [(source, source ^ bit) for source in range(count)])


class Reduction:
    def __init__(self, keep, sent, bits):
        self.keep, self.bits = keep, list(bits)
        self.pass_on(sent)

    def pass_on(self, sent):
        self.sent = sent
        self.received = flip(sent, self.bits.pop(0))

    def step(self):
        middle = self.keep.shape[0] // 2
        keep, received = self.keep, self.received
        self.keep = (keep[:middle].astype(F32) + received[:middle].astype(F32)).astype(BF16)
        self.pass_on((keep[middle:].astype(F32) + received[middle:].astype(F32)).astype(BF16))
        return self.sent

    def total(self):
        return self.keep.astype(F32) + self.received.astype(F32)


def after(value, *others):
    return lax.optimization_barrier((value, *others))[0]


def sum_everywhere(value):
    value = value + swap(value)
    for bit in stage_bits(lax.axis_size("dp")):
        value = value + flip(value, bit)
    return value


def norm_back(values, gain, grad):
    scale = lax.rsqrt(jnp.mean(values * values, axis=-1, keepdims=True) + EPS)
    lifted = gain * grad
    pull = jnp.mean(values * lifted, axis=-1, keepdims=True)
    grad_values = scale * lifted - values * (scale * scale * scale * pull)
    return grad_values, grad * values * scale


def weight_grad(parts, right, bits):
    keep, send = parts
    sent = matmul_left(send, right).astype(BF16)
    kept = matmul_left(after(keep, sent), right).astype(BF16)
    return Reduction(kept, sent, bits)


def local_channels(
    layer_in, cotangent, resets, norm_gains, w_x, w_y, conv_w, lru_bias, a_param, gate_blocks, w_out, w_gate, w_up, w_down,
):
    place = lax.axis_index("tp")
    me = lax.axis_index("dp")
    count = lax.axis_size("dp")
    bits = stage_bits(count)
    width = w_x.shape[1]
    full_width = conv_w.shape[1]
    heads = gate_blocks.shape[1] // 2
    model = norm_gains.shape[1]

    own_in, own_cot = layer_in[0], cotangent[0]
    oth_in = swap(own_in)
    oth_resets = swap(resets[0])
    oth_cot = swap(own_cot)
    normed_own = rms_scale(own_in.astype(F32), norm_gains[0]).astype(BF16)
    bx_own = matmul(normed_own, w_x).astype(BF16)
    by_own = matmul(normed_own, w_y)

    first_place = place == 0
    in_time = jnp.where(first_place, resets[0], oth_resets), jnp.where(first_place, oth_resets, resets[0])
    keep = 1.0 - jnp.concatenate(in_time).astype(F32)
    keep_1 = jnp.concatenate([jnp.ones((1,), F32), keep[:-1]])
    keep_2 = jnp.concatenate([jnp.ones((1,), F32), keep_1[:-1]])
    valid = [keep, keep, keep * keep_1, keep * keep_1 * keep_2]
    mask = jnp.pad(jnp.stack(valid, axis=1), ((0, 8), (0, 4)))
    table = jnp.concatenate([conv_w, lru_bias, -8.0 * jax.nn.softplus(a_param)[None]], axis=0)
    prm = lax.dynamic_slice(table, (0, place * width), (8, width))
    gates = lax.dynamic_slice_in_dim(gate_blocks, place * heads, heads, axis=1)

    normed_oth = rms_scale(oth_in.astype(F32), norm_gains[0]).astype(BF16)
    bx_oth = matmul(normed_oth, w_x).astype(BF16)
    by_oth = matmul(normed_oth, w_y)
    gated_own, gated_oth, states = rec_fwd(bx_own, bx_oth, by_own, by_oth, mask, prm, gates)

    part_oth = matmul(gated_oth, w_out).astype(BF16)
    swap_own = swap(part_oth)
    part_own = matmul(after(gated_own, part_oth), w_out).astype(BF16)
    swap_oth = swap(part_own)
    cot_cols = arrange(after(own_cot, part_own), oth_cot, count)

    def feed_in(tokens, part, other):
        middle = tokens.astype(F32) + (part.astype(F32) + other.astype(F32))
        normed = rms_scale(middle, norm_gains[1]).astype(BF16)
        gate_val = matmul(normed, w_gate)
        up_val = matmul(normed, w_up)
        hidden_val, pull = jax.vjp(gelu_product, gate_val, up_val)
        return middle, normed, hidden_val.astype(BF16), pull

    def feed_back(cot, pull):
        grad_gate, grad_up = pull(matmul_right(cot, w_down))
        grad_gate, grad_up = grad_gate.astype(BF16), grad_up.astype(BF16)
        back = (matmul_right(grad_gate, w_gate) + matmul_right(grad_up, w_up)).astype(BF16)
        return grad_gate, grad_up, back

    def norm_two_back(middle, back, other, cot):
        grad, gain_rows = norm_back(middle, norm_gains[1], back.astype(F32) + other.astype(F32))
        grad = cot.astype(F32) + grad
        return grad, grad.astype(BF16), gain_rows

    middle_own, normed_two_own, hidden_own, pull_own = feed_in(own_in, part_own, swap_own)
    gg_own, gu_own, back_own = feed_back(own_cot, pull_own)
    back_own_swapped = swap(back_own)
    middle_oth, normed_two_oth, hidden_oth, pull_oth = feed_in(after(oth_in, back_own), part_oth, swap_oth)
    hidden = jnp.concatenate([hidden_own, hidden_oth], axis=0)
    down = weight_grad(cot_cols, hidden, bits)
    gg_oth, gu_oth, back_oth = feed_back(after(oth_cot, down.keep), pull_oth)
    back_oth_swapped = swap(back_oth)
    normed_two_own_late = after(normed_two_own, back_oth, down.step())
    normed_two_cols = arrange(normed_two_own_late, normed_two_oth, count)
    gate = weight_grad(normed_two_cols, jnp.concatenate([gg_own, gg_oth], axis=0), bits)
    keep_cols, send_cols = normed_two_cols
    up = weight_grad((keep_cols, after(send_cols, gate.keep)), jnp.concatenate([gu_own, gu_oth], axis=0), bits)
    hidden_late = after(hidden_oth, up.keep, gate.step())
    out_send = matmul(hidden_late, w_down).astype(BF16)
    out_swapped = swap(out_send)

    grad_own, rec_own, gain_rows = norm_two_back(after(middle_own, out_send, up.step()), back_own, back_oth_swapped, own_cot)
    gain_two = jnp.sum(gain_rows, axis=0)
    _, rec_oth, _ = norm_two_back(middle_oth, back_oth, back_own_swapped, oth_cot)
    up_own = matmul_right(rec_own, w_out)
    up_oth = matmul_right(rec_oth, w_out)
    gx_own, gx_oth, gy_own, gy_oth, gate_grad, sums = rec_bwd(
        bx_own, bx_oth, by_own, by_oth, states, up_own, up_oth, mask, prm, gates, count
    )

    def rec_back(piece_x, piece_y):
        return (matmul_right(piece_x, w_x) + matmul_right(piece_y, w_y)).astype(BF16)

    rec_cols = arrange(after(rec_own, gx_oth, down.step()), rec_oth, count)
    out = weight_grad(rec_cols, jnp.concatenate([gated_own, gated_oth], axis=0), bits)
    half_gates = count // 2
    blocks = Reduction(gate_grad[:half_gates], gate_grad[half_gates:], bits)
    normed_cols = arrange(after(normed_own, out.keep), normed_oth, count)
    keep_cols, send_cols = normed_cols
    in_x = weight_grad(normed_cols, jnp.concatenate([gx_own, gx_oth], axis=0), bits)
    in_y = weight_grad((keep_cols, after(send_cols, in_x.keep)), jnp.concatenate([gy_own, gy_oth], axis=0), bits)
    rec_send = rec_back(after(gx_oth, in_y.keep, out.step(), gate.step()), gy_oth)
    rec_swapped = swap(rec_send)
    sums = sums.at[7].multiply(-8.0 * lax.dynamic_slice(jax.nn.sigmoid(a_param), (place * width,), (width,)))
    wide = lax.dynamic_update_slice(jnp.zeros((8, full_width), F32), sums, (0, place * width))
    rec_keep = rec_back(after(gx_own, rec_send, in_x.step(), in_y.step(), blocks.step()), gy_own)
    out_keep = matmul(after(hidden_own, rec_keep, up.step()), w_down).astype(BF16)
    layer_out = (middle_own + out_keep.astype(F32) + out_swapped.astype(F32)).astype(BF16)
    grad_normed = rec_keep.astype(F32) + after(rec_swapped, out_keep).astype(F32)
    grad_inputs, gain_rows = norm_back(own_in.astype(F32), norm_gains[0], grad_normed)
    input_grad = grad_own + grad_inputs
    gain_one = jnp.sum(gain_rows, axis=0)
    packed = jnp.concatenate([wide.reshape(-1), gain_one, gain_two]).reshape(-1, 128)
    packed = sum_everywhere(packed).reshape(-1)
    for task in (down, blocks, out, gate, up, in_x, in_y) * 3:
        if task.bits:
            task.step()

    small = packed[: 8 * full_width].reshape(8, full_width)
    small = lax.dynamic_slice(small, (0, me * (full_width // count)), (8, full_width // count))
    gains = packed[8 * full_width :].reshape(2, model)
    gains = lax.dynamic_slice(gains, (0, me * (model // count)), (2, model // count))
    mine = blocks.total()[0].astype(BF16)
    others = swap(mine)
    mine = jnp.concatenate([jnp.where(first_place, mine, others), jnp.where(first_place, others, mine)], axis=0)
    mine = mine.astype(F32).reshape(2 * heads, 2, -1, mine.shape[-1])
    return (
        layer_out[None],
        input_grad[None],
        gains,
        in_x.total(),
        in_y.total(),
        small[0:4],
        small[4:7],
        small[7],
        jnp.swapaxes(mine, 0, 1),
        out.total().T,
        gate.total(),
        up.total(),
        down.total().T,
    )


def from_behind(value, axis, steps):
    count = lax.axis_size(axis)
    first, last = (max(0, -steps), min(count, count - steps))
    return lax.ppermute(value, axis, [(source, source + steps) for source in range(first, last)])


def rms_scale(values, gain_vec):
    return values * lax.rsqrt(jnp.mean(values * values, axis=-1, keepdims=True) + EPS) * gain_vec


def gelu_product(gate_val, up_val):
    return jax.nn.gelu(gate_val, approximate=True) * up_val


def lru_terms(conv_out, gate_in, gate_rate, a_param, starts):
    keep_mask = 1.0 - starts
    input_gate = jax.nn.sigmoid(gate_in)
    rate_gate = jax.nn.sigmoid(gate_rate)
    log_decay = -8.0 * rate_gate * jax.nn.softplus(a_param)
    scaling = starts + keep_mask * jnp.sqrt(-jnp.expm1(2.0 * log_decay))
    return (jnp.exp(log_decay) * keep_mask, conv_out * input_gate * scaling)


def matmul(first_mat, second_mat):
    return jnp.dot(first_mat, second_mat, preferred_element_type=jnp.float32)


def matmul_left(first_mat, second_mat):
    return lax.dot_general(
        first_mat, second_mat, (((0,), (0,)), ((), ())), preferred_element_type=jnp.float32
    )


def matmul_right(first_mat, second_mat):
    return lax.dot_general(
        first_mat, second_mat, (((1,), (1,)), ((), ())), preferred_element_type=jnp.float32
    )


def combine_state(first_item, second_item):
    return (first_item[0] * second_item[0], second_item[1] + second_item[0] * first_item[1])


def carry_across(coef_end, state_end, reverse):
    incoming = jnp.zeros_like(state_end)
    direction = -1 if reverse else 1
    for turn_index in range(lax.axis_size("tp") - 1):
        incoming = from_behind(state_end + coef_end * incoming, "tp", direction)
    return incoming


def local(
    layer_in,
    cotangent,
    resets,
    norm_gains,
    w_x,
    w_y,
    conv_w,
    lru_bias,
    a_param,
    gate_blocks,
    w_out,
    w_gate,
    w_up,
    w_down,
):
    inputs = layer_in[0].astype(jnp.float32)
    starts = resets[0].astype(jnp.float32)
    keep_mask = 1.0 - starts
    rim_size = conv_w.shape[0] - 1
    head_count = gate_blocks.shape[1]
    block_size = gate_blocks.shape[2]
    full_width = conv_w.shape[1]
    normed, norm_pull = jax.vjp(rms_scale, inputs, norm_gains[0])
    normed_low = normed.astype(jnp.bfloat16)
    proj_x, proj_y, proj_out = (
        lax.all_gather(w_x, "tp", axis=1, tiled=True),
        lax.all_gather(w_y, "tp", axis=1, tiled=True),
        lax.all_gather(w_out, "tp", axis=0, tiled=True),
    )
    rec_len = normed_low.shape[0]
    branch_x = matmul(normed_low, proj_x).astype(jnp.bfloat16)
    branch_y = matmul(normed_low, proj_y)
    rim_rows, rim_keep = from_behind(
        (branch_x[rec_len - rim_size :], keep_mask[rec_len - rim_size :].astype(jnp.bfloat16)),
        "tp",
        1,
    )
    padded_x = jnp.concatenate([rim_rows, branch_x], axis=0).astype(jnp.float32)
    padded_keep = jnp.concatenate([rim_keep.astype(jnp.float32), keep_mask])
    conv_sum = conv_w[0] * padded_x[rim_size:]
    valid_mask = keep_mask
    valid_list = []
    for offset in range(1, rim_size + 1):
        valid_list.append(valid_mask)
        conv_sum = (
            conv_sum
            + valid_mask[:, None]
            * conv_w[offset]
            * padded_x[rim_size - offset : rim_size - offset + rec_len]
        )
        valid_mask = valid_mask * padded_keep[rim_size - offset : rim_size - offset + rec_len]
    conv_out = (conv_sum + lru_bias[0]).astype(jnp.bfloat16)
    row_count = conv_out.shape[0]
    conv_blocks = conv_out.reshape(row_count, head_count, block_size)
    pre_rows = (
        jnp.einsum(
            "lhb,ghbc->glhc", conv_blocks, gate_blocks, preferred_element_type=jnp.float32
        ).reshape(2, row_count, full_width)
        + lru_bias[1:3][:, None, :]
    )
    gate_in = pre_rows[0]
    gate_rate = pre_rows[1]
    conv_float = conv_out.astype(jnp.float32)

    def lru_local(conv_in, in_pre, rate_pre, decay_in):
        return lru_terms(conv_in, in_pre, rate_pre, decay_in, starts[:, None])

    (decay_rate, pushed), lru_pull = jax.vjp(lru_local, conv_float, gate_in, gate_rate, a_param)
    decay_cum, local_states = lax.associative_scan(combine_state, (decay_rate, pushed), axis=0)
    incoming = carry_across(decay_cum[-1], local_states[-1], False)
    states = local_states + decay_cum * incoming
    gated_val, gated_pull = jax.vjp(gelu_product, branch_y, states)
    gated_low = gated_val.astype(jnp.bfloat16)
    recurrent = matmul(gated_low, proj_out)
    middle = inputs + recurrent
    normed_two, norm_two_pull = jax.vjp(rms_scale, middle, norm_gains[1])
    normed_two_low = normed_two.astype(jnp.bfloat16)
    group_rows = lax.all_gather(normed_two_low, "tp", axis=0, tiled=True)
    gate_val = matmul(group_rows, w_gate)
    up_val = matmul(group_rows, w_up)
    hidden_val, mlp_pull = jax.vjp(gelu_product, gate_val, up_val)
    hidden = hidden_val.astype(jnp.bfloat16)
    mlp_out = lax.psum_scatter(
        matmul(hidden, w_down).astype(jnp.bfloat16), "tp", scatter_dimension=0, tiled=True
    ).astype(jnp.float32)
    layer_out = (middle + mlp_out).astype(jnp.bfloat16)
    grad_out = cotangent[0].astype(jnp.float32)
    group_grad = lax.all_gather(cotangent[0], "tp", axis=0, tiled=True)
    w_down_grad = matmul_left(hidden, group_grad)
    grad_hidden = matmul_right(group_grad, w_down)
    grad_gate, grad_up = mlp_pull(grad_hidden)
    grad_gate = grad_gate.astype(jnp.bfloat16)
    grad_up = grad_up.astype(jnp.bfloat16)
    w_gate_grad = matmul_left(group_rows, grad_gate)
    w_up_grad = matmul_left(group_rows, grad_up)
    grad_normed_two = lax.psum_scatter(
        (matmul_right(grad_gate, w_gate) + matmul_right(grad_up, w_up)).astype(jnp.bfloat16),
        "tp",
        scatter_dimension=0,
        tiled=True,
    ).astype(jnp.float32)
    grad_middle, gain_two_grad = norm_two_pull(grad_normed_two)
    grad_middle = grad_middle + grad_out
    grad_rec = grad_middle.astype(jnp.bfloat16)
    grad_gated = matmul_right(grad_rec, proj_out)
    grad_branch_y, grad_direct = gated_pull(grad_gated)
    grad_branch_y = grad_branch_y.astype(jnp.bfloat16)
    decay_next = jnp.concatenate([decay_rate[1:], jnp.ones_like(decay_rate[:1])], axis=0)
    reach_back, local_grads = lax.associative_scan(
        combine_state, (decay_next, grad_direct), reverse=True, axis=0
    )
    outgoing = carry_across(decay_rate[0] * reach_back[0], decay_rate[0] * local_grads[0], True)
    state_grads = local_grads + reach_back * outgoing
    prior_states = jnp.concatenate([incoming[None], states[:-1]], axis=0)
    grad_conv, grad_in, grad_rate, a_local_grad = lru_pull(
        (state_grads * prior_states, state_grads)
    )
    grad_pre = jnp.stack([grad_in, grad_rate]).astype(jnp.bfloat16)
    pre_sums = jnp.sum(grad_pre.astype(jnp.float32), axis=1)
    pre_blocks = grad_pre.reshape(2, row_count, head_count, block_size)
    gate_blocks_grad = jnp.einsum(
        "lhb,glhc->ghbc", conv_blocks, pre_blocks, preferred_element_type=jnp.float32
    )
    gate_back = jnp.einsum(
        "glhc,ghbc->lhb", pre_blocks, gate_blocks, preferred_element_type=jnp.float32
    ).reshape(row_count, full_width)
    grad_conv = grad_conv + gate_back
    conv_w_rows = [jnp.sum(grad_conv * padded_x[rim_size:], axis=0)]
    grad_padded = (
        jnp.zeros((rec_len + rim_size, full_width), jnp.float32)
        .at[rim_size:]
        .add(conv_w[0] * grad_conv)
    )
    for offset in range(1, rim_size + 1):
        masked = valid_list[offset - 1][:, None] * grad_conv
        conv_w_rows.append(
            jnp.sum(masked * padded_x[rim_size - offset : rim_size - offset + rec_len], axis=0)
        )
        grad_padded = grad_padded.at[rim_size - offset : rim_size - offset + rec_len].add(
            conv_w[offset] * masked
        )
    returned = from_behind(grad_padded[:rim_size], "tp", -1)
    grad_x_branch = (
        grad_padded[rim_size:].at[rec_len - rim_size :].add(returned).astype(jnp.bfloat16)
    )
    conv_w_grad = jnp.stack(conv_w_rows)
    lru_bias_grad = jnp.concatenate([jnp.sum(grad_conv, axis=0)[None], pre_sums], axis=0)
    grad_normed = matmul_right(grad_x_branch, proj_x) + matmul_right(grad_branch_y, proj_y)
    grad_inputs, gain_one_grad = norm_pull(grad_normed)
    input_grad = grad_middle + grad_inputs
    w_x_grad, w_y_grad, w_out_grad = (
        lax.psum_scatter(
            matmul_left(normed_low, grad_x_branch).astype(jnp.bfloat16),
            "tp",
            scatter_dimension=1,
            tiled=True,
        ).astype(jnp.float32),
        lax.psum_scatter(
            matmul_left(normed_low, grad_branch_y).astype(jnp.bfloat16),
            "tp",
            scatter_dimension=1,
            tiled=True,
        ).astype(jnp.float32),
        lax.psum_scatter(
            matmul_left(gated_low, grad_rec).astype(jnp.bfloat16),
            "tp",
            scatter_dimension=0,
            tiled=True,
        ).astype(jnp.float32),
    )
    norm_gains_grad = jnp.stack([gain_one_grad, gain_two_grad])
    totals = (
        lax.psum_scatter(
            w_x_grad.astype(jnp.bfloat16), "dp", scatter_dimension=0, tiled=True
        ).astype(jnp.float32),
        lax.psum_scatter(
            w_y_grad.astype(jnp.bfloat16), "dp", scatter_dimension=0, tiled=True
        ).astype(jnp.float32),
        lax.psum_scatter(
            w_out_grad.astype(jnp.bfloat16), "dp", scatter_dimension=1, tiled=True
        ).astype(jnp.float32),
        lax.psum_scatter(
            w_gate_grad.astype(jnp.bfloat16), "dp", scatter_dimension=0, tiled=True
        ).astype(jnp.float32),
        lax.psum_scatter(
            w_up_grad.astype(jnp.bfloat16), "dp", scatter_dimension=0, tiled=True
        ).astype(jnp.float32),
        lax.psum_scatter(
            w_down_grad.astype(jnp.bfloat16), "dp", scatter_dimension=1, tiled=True
        ).astype(jnp.float32),
        lax.psum_scatter(
            norm_gains_grad.astype(jnp.bfloat16), "dp", scatter_dimension=1, tiled=True
        ).astype(jnp.float32),
        lax.psum_scatter(
            conv_w_grad.astype(jnp.bfloat16), "dp", scatter_dimension=1, tiled=True
        ).astype(jnp.float32),
        lax.psum_scatter(
            lru_bias_grad.astype(jnp.bfloat16), "dp", scatter_dimension=1, tiled=True
        ).astype(jnp.float32),
        lax.psum_scatter(
            a_local_grad.astype(jnp.bfloat16), "dp", scatter_dimension=0, tiled=True
        ).astype(jnp.float32),
        lax.psum_scatter(
            gate_blocks_grad.astype(jnp.bfloat16), "dp", scatter_dimension=2, tiled=True
        ).astype(jnp.float32),
    )
    reduced_small = (
        lax.psum(totals[6].astype(jnp.bfloat16), "tp").astype(jnp.float32),
        lax.psum(totals[7].astype(jnp.bfloat16), "tp").astype(jnp.float32),
        lax.psum(totals[8].astype(jnp.bfloat16), "tp").astype(jnp.float32),
        lax.psum(totals[9].astype(jnp.bfloat16), "tp").astype(jnp.float32),
        lax.psum(totals[10].astype(jnp.bfloat16), "tp").astype(jnp.float32),
    )
    return (
        layer_out[None],
        input_grad[None],
        reduced_small[0],
        totals[0],
        totals[1],
        reduced_small[1],
        reduced_small[2],
        reduced_small[3],
        reduced_small[4],
        totals[2],
        totals[3],
        totals[4],
        totals[5],
    )


def solution(mesh):
    rows, cols = mesh.shape["dp"], mesh.shape["tp"]
    by_channels = cols == 2 and rows >= 4 and rows & (rows - 1) == 0

    def step(*args):
        heads, model = args[9].shape[1], args[3].shape[1]
        fits = by_channels and heads % cols == 0 and model % (128 * rows) == 0
        return (local_channels if fits else local)(*args)

    return jax.shard_map(
        step,
        mesh=mesh,
        in_specs=(
            P("dp", "tp", None),
            P("dp", "tp", None),
            P("dp", "tp"),
            P(),
            P(None, "tp"),
            P(None, "tp"),
            P(),
            P(),
            P(),
            P(),
            P("tp", None),
            P(None, "tp"),
            P(None, "tp"),
            P("tp", None),
        ),
        out_specs=(
            P("dp", "tp", None),
            P("dp", "tp", None),
            P(None, "dp"),
            P("dp", "tp"),
            P("dp", "tp"),
            P(None, "dp"),
            P(None, "dp"),
            P("dp"),
            P(None, None, "dp", None),
            P("tp", "dp"),
            P("dp", "tp"),
            P("dp", "tp"),
            P("tp", "dp"),
        ),
        check_vma=False,
    )
```

```python
import functools

import jax
import jax.numpy as jnp
from jax import lax
from jax.experimental import pallas as pl
from jax.experimental.pallas import tpu as pltpu
from jax.sharding import PartitionSpec as P

EPS = 1e-06
F32, BF16 = jnp.float32, jnp.bfloat16
STEP = 64
GELU_A, GELU_B = 0.7978845608028654, 0.044715


def one_minus_exp(value, exp_neg):
    series = 1.0 / 5040.0
    for term in (-1.0 / 720.0, 1.0 / 120.0, -1.0 / 24.0, 1.0 / 6.0, -0.5, 1.0):
        series = series * value + term
    return jnp.where(value < 0.25, series * value, 1.0 - exp_neg)


def group_scan(coef, term, carry, reverse):
    rows, lanes = coef.shape
    groups = rows // 8
    coef = coef.reshape(groups, 8, lanes)
    term = term.reshape(groups, 8, lanes)
    row = lax.broadcasted_iota(jnp.int32, (1, 8, lanes), 1)
    for dist in (1, 2, 4):
        shift = 8 - dist if reverse else dist
        inside = row < 8 - dist if reverse else row >= dist
        coef_by = jnp.where(inside, pltpu.roll(coef, shift, 1), 1.0)
        term_by = jnp.where(inside, pltpu.roll(term, shift, 1), 0.0)
        term = term + coef * term_by
        coef = coef * coef_by
    parts = [None] * groups
    for group in reversed(range(groups)) if reverse else range(groups):
        parts[group] = term[group] + coef[group] * carry
        carry = parts[group][0:1] if reverse else parts[group][7:8]
    return jnp.concatenate(parts, axis=0), carry


def gate_setup(place, bx_own, bx_oth, mask_ref, prm_ref, gate_ref, xs, cs, pre):
    half = bx_own.shape[0]
    length = 2 * half
    lanes = bx_own.shape[1]
    xs[0:8, :] = jnp.zeros((8, lanes), F32)
    xs[pl.ds(pl.multiple_of(8 + place * half, 8), half), :] = bx_own[...].astype(F32)
    xs[pl.ds(pl.multiple_of(8 + (1 - place) * half, 8), half), :] = bx_oth[...].astype(F32)
    taps = [prm_ref[k : k + 1, :] for k in range(4)]
    bias = prm_ref[4:5, :]

    def conv_step(index, _):
        at = pl.multiple_of(index * STEP, STEP)
        window = xs[pl.ds(at, STEP + 8), :]
        mask = mask_ref[pl.ds(at, STEP), :]
        total = taps[0] * window[8 : 8 + STEP] + bias
        for k in (1, 2, 3):
            total = total + (mask[:, k : k + 1] * taps[k]) * window[8 - k : 8 - k + STEP]
        cs[pl.ds(at, STEP), :] = total.astype(BF16)
        return 0

    lax.fori_loop(0, length // STEP, conv_step, 0)

    def gate_step(index, _):
        rows = pl.ds(pl.multiple_of(index * 256, 256), 256)
        conv = cs[rows, :]
        pre[rows, 0:lanes] = jnp.dot(conv, gate_ref[0, 0], preferred_element_type=F32)
        pre[rows, lanes:] = jnp.dot(conv, gate_ref[1, 0], preferred_element_type=F32)
        return 0

    lax.fori_loop(0, length // 256, gate_step, 0)


def gate_terms(pre_rows, prm_ref, keep):
    lanes = pre_rows.shape[1] // 2
    in_gate = jax.nn.sigmoid(pre_rows[:, :lanes] + prm_ref[5:6, :])
    rate_gate = jax.nn.sigmoid(pre_rows[:, lanes:] + prm_ref[6:7, :])
    log_decay = prm_ref[7:8, :] * rate_gate
    decay = jnp.exp(log_decay)
    squared = decay * decay
    gap = one_minus_exp(-2.0 * log_decay, squared)
    return in_gate, rate_gate, decay, squared, gap


def own_rows(place, half):
    return pl.ds(pl.multiple_of(place * half, half), half), pl.ds(pl.multiple_of((1 - place) * half, half), half)


def rec_fwd_kernel(
    bx_own, bx_oth, by_own, by_oth, mask_ref, prm_ref, gate_ref, gated_own, gated_oth, state_ref, xs, cs, pre, ys, gated,
):
    place = lax.axis_index("tp")
    half, lanes = bx_own.shape
    own, oth = own_rows(place, half)
    gate_setup(place, bx_own, bx_oth, mask_ref, prm_ref, gate_ref, xs, cs, pre)
    ys[own, :] = by_own[...]
    ys[oth, :] = by_oth[...]

    def step(index, carry):
        rows = pl.ds(pl.multiple_of(index * STEP, STEP), STEP)
        keep = mask_ref[rows, :][:, 0:1]
        in_gate, _, decay, _, gap = gate_terms(pre[rows, :], prm_ref, keep)
        scaling = (1.0 - keep) + keep * jnp.sqrt(gap)
        pushed = cs[rows, :].astype(F32) * in_gate * scaling
        state, carry = group_scan(decay * keep, pushed, carry, False)
        state_ref[rows, :] = state
        y = ys[rows, :]
        tanh = jnp.tanh(GELU_A * (y + GELU_B * (y * y * y)))
        gated[rows, :] = (state * (0.5 * y * (1.0 + tanh))).astype(BF16)
        return carry

    lax.fori_loop(0, 2 * half // STEP, step, jnp.zeros((1, lanes), F32))
    gated_own[...] = gated[own, :]
    gated_oth[...] = gated[oth, :]


def fold(value):
    return jnp.sum(value.reshape(value.shape[0] // 8, 8, value.shape[1]), axis=0)


def rec_bwd_kernel(
    count, bits, bx_own, bx_oth, by_own, by_oth, state_ref, up_own, up_oth, mask_ref, prm_ref, gate_ref,
    gx_own, gx_oth, gy_own, gy_oth, gw_ref, sum_ref, xs, cs, pre, ys, up_ref, gx_ref, gy_ref, gw, dg, gc,
):
    place = lax.axis_index("tp")
    half, lanes = bx_own.shape
    length = 2 * half
    steps = length // STEP
    own, oth = own_rows(place, half)
    gate_setup(place, bx_own, bx_oth, mask_ref, prm_ref, gate_ref, xs, cs, pre)
    ys[own, :] = by_own[...]
    ys[oth, :] = by_oth[...]
    up_ref[own, :] = up_own[...]
    up_ref[oth, :] = up_oth[...]
    zero8 = jnp.zeros((8, lanes), F32)

    def step(index, carried):
        carry, sum_in, sum_rate, sum_log = carried
        rows = pl.ds(pl.multiple_of((steps - 1 - index) * STEP, STEP), STEP)
        keep = mask_ref[rows, :][:, 0:1]
        in_gate, rate_gate, decay, squared, gap = gate_terms(pre[rows, :], prm_ref, keep)
        inverse = lax.rsqrt(gap)
        scaling = (1.0 - keep) + keep * (gap * inverse)
        y = ys[rows, :]
        y2 = y * y
        tanh = jnp.tanh(GELU_A * y * (1.0 + GELU_B * y2))
        lift = 0.5 * (1.0 + tanh)
        slope = lift + (0.5 * GELU_A) * y * (1.0 - tanh * tanh) * (1.0 + (3.0 * GELU_B) * y2)
        up = up_ref[rows, :]
        state = state_ref[rows, :]
        gy_ref[rows, :] = (up * state * slope).astype(BF16)
        direct = up * (y * lift)
        coef = decay * keep
        sent, below = group_scan(coef, coef * direct, carry, True)
        shifted = jnp.concatenate([sent[1:], carry], axis=0)
        grad_state = direct + shifted
        entered = cs[rows, :].astype(F32) * in_gate
        pushed = entered * scaling
        grad_log = grad_state * ((state - pushed) - entered * (keep * squared * inverse))
        grad_in = (grad_state * pushed * (1.0 - in_gate)).astype(BF16)
        through = grad_log * rate_gate
        grad_rate = (through * (1.0 - rate_gate) * prm_ref[7:8, :]).astype(BF16)
        dg[rows, 0:lanes] = grad_in
        dg[rows, lanes:] = grad_rate
        gc[rows, :] = grad_state * in_gate * scaling
        return (
            below,
            sum_in + fold(grad_in.astype(F32)),
            sum_rate + fold(grad_rate.astype(F32)),
            sum_log + fold(through),
        )

    _, sum_in, sum_rate, sum_log = lax.fori_loop(
        0, steps, step, (jnp.zeros((1, lanes), F32), zero8, zero8, zero8)
    )
    gc[length : length + 8, :] = zero8

    def back_step(index, _):
        rows = pl.ds(pl.multiple_of(index * 256, 256), 256)
        gc[rows, :] += matmul_right(dg[rows, 0:lanes], gate_ref[0, 0]) + matmul_right(
            dg[rows, lanes:], gate_ref[1, 0]
        )
        return 0

    lax.fori_loop(0, length // 256, back_step, 0)
    gw[0:lanes, :] = matmul_left(cs[...], dg[:, 0:lanes]).astype(BF16)
    gw[lanes:, :] = matmul_left(cs[...], dg[:, lanes:]).astype(BF16)
    rows_each = lanes // count
    me = lax.axis_index("dp")
    for spot in range(count):
        block = block_from(me, spot, bits)
        for gate in (0, 1):
            source = pl.ds(pl.multiple_of(gate * lanes + block * rows_each, rows_each), rows_each)
            gw_ref[spot, 0, gate * rows_each : (gate + 1) * rows_each, :] = gw[source, :]
    taps = [prm_ref[k : k + 1, :] for k in range(4)]

    def conv_step(index, sums):
        at = pl.multiple_of(index * STEP, STEP)
        grad = gc[pl.ds(at, STEP + 8), :]
        window = xs[pl.ds(at, STEP + 8), :]
        mask = mask_ref[pl.ds(at, STEP + 8), :]
        here = grad[0:STEP]
        total = taps[0] * here
        sums = [sums[0] + fold(here), sums[1] + fold(here * window[8 : 8 + STEP])] + list(sums[2:])
        for k in (1, 2, 3):
            masked = grad * mask[:, k : k + 1]
            total = total + taps[k] * masked[k : k + STEP]
            sums[k + 1] = sums[k + 1] + fold(masked[0:STEP] * window[8 - k : 8 - k + STEP])
        gx_ref[pl.ds(at, STEP), :] = total.astype(BF16)
        return tuple(sums)

    sums = lax.fori_loop(0, steps, conv_step, (zero8,) * 5)
    for index, value in enumerate(sums[1:5] + (sums[0], sum_in, sum_rate, sum_log)):
        sum_ref[index : index + 1, :] = jnp.sum(value, axis=0, keepdims=True)
    for source, first, second in ((gx_ref, gx_own, gx_oth), (gy_ref, gy_own, gy_oth)):
        first[...] = source[own, :]
        second[...] = source[oth, :]


def rec_specs(half, lanes, length):
    piece = pl.BlockSpec((half, lanes), lambda h: (0, h))
    whole = pl.BlockSpec((length, lanes), lambda h: (0, h))
    mask = pl.BlockSpec((length + 8, 8), lambda h: (0, 0))
    prm = pl.BlockSpec((8, lanes), lambda h: (0, h))
    gate = pl.BlockSpec((2, 1, lanes, lanes), lambda h: (0, h, 0, 0))
    return piece, whole, mask, prm, gate


def rec_scratch(length, lanes):
    return [
        pltpu.VMEM((length + 8, lanes), F32),
        pltpu.VMEM((length, lanes), BF16),
        pltpu.VMEM((length, 2 * lanes), F32),
        pltpu.VMEM((length, lanes), F32),
    ]


def rec_fwd(bx_own, bx_oth, by_own, by_oth, mask, prm, gates):
    half, width = bx_own.shape
    length, lanes, heads = 2 * half, gates.shape[2], gates.shape[1]
    piece, whole, mask_spec, prm_spec, gate_spec = rec_specs(half, lanes, length)
    return pl.pallas_call(
        rec_fwd_kernel,
        grid=(heads,),
        in_specs=[piece] * 4 + [mask_spec, prm_spec, gate_spec],
        out_specs=[piece, piece, whole],
        out_shape=[
            jax.ShapeDtypeStruct((half, width), BF16),
            jax.ShapeDtypeStruct((half, width), BF16),
            jax.ShapeDtypeStruct((length, width), F32),
        ],
        scratch_shapes=rec_scratch(length, lanes) + [pltpu.VMEM((length, lanes), BF16)],
        compiler_params=pltpu.CompilerParams(vmem_limit_bytes=40 << 20),
        cost_estimate=pl.CostEstimate(
            flops=4 * length * width * lanes + 100 * length * width,
            bytes_accessed=16 * length * width,
            transcendentals=6 * length * width,
        ),
        name="rec_fwd",
    )(bx_own, bx_oth, by_own, by_oth, mask, prm, gates)


def rec_bwd(bx_own, bx_oth, by_own, by_oth, states, up_own, up_oth, mask, prm, gates, count):
    half, width = bx_own.shape
    length, lanes, heads = 2 * half, gates.shape[2], gates.shape[1]
    piece, whole, mask_spec, prm_spec, gate_spec = rec_specs(half, lanes, length)
    return pl.pallas_call(
        functools.partial(rec_bwd_kernel, count, stage_bits(count)),
        grid=(heads,),
        in_specs=[piece] * 4 + [whole, piece, piece, mask_spec, prm_spec, gate_spec],
        out_specs=[piece] * 4 + [pl.BlockSpec((count, 1, 2 * lanes // count, lanes), lambda h: (0, h, 0, 0)), prm_spec],
        out_shape=[jax.ShapeDtypeStruct((half, width), BF16)] * 4
        + [
            jax.ShapeDtypeStruct((count, heads, 2 * lanes // count, lanes), BF16),
            jax.ShapeDtypeStruct((8, width), F32),
        ],
        scratch_shapes=rec_scratch(length, lanes)
        + [
            pltpu.VMEM((length, lanes), F32),
            pltpu.VMEM((length, lanes), BF16),
            pltpu.VMEM((length, lanes), BF16),
            pltpu.VMEM((2 * lanes, lanes), BF16),
            pltpu.VMEM((length, 2 * lanes), BF16),
            pltpu.VMEM((length + 8, lanes), F32),
        ],
        compiler_params=pltpu.CompilerParams(vmem_limit_bytes=48 << 20),
        cost_estimate=pl.CostEstimate(
            flops=12 * length * width * lanes + 250 * length * width,
            bytes_accessed=24 * length * width,
            transcendentals=8 * length * width,
        ),
        name="rec_bwd",
    )(bx_own, bx_oth, by_own, by_oth, states, up_own, up_oth, mask, prm, gates)


def stage_bits(count):
    bits = count.bit_length() - 1
    return [1 << bit for bit in ([0, 1] + list(reversed(range(2, bits))))[:bits]]


def block_at(place, bits):
    return sum(bit for step, bit in enumerate(bits) if (place >> (len(bits) - 1 - step)) & 1)


def block_from(me, place, bits):
    relative = block_at(place, bits)
    block = 0
    for bit in bits:
        mine = lax.rem(me // bit, 2)
        block = block + bit * (1 - mine if relative & bit else mine)
    return block


def arrange_kernel(count, bits, steps, first, second, *parts):
    me = lax.axis_index("dp")
    cols = first.shape[1] // count

    def move(piece):
        for place in range(count):
            source = pl.ds(pl.multiple_of(block_from(me, place, bits) * cols, cols), cols)
            if place < count // 4:
                into, spot = parts[0], place
            elif place < count // 2:
                into, spot = parts[1], place - count // 4
            else:
                into, spot = parts[2], place - count // 2
            into[:, spot * cols : (spot + 1) * cols] = piece[:, source]

    @pl.when(pl.program_id(0) < steps)
    def _():
        move(first)

    @pl.when(pl.program_id(0) >= steps)
    def _():
        move(second)


def arrange(first, second, count):
    half, width = first.shape
    steps = 2
    block = half // steps
    widths = width // 4, width // 4, width // 2
    return pl.pallas_call(
        functools.partial(arrange_kernel, count, stage_bits(count), steps),
        grid=(2 * steps,),
        in_specs=[
            pl.BlockSpec((block, width), lambda i: (jnp.minimum(i, steps - 1), 0)),
            pl.BlockSpec((block, width), lambda i: (jnp.maximum(i - steps, 0), 0)),
        ],
        out_specs=[pl.BlockSpec((block, cols), lambda i: (i, 0)) for cols in widths],
        out_shape=[jax.ShapeDtypeStruct((2 * half, cols), first.dtype) for cols in widths],
        cost_estimate=pl.CostEstimate(flops=0, bytes_accessed=8 * half * width, transcendentals=0),
        name="arrange",
    )(first, second)


def swap(value):
    return lax.ppermute(value, "tp", [(0, 1), (1, 0)])


def flip(value, bit):
    count = lax.axis_size("dp")
    return lax.ppermute(value, "dp", [(source, source ^ bit) for source in range(count)])


class Reduction:
    def __init__(self, parts, right, bits):
        self.keep_cols, self.next_cols, self.first_cols = parts
        self.right, self.bits = right, list(bits)

    def send(self, *others):
        sent = matmul_left(after(self.first_cols, *others), self.right).astype(BF16)
        self.received = flip(sent, self.bits.pop(0))
        return sent

    def send_next(self, *others):
        received = self.received
        middle = received.shape[0] // 2
        left, received = lax.optimization_barrier((self.next_cols, received, *others))[:2]
        sent = (matmul_left(left, self.right) + received[middle:].astype(F32)).astype(BF16)
        self.received = flip(sent, self.bits.pop(0))
        self.keep = (matmul_left(after(self.keep_cols, sent), self.right) + received[:middle].astype(F32)).astype(BF16)
        return self.keep

    def step(self, *others):
        received = after(self.received, *others)
        middle = received.shape[0] // 2
        sent = (self.keep[middle:].astype(F32) + received[middle:].astype(F32)).astype(BF16)
        self.keep = (self.keep[:middle].astype(F32) + received[:middle].astype(F32)).astype(BF16)
        self.received = flip(sent, self.bits.pop(0))
        return sent

    def total(self, *others):
        return self.keep.astype(F32) + after(self.received, *others).astype(F32)


def after(value, *others):
    return lax.optimization_barrier((value, *others))[0]


def norm_back(values, gain, grad):
    scale = lax.rsqrt(jnp.mean(values * values, axis=-1, keepdims=True) + EPS)
    lifted = gain * grad
    pull = jnp.mean(values * lifted, axis=-1, keepdims=True)
    return scale * lifted - values * (scale * scale * scale * pull)


def local_channels(
    layer_in, cotangent, resets, norm_gains, w_x, w_y, conv_w, lru_bias, a_param, gate_blocks, w_out, w_gate, w_up, w_down,
):
    place = lax.axis_index("tp")
    me = lax.axis_index("dp")
    count = lax.axis_size("dp")
    bits = stage_bits(count)
    width = w_x.shape[1]
    full_width = conv_w.shape[1]
    heads = gate_blocks.shape[1] // 2
    model = norm_gains.shape[1]

    own_in, own_cot = layer_in[0], cotangent[0]
    oth_in = swap(own_in)
    oth_resets = swap(resets[0])
    oth_cot = swap(own_cot)
    normed_own = rms_scale(own_in.astype(F32), norm_gains[0]).astype(BF16)
    bx_own = matmul(normed_own, w_x).astype(BF16)
    by_own = matmul(normed_own, w_y)

    first_place = place == 0
    in_time = jnp.where(first_place, resets[0], oth_resets), jnp.where(first_place, oth_resets, resets[0])
    keep = 1.0 - jnp.concatenate(in_time).astype(F32)
    keep_1 = jnp.concatenate([jnp.ones((1,), F32), keep[:-1]])
    keep_2 = jnp.concatenate([jnp.ones((1,), F32), keep_1[:-1]])
    valid = [keep, keep, keep * keep_1, keep * keep_1 * keep_2]
    mask = jnp.pad(jnp.stack(valid, axis=1), ((0, 8), (0, 4)))
    table = jnp.concatenate([conv_w, lru_bias, -8.0 * jax.nn.softplus(a_param)[None]], axis=0)
    prm = lax.dynamic_slice(table, (0, place * width), (8, width))
    gates = lax.dynamic_slice_in_dim(gate_blocks, place * heads, heads, axis=1)

    gh_own = matmul_right(after(own_cot, bx_own, by_own), w_down)
    normed_oth = rms_scale(after(oth_in, gh_own).astype(F32), norm_gains[0]).astype(BF16)
    bx_oth = matmul(normed_oth, w_x).astype(BF16)
    by_oth = matmul(normed_oth, w_y)
    gated_own, gated_oth, states = rec_fwd(bx_own, bx_oth, by_own, by_oth, mask, prm, gates)

    gated = jnp.concatenate([gated_own, gated_oth], axis=0)
    part_oth = matmul(gated_oth, w_out).astype(BF16)
    swap_own = swap(part_oth)
    part_own = matmul(after(gated_own, part_oth), w_out).astype(BF16)
    swap_oth = swap(part_own)
    gh_oth = matmul_right(after(oth_cot, part_own), w_down)
    cot_cols = arrange(after(own_cot, gh_oth), oth_cot, count)

    def feed_in(tokens, part, other):
        middle = tokens.astype(F32) + (part.astype(F32) + other.astype(F32))
        normed = rms_scale(middle, norm_gains[1]).astype(BF16)
        gate_val = matmul(normed, w_gate)
        up_val = matmul(normed, w_up)
        hidden = (jax.nn.gelu(gate_val, approximate=True) * up_val).astype(BF16)
        return middle, normed, gate_val, up_val, hidden

    def feed_grads(gate_val, up_val, grad_hidden):
        _, pull = jax.vjp(gelu_product, gate_val, up_val)
        grad_gate, grad_up = pull(grad_hidden)
        return grad_gate.astype(BF16), grad_up.astype(BF16)

    def feed_back(grad_gate, grad_up):
        return (matmul_right(grad_gate, w_gate) + matmul_right(grad_up, w_up)).astype(BF16)

    def norm_two_back(middle, back, other, cot):
        grad = cot.astype(F32) + norm_back(middle, norm_gains[1], back.astype(F32) + other.astype(F32))
        return grad, grad.astype(BF16)

    middle_own, normed_two_own, gate_own, up_own, hidden_own = feed_in(own_in, part_own, after(swap_own, *cot_cols))
    gg_own, gu_own = feed_grads(gate_own, up_own, after(gh_own, hidden_own))
    middle_oth, normed_two_oth, gate_oth, up_oth, hidden_oth = feed_in(oth_in, part_oth, after(swap_oth, gg_own, gu_own))
    down = Reduction(cot_cols, jnp.concatenate([hidden_own, hidden_oth], axis=0), bits)
    done = down.send()
    gg_oth, gu_oth = feed_grads(gate_oth, up_oth, after(gh_oth, done))
    normed_two_cols = arrange(after(normed_two_own, gg_oth, gu_oth), normed_two_oth, count)
    done = down.send_next(*normed_two_cols)
    back_own = feed_back(after(gg_own, done), gu_own)
    back_own_swapped = swap(back_own)
    gate = Reduction(normed_two_cols, jnp.concatenate([gg_own, gg_oth], axis=0), bits)
    up = Reduction(normed_two_cols, jnp.concatenate([gu_own, gu_oth], axis=0), bits)
    done = gate.send(back_own)
    done = up.send(done)
    done = gate.send_next(done)
    back_oth = feed_back(after(gg_oth, done), gu_oth)
    back_oth_swapped = swap(back_oth)
    done = up.send_next(back_oth)
    done = down.step(done)
    out_send = matmul(after(hidden_oth, done), w_down).astype(BF16)
    out_swapped = swap(out_send)
    out_keep = matmul(after(hidden_own, out_send), w_down).astype(BF16)

    grad_own, rec_own = norm_two_back(middle_own, back_own, after(back_oth_swapped, out_keep), own_cot)
    _, rec_oth = norm_two_back(middle_oth, back_oth, after(back_own_swapped, out_keep), oth_cot)
    into_own = matmul_right(rec_own, w_out)
    into_oth = matmul_right(rec_oth, w_out)
    gx_own, gx_oth, gy_own, gy_oth, gate_grad, sums = rec_bwd(
        bx_own, bx_oth, by_own, by_oth, states, into_own, into_oth, mask, prm, gates, count
    )
    done = gate.step(gx_own, down.step(gx_own))
    rec_cols = arrange(after(rec_own, done), rec_oth, count)
    normed_cols = arrange(after(normed_own, *rec_cols), normed_oth, count)
    in_x = Reduction(normed_cols, jnp.concatenate([gx_own, gx_oth], axis=0), bits)
    in_y = Reduction(normed_cols, jnp.concatenate([gy_own, gy_oth], axis=0), bits)
    out = Reduction(rec_cols, gated, bits)
    done = in_x.send(*normed_cols)
    done = in_y.send(done)
    done = out.send(done)
    done = in_x.send_next(done)
    done = in_y.send_next(done)
    done = out.send_next(done)

    def rec_back(piece_x, piece_y):
        return (matmul_right(piece_x, w_x) + matmul_right(piece_y, w_y)).astype(BF16)

    rec_send = rec_back(after(gx_oth, done), gy_oth)
    rec_swapped = swap(rec_send)
    layer_out = (middle_own + out_keep.astype(F32) + after(out_swapped, rec_send).astype(F32)).astype(BF16)
    lanes = gate_grad.shape[-1]
    blocks = gate_grad.reshape(-1, lanes)
    row = jnp.arange(8)[:, None] == 7
    slopes = -8.0 * lax.dynamic_slice(jax.nn.sigmoid(a_param), (place * width,), (width,))
    sums = jnp.where(row, sums * slopes, sums).astype(BF16).reshape(-1, lanes)
    done = rec_send
    for bit in bits:
        middle = blocks.shape[0] // 2
        message = jnp.concatenate([blocks[middle:], sums], axis=0)
        received = after(flip(message, bit), done).astype(F32)
        blocks = (blocks[:middle].astype(F32) + received[:middle]).astype(BF16)
        sums = (sums.astype(F32) + received[middle:]).astype(BF16)
        if bit == bits[0]:
            rec_keep = rec_back(after(gx_own, blocks), gy_own)
            done = rec_keep
    message = jnp.concatenate([blocks, sums], axis=0)
    others = swap(message)
    low, high = jnp.where(first_place, message, others), jnp.where(first_place, others, message)
    n_blocks = blocks.shape[0]
    block_sums = jnp.stack([low[:n_blocks], high[:n_blocks]]).astype(F32).reshape(2 * heads, 2, -1, lanes)
    small = jnp.concatenate([low[n_blocks:].reshape(8, width), high[n_blocks:].reshape(8, width)], axis=1)
    small = lax.dynamic_slice(small, (0, me * (full_width // count)), (8, full_width // count)).astype(F32)

    grad_normed = rec_keep.astype(F32) + rec_swapped.astype(F32)
    input_grad = grad_own + norm_back(own_in.astype(F32), norm_gains[0], grad_normed)
    done = up.step(input_grad)
    down_grad = down.total(done)
    done = gate.step(down_grad)
    done = in_x.step(done)
    done = in_y.step(done)
    gate_grad = gate.total(done)
    done = up.step(gate_grad)
    done = out.step(done)
    done = in_x.step(done)
    done = in_y.step(done)
    up_grad = up.total(done)
    done = out.step(up_grad)
    x_grad = in_x.total(done)
    y_grad = in_y.total(done)
    out_grad = out.total()

    block = model // count

    def gain_grad(gain, *pairs):
        weights = sum(
            jnp.sum(lax.dynamic_slice_in_dim(weight, me * block, block, axis=0).astype(F32) * grad, axis=1)
            for weight, grad in pairs
        )
        return weights / lax.dynamic_slice_in_dim(gain, me * block, block, axis=0)

    gains = jnp.stack(
        [
            gain_grad(norm_gains[0], (w_x, x_grad), (w_y, y_grad)),
            gain_grad(norm_gains[1], (w_gate, gate_grad), (w_up, up_grad)),
        ]
    )
    gains = gains + swap(gains)
    return (
        layer_out[None],
        input_grad[None],
        gains,
        x_grad,
        y_grad,
        small[0:4],
        small[4:7],
        small[7],
        jnp.swapaxes(block_sums, 0, 1),
        out_grad.T,
        gate_grad,
        up_grad,
        down_grad.T,
    )


def from_behind(value, axis, steps):
    count = lax.axis_size(axis)
    first, last = (max(0, -steps), min(count, count - steps))
    return lax.ppermute(value, axis, [(source, source + steps) for source in range(first, last)])


def rms_scale(values, gain_vec):
    return values * lax.rsqrt(jnp.mean(values * values, axis=-1, keepdims=True) + EPS) * gain_vec


def gelu_product(gate_val, up_val):
    return jax.nn.gelu(gate_val, approximate=True) * up_val


def lru_terms(conv_out, gate_in, gate_rate, a_param, starts):
    keep_mask = 1.0 - starts
    input_gate = jax.nn.sigmoid(gate_in)
    rate_gate = jax.nn.sigmoid(gate_rate)
    log_decay = -8.0 * rate_gate * jax.nn.softplus(a_param)
    scaling = starts + keep_mask * jnp.sqrt(-jnp.expm1(2.0 * log_decay))
    return (jnp.exp(log_decay) * keep_mask, conv_out * input_gate * scaling)


def matmul(first_mat, second_mat):
    return jnp.dot(first_mat, second_mat, preferred_element_type=jnp.float32)


def matmul_left(first_mat, second_mat):
    return lax.dot_general(
        first_mat, second_mat, (((0,), (0,)), ((), ())), preferred_element_type=jnp.float32
    )


def matmul_right(first_mat, second_mat):
    return lax.dot_general(
        first_mat, second_mat, (((1,), (1,)), ((), ())), preferred_element_type=jnp.float32
    )


def combine_state(first_item, second_item):
    return (first_item[0] * second_item[0], second_item[1] + second_item[0] * first_item[1])


def carry_across(coef_end, state_end, reverse):
    incoming = jnp.zeros_like(state_end)
    direction = -1 if reverse else 1
    for turn_index in range(lax.axis_size("tp") - 1):
        incoming = from_behind(state_end + coef_end * incoming, "tp", direction)
    return incoming


def local(
    layer_in,
    cotangent,
    resets,
    norm_gains,
    w_x,
    w_y,
    conv_w,
    lru_bias,
    a_param,
    gate_blocks,
    w_out,
    w_gate,
    w_up,
    w_down,
):
    inputs = layer_in[0].astype(jnp.float32)
    starts = resets[0].astype(jnp.float32)
    keep_mask = 1.0 - starts
    rim_size = conv_w.shape[0] - 1
    head_count = gate_blocks.shape[1]
    block_size = gate_blocks.shape[2]
    full_width = conv_w.shape[1]
    normed, norm_pull = jax.vjp(rms_scale, inputs, norm_gains[0])
    normed_low = normed.astype(jnp.bfloat16)
    proj_x, proj_y, proj_out = (
        lax.all_gather(w_x, "tp", axis=1, tiled=True),
        lax.all_gather(w_y, "tp", axis=1, tiled=True),
        lax.all_gather(w_out, "tp", axis=0, tiled=True),
    )
    rec_len = normed_low.shape[0]
    branch_x = matmul(normed_low, proj_x).astype(jnp.bfloat16)
    branch_y = matmul(normed_low, proj_y)
    rim_rows, rim_keep = from_behind(
        (branch_x[rec_len - rim_size :], keep_mask[rec_len - rim_size :].astype(jnp.bfloat16)),
        "tp",
        1,
    )
    padded_x = jnp.concatenate([rim_rows, branch_x], axis=0).astype(jnp.float32)
    padded_keep = jnp.concatenate([rim_keep.astype(jnp.float32), keep_mask])
    conv_sum = conv_w[0] * padded_x[rim_size:]
    valid_mask = keep_mask
    valid_list = []
    for offset in range(1, rim_size + 1):
        valid_list.append(valid_mask)
        conv_sum = (
            conv_sum
            + valid_mask[:, None]
            * conv_w[offset]
            * padded_x[rim_size - offset : rim_size - offset + rec_len]
        )
        valid_mask = valid_mask * padded_keep[rim_size - offset : rim_size - offset + rec_len]
    conv_out = (conv_sum + lru_bias[0]).astype(jnp.bfloat16)
    row_count = conv_out.shape[0]
    conv_blocks = conv_out.reshape(row_count, head_count, block_size)
    pre_rows = (
        jnp.einsum(
            "lhb,ghbc->glhc", conv_blocks, gate_blocks, preferred_element_type=jnp.float32
        ).reshape(2, row_count, full_width)
        + lru_bias[1:3][:, None, :]
    )
    gate_in = pre_rows[0]
    gate_rate = pre_rows[1]
    conv_float = conv_out.astype(jnp.float32)

    def lru_local(conv_in, in_pre, rate_pre, decay_in):
        return lru_terms(conv_in, in_pre, rate_pre, decay_in, starts[:, None])

    (decay_rate, pushed), lru_pull = jax.vjp(lru_local, conv_float, gate_in, gate_rate, a_param)
    decay_cum, local_states = lax.associative_scan(combine_state, (decay_rate, pushed), axis=0)
    incoming = carry_across(decay_cum[-1], local_states[-1], False)
    states = local_states + decay_cum * incoming
    gated_val, gated_pull = jax.vjp(gelu_product, branch_y, states)
    gated_low = gated_val.astype(jnp.bfloat16)
    recurrent = matmul(gated_low, proj_out)
    middle = inputs + recurrent
    normed_two, norm_two_pull = jax.vjp(rms_scale, middle, norm_gains[1])
    normed_two_low = normed_two.astype(jnp.bfloat16)
    group_rows = lax.all_gather(normed_two_low, "tp", axis=0, tiled=True)
    gate_val = matmul(group_rows, w_gate)
    up_val = matmul(group_rows, w_up)
    hidden_val, mlp_pull = jax.vjp(gelu_product, gate_val, up_val)
    hidden = hidden_val.astype(jnp.bfloat16)
    mlp_out = lax.psum_scatter(
        matmul(hidden, w_down).astype(jnp.bfloat16), "tp", scatter_dimension=0, tiled=True
    ).astype(jnp.float32)
    layer_out = (middle + mlp_out).astype(jnp.bfloat16)
    grad_out = cotangent[0].astype(jnp.float32)
    group_grad = lax.all_gather(cotangent[0], "tp", axis=0, tiled=True)
    w_down_grad = matmul_left(hidden, group_grad)
    grad_hidden = matmul_right(group_grad, w_down)
    grad_gate, grad_up = mlp_pull(grad_hidden)
    grad_gate = grad_gate.astype(jnp.bfloat16)
    grad_up = grad_up.astype(jnp.bfloat16)
    w_gate_grad = matmul_left(group_rows, grad_gate)
    w_up_grad = matmul_left(group_rows, grad_up)
    grad_normed_two = lax.psum_scatter(
        (matmul_right(grad_gate, w_gate) + matmul_right(grad_up, w_up)).astype(jnp.bfloat16),
        "tp",
        scatter_dimension=0,
        tiled=True,
    ).astype(jnp.float32)
    grad_middle, gain_two_grad = norm_two_pull(grad_normed_two)
    grad_middle = grad_middle + grad_out
    grad_rec = grad_middle.astype(jnp.bfloat16)
    grad_gated = matmul_right(grad_rec, proj_out)
    grad_branch_y, grad_direct = gated_pull(grad_gated)
    grad_branch_y = grad_branch_y.astype(jnp.bfloat16)
    decay_next = jnp.concatenate([decay_rate[1:], jnp.ones_like(decay_rate[:1])], axis=0)
    reach_back, local_grads = lax.associative_scan(
        combine_state, (decay_next, grad_direct), reverse=True, axis=0
    )
    outgoing = carry_across(decay_rate[0] * reach_back[0], decay_rate[0] * local_grads[0], True)
    state_grads = local_grads + reach_back * outgoing
    prior_states = jnp.concatenate([incoming[None], states[:-1]], axis=0)
    grad_conv, grad_in, grad_rate, a_local_grad = lru_pull(
        (state_grads * prior_states, state_grads)
    )
    grad_pre = jnp.stack([grad_in, grad_rate]).astype(jnp.bfloat16)
    pre_sums = jnp.sum(grad_pre.astype(jnp.float32), axis=1)
    pre_blocks = grad_pre.reshape(2, row_count, head_count, block_size)
    gate_blocks_grad = jnp.einsum(
        "lhb,glhc->ghbc", conv_blocks, pre_blocks, preferred_element_type=jnp.float32
    )
    gate_back = jnp.einsum(
        "glhc,ghbc->lhb", pre_blocks, gate_blocks, preferred_element_type=jnp.float32
    ).reshape(row_count, full_width)
    grad_conv = grad_conv + gate_back
    conv_w_rows = [jnp.sum(grad_conv * padded_x[rim_size:], axis=0)]
    grad_padded = (
        jnp.zeros((rec_len + rim_size, full_width), jnp.float32)
        .at[rim_size:]
        .add(conv_w[0] * grad_conv)
    )
    for offset in range(1, rim_size + 1):
        masked = valid_list[offset - 1][:, None] * grad_conv
        conv_w_rows.append(
            jnp.sum(masked * padded_x[rim_size - offset : rim_size - offset + rec_len], axis=0)
        )
        grad_padded = grad_padded.at[rim_size - offset : rim_size - offset + rec_len].add(
            conv_w[offset] * masked
        )
    returned = from_behind(grad_padded[:rim_size], "tp", -1)
    grad_x_branch = (
        grad_padded[rim_size:].at[rec_len - rim_size :].add(returned).astype(jnp.bfloat16)
    )
    conv_w_grad = jnp.stack(conv_w_rows)
    lru_bias_grad = jnp.concatenate([jnp.sum(grad_conv, axis=0)[None], pre_sums], axis=0)
    grad_normed = matmul_right(grad_x_branch, proj_x) + matmul_right(grad_branch_y, proj_y)
    grad_inputs, gain_one_grad = norm_pull(grad_normed)
    input_grad = grad_middle + grad_inputs
    w_x_grad, w_y_grad, w_out_grad = (
        lax.psum_scatter(
            matmul_left(normed_low, grad_x_branch).astype(jnp.bfloat16),
            "tp",
            scatter_dimension=1,
            tiled=True,
        ).astype(jnp.float32),
        lax.psum_scatter(
            matmul_left(normed_low, grad_branch_y).astype(jnp.bfloat16),
            "tp",
            scatter_dimension=1,
            tiled=True,
        ).astype(jnp.float32),
        lax.psum_scatter(
            matmul_left(gated_low, grad_rec).astype(jnp.bfloat16),
            "tp",
            scatter_dimension=0,
            tiled=True,
        ).astype(jnp.float32),
    )
    norm_gains_grad = jnp.stack([gain_one_grad, gain_two_grad])
    totals = (
        lax.psum_scatter(
            w_x_grad.astype(jnp.bfloat16), "dp", scatter_dimension=0, tiled=True
        ).astype(jnp.float32),
        lax.psum_scatter(
            w_y_grad.astype(jnp.bfloat16), "dp", scatter_dimension=0, tiled=True
        ).astype(jnp.float32),
        lax.psum_scatter(
            w_out_grad.astype(jnp.bfloat16), "dp", scatter_dimension=1, tiled=True
        ).astype(jnp.float32),
        lax.psum_scatter(
            w_gate_grad.astype(jnp.bfloat16), "dp", scatter_dimension=0, tiled=True
        ).astype(jnp.float32),
        lax.psum_scatter(
            w_up_grad.astype(jnp.bfloat16), "dp", scatter_dimension=0, tiled=True
        ).astype(jnp.float32),
        lax.psum_scatter(
            w_down_grad.astype(jnp.bfloat16), "dp", scatter_dimension=1, tiled=True
        ).astype(jnp.float32),
        lax.psum_scatter(
            norm_gains_grad.astype(jnp.bfloat16), "dp", scatter_dimension=1, tiled=True
        ).astype(jnp.float32),
        lax.psum_scatter(
            conv_w_grad.astype(jnp.bfloat16), "dp", scatter_dimension=1, tiled=True
        ).astype(jnp.float32),
        lax.psum_scatter(
            lru_bias_grad.astype(jnp.bfloat16), "dp", scatter_dimension=1, tiled=True
        ).astype(jnp.float32),
        lax.psum_scatter(
            a_local_grad.astype(jnp.bfloat16), "dp", scatter_dimension=0, tiled=True
        ).astype(jnp.float32),
        lax.psum_scatter(
            gate_blocks_grad.astype(jnp.bfloat16), "dp", scatter_dimension=2, tiled=True
        ).astype(jnp.float32),
    )
    reduced_small = (
        lax.psum(totals[6].astype(jnp.bfloat16), "tp").astype(jnp.float32),
        lax.psum(totals[7].astype(jnp.bfloat16), "tp").astype(jnp.float32),
        lax.psum(totals[8].astype(jnp.bfloat16), "tp").astype(jnp.float32),
        lax.psum(totals[9].astype(jnp.bfloat16), "tp").astype(jnp.float32),
        lax.psum(totals[10].astype(jnp.bfloat16), "tp").astype(jnp.float32),
    )
    return (
        layer_out[None],
        input_grad[None],
        reduced_small[0],
        totals[0],
        totals[1],
        reduced_small[1],
        reduced_small[2],
        reduced_small[3],
        reduced_small[4],
        totals[2],
        totals[3],
        totals[4],
        totals[5],
    )


def solution(mesh):
    rows, cols = mesh.shape["dp"], mesh.shape["tp"]
    by_channels = cols == 2 and rows >= 16 and rows & (rows - 1) == 0

    def step(*args):
        heads, model = args[9].shape[1], args[3].shape[1]
        fits = by_channels and heads % cols == 0 and model % (128 * rows) == 0
        return (local_channels if fits else local)(*args)

    return jax.shard_map(
        step,
        mesh=mesh,
        in_specs=(
            P("dp", "tp", None),
            P("dp", "tp", None),
            P("dp", "tp"),
            P(),
            P(None, "tp"),
            P(None, "tp"),
            P(),
            P(),
            P(),
            P(),
            P("tp", None),
            P(None, "tp"),
            P(None, "tp"),
            P("tp", None),
        ),
        out_specs=(
            P("dp", "tp", None),
            P("dp", "tp", None),
            P(None, "dp"),
            P("dp", "tp"),
            P("dp", "tp"),
            P(None, "dp"),
            P(None, "dp"),
            P("dp"),
            P(None, None, "dp", None),
            P("tp", "dp"),
            P("dp", "tp"),
            P("dp", "tp"),
            P("tp", "dp"),
        ),
        check_vma=False,
    )
```

```python
import functools

import jax
import jax.numpy as jnp
from jax import lax
from jax.experimental import pallas as pl
from jax.experimental.pallas import tpu as pltpu
from jax.sharding import PartitionSpec as P

EPS = 1e-06
F32, BF16 = jnp.float32, jnp.bfloat16
STEP = 64
GELU_A, GELU_B = 0.7978845608028654, 0.044715
MESH = pl.DeviceIdType.MESH


def one_minus_exp(value, exp_neg):
    series = 1.0 / 5040.0
    for term in (-1.0 / 720.0, 1.0 / 120.0, -1.0 / 24.0, 1.0 / 6.0, -0.5, 1.0):
        series = series * value + term
    return jnp.where(value < 0.25, series * value, 1.0 - exp_neg)


def group_scan(coef, term, carry, reverse):
    rows, lanes = coef.shape
    groups = rows // 8
    coef = coef.reshape(groups, 8, lanes)
    term = term.reshape(groups, 8, lanes)
    row = lax.broadcasted_iota(jnp.int32, (1, 8, lanes), 1)
    for dist in (1, 2, 4):
        shift = 8 - dist if reverse else dist
        inside = row < 8 - dist if reverse else row >= dist
        coef_by = jnp.where(inside, pltpu.roll(coef, shift, 1), 1.0)
        term_by = jnp.where(inside, pltpu.roll(term, shift, 1), 0.0)
        term = term + coef * term_by
        coef = coef * coef_by
    parts = [None] * groups
    for group in reversed(range(groups)) if reverse else range(groups):
        parts[group] = term[group] + coef[group] * carry
        carry = parts[group][0:1] if reverse else parts[group][7:8]
    return jnp.concatenate(parts, axis=0), carry


def gate_setup(place, bx_own, bx_oth, mask_ref, prm_ref, gate_ref, xs, cs, pre):
    half = bx_own.shape[0]
    length = 2 * half
    lanes = bx_own.shape[1]
    xs[0:8, :] = jnp.zeros((8, lanes), F32)
    xs[pl.ds(pl.multiple_of(8 + place * half, 8), half), :] = bx_own[...].astype(F32)
    xs[pl.ds(pl.multiple_of(8 + (1 - place) * half, 8), half), :] = bx_oth[...].astype(F32)
    taps = [prm_ref[k : k + 1, :] for k in range(4)]
    bias = prm_ref[4:5, :]

    def conv_step(index, _):
        at = pl.multiple_of(index * STEP, STEP)
        window = xs[pl.ds(at, STEP + 8), :]
        mask = mask_ref[pl.ds(at, STEP), :]
        total = taps[0] * window[8 : 8 + STEP] + bias
        for k in (1, 2, 3):
            total = total + (mask[:, k : k + 1] * taps[k]) * window[8 - k : 8 - k + STEP]
        cs[pl.ds(at, STEP), :] = total.astype(BF16)
        return 0

    lax.fori_loop(0, length // STEP, conv_step, 0)

    def gate_step(index, _):
        rows = pl.ds(pl.multiple_of(index * 256, 256), 256)
        conv = cs[rows, :]
        pre[rows, 0:lanes] = jnp.dot(conv, gate_ref[0, 0], preferred_element_type=F32)
        pre[rows, lanes:] = jnp.dot(conv, gate_ref[1, 0], preferred_element_type=F32)
        return 0

    lax.fori_loop(0, length // 256, gate_step, 0)


def gate_terms(pre_rows, prm_ref, keep):
    lanes = pre_rows.shape[1] // 2
    in_gate = jax.nn.sigmoid(pre_rows[:, :lanes] + prm_ref[5:6, :])
    rate_gate = jax.nn.sigmoid(pre_rows[:, lanes:] + prm_ref[6:7, :])
    log_decay = prm_ref[7:8, :] * rate_gate
    decay = jnp.exp(log_decay)
    squared = decay * decay
    gap = one_minus_exp(-2.0 * log_decay, squared)
    return in_gate, rate_gate, decay, squared, gap


def own_rows(place, half):
    return pl.ds(pl.multiple_of(place * half, half), half), pl.ds(pl.multiple_of((1 - place) * half, half), half)


def rec_fwd_kernel(
    bx_own, bx_oth, by_own, by_oth, mask_ref, prm_ref, gate_ref, gated_own, gated_oth, state_ref, xs, cs, pre, ys, gated,
):
    place = lax.axis_index("tp")
    half, lanes = bx_own.shape
    own, oth = own_rows(place, half)
    gate_setup(place, bx_own, bx_oth, mask_ref, prm_ref, gate_ref, xs, cs, pre)
    ys[own, :] = by_own[...]
    ys[oth, :] = by_oth[...]

    def step(index, carry):
        rows = pl.ds(pl.multiple_of(index * STEP, STEP), STEP)
        keep = mask_ref[rows, :][:, 0:1]
        in_gate, _, decay, _, gap = gate_terms(pre[rows, :], prm_ref, keep)
        scaling = (1.0 - keep) + keep * jnp.sqrt(gap)
        pushed = cs[rows, :].astype(F32) * in_gate * scaling
        state, carry = group_scan(decay * keep, pushed, carry, False)
        state_ref[rows, :] = state
        y = ys[rows, :]
        tanh = jnp.tanh(GELU_A * (y + GELU_B * (y * y * y)))
        gated[rows, :] = (state * (0.5 * y * (1.0 + tanh))).astype(BF16)
        return carry

    lax.fori_loop(0, 2 * half // STEP, step, jnp.zeros((1, lanes), F32))
    gated_own[...] = gated[own, :]
    gated_oth[...] = gated[oth, :]


def fold(value):
    return jnp.sum(value.reshape(value.shape[0] // 8, 8, value.shape[1]), axis=0)


def rec_bwd_kernel(
    count, bx_own, bx_oth, by_own, by_oth, state_ref, up_own, up_oth, mask_ref, prm_ref, gate_ref,
    gx_own, gx_oth, gy_own, gy_oth, gw_ref, sum_ref, xs, cs, pre, ys, up_ref, gx_ref, gy_ref, gw, dg, gc,
):
    place = lax.axis_index("tp")
    half, lanes = bx_own.shape
    length = 2 * half
    steps = length // STEP
    own, oth = own_rows(place, half)
    gate_setup(place, bx_own, bx_oth, mask_ref, prm_ref, gate_ref, xs, cs, pre)
    ys[own, :] = by_own[...]
    ys[oth, :] = by_oth[...]
    up_ref[own, :] = up_own[...]
    up_ref[oth, :] = up_oth[...]
    zero8 = jnp.zeros((8, lanes), F32)

    def step(index, carried):
        carry, sum_in, sum_rate, sum_log = carried
        rows = pl.ds(pl.multiple_of((steps - 1 - index) * STEP, STEP), STEP)
        keep = mask_ref[rows, :][:, 0:1]
        in_gate, rate_gate, decay, squared, gap = gate_terms(pre[rows, :], prm_ref, keep)
        inverse = lax.rsqrt(gap)
        scaling = (1.0 - keep) + keep * (gap * inverse)
        y = ys[rows, :]
        y2 = y * y
        tanh = jnp.tanh(GELU_A * y * (1.0 + GELU_B * y2))
        lift = 0.5 * (1.0 + tanh)
        slope = lift + (0.5 * GELU_A) * y * (1.0 - tanh * tanh) * (1.0 + (3.0 * GELU_B) * y2)
        up = up_ref[rows, :]
        state = state_ref[rows, :]
        gy_ref[rows, :] = (up * state * slope).astype(BF16)
        direct = up * (y * lift)
        coef = decay * keep
        sent, below = group_scan(coef, coef * direct, carry, True)
        shifted = jnp.concatenate([sent[1:], carry], axis=0)
        grad_state = direct + shifted
        entered = cs[rows, :].astype(F32) * in_gate
        pushed = entered * scaling
        grad_log = grad_state * ((state - pushed) - entered * (keep * squared * inverse))
        grad_in = (grad_state * pushed * (1.0 - in_gate)).astype(BF16)
        through = grad_log * rate_gate
        grad_rate = (through * (1.0 - rate_gate) * prm_ref[7:8, :]).astype(BF16)
        dg[rows, 0:lanes] = grad_in
        dg[rows, lanes:] = grad_rate
        gc[rows, :] = grad_state * in_gate * scaling
        return (
            below,
            sum_in + fold(grad_in.astype(F32)),
            sum_rate + fold(grad_rate.astype(F32)),
            sum_log + fold(through),
        )

    _, sum_in, sum_rate, sum_log = lax.fori_loop(
        0, steps, step, (jnp.zeros((1, lanes), F32), zero8, zero8, zero8)
    )
    gc[length : length + 8, :] = zero8

    def back_step(index, _):
        rows = pl.ds(pl.multiple_of(index * 256, 256), 256)
        gc[rows, :] += matmul_right(dg[rows, 0:lanes], gate_ref[0, 0]) + matmul_right(
            dg[rows, lanes:], gate_ref[1, 0]
        )
        return 0

    lax.fori_loop(0, length // 256, back_step, 0)
    gw[0:lanes, :] = matmul_left(cs[...], dg[:, 0:lanes]).astype(BF16)
    gw[lanes:, :] = matmul_left(cs[...], dg[:, lanes:]).astype(BF16)
    rows_each = lanes // count
    for block in range(count):
        for gate in (0, 1):
            source = gate * lanes + block * rows_each
            gw_ref[block, 0, gate * rows_each : (gate + 1) * rows_each, :] = gw[source : source + rows_each, :]
    taps = [prm_ref[k : k + 1, :] for k in range(4)]

    def conv_step(index, sums):
        at = pl.multiple_of(index * STEP, STEP)
        grad = gc[pl.ds(at, STEP + 8), :]
        window = xs[pl.ds(at, STEP + 8), :]
        mask = mask_ref[pl.ds(at, STEP + 8), :]
        here = grad[0:STEP]
        total = taps[0] * here
        sums = [sums[0] + fold(here), sums[1] + fold(here * window[8 : 8 + STEP])] + list(sums[2:])
        for k in (1, 2, 3):
            masked = grad * mask[:, k : k + 1]
            total = total + taps[k] * masked[k : k + STEP]
            sums[k + 1] = sums[k + 1] + fold(masked[0:STEP] * window[8 - k : 8 - k + STEP])
        gx_ref[pl.ds(at, STEP), :] = total.astype(BF16)
        return tuple(sums)

    sums = lax.fori_loop(0, steps, conv_step, (zero8,) * 5)
    for index, value in enumerate(sums[1:5] + (sums[0], sum_in, sum_rate, sum_log)):
        sum_ref[index : index + 1, :] = jnp.sum(value, axis=0, keepdims=True)
    for source, first, second in ((gx_ref, gx_own, gx_oth), (gy_ref, gy_own, gy_oth)):
        first[...] = source[own, :]
        second[...] = source[oth, :]


def rec_specs(half, lanes, length):
    piece = pl.BlockSpec((half, lanes), lambda h: (0, h))
    whole = pl.BlockSpec((length, lanes), lambda h: (0, h))
    mask = pl.BlockSpec((length + 8, 8), lambda h: (0, 0))
    prm = pl.BlockSpec((8, lanes), lambda h: (0, h))
    gate = pl.BlockSpec((2, 1, lanes, lanes), lambda h: (0, h, 0, 0))
    return piece, whole, mask, prm, gate


def rec_scratch(length, lanes):
    return [
        pltpu.VMEM((length + 8, lanes), F32),
        pltpu.VMEM((length, lanes), BF16),
        pltpu.VMEM((length, 2 * lanes), F32),
        pltpu.VMEM((length, lanes), F32),
    ]


def rec_fwd(bx_own, bx_oth, by_own, by_oth, mask, prm, gates):
    half, width = bx_own.shape
    length, lanes, heads = 2 * half, gates.shape[2], gates.shape[1]
    piece, whole, mask_spec, prm_spec, gate_spec = rec_specs(half, lanes, length)
    return pl.pallas_call(
        rec_fwd_kernel,
        grid=(heads,),
        in_specs=[piece] * 4 + [mask_spec, prm_spec, gate_spec],
        out_specs=[piece, piece, whole],
        out_shape=[
            jax.ShapeDtypeStruct((half, width), BF16),
            jax.ShapeDtypeStruct((half, width), BF16),
            jax.ShapeDtypeStruct((length, width), F32),
        ],
        scratch_shapes=rec_scratch(length, lanes) + [pltpu.VMEM((length, lanes), BF16)],
        compiler_params=pltpu.CompilerParams(vmem_limit_bytes=40 << 20),
        cost_estimate=pl.CostEstimate(
            flops=4 * length * width * lanes + 100 * length * width,
            bytes_accessed=16 * length * width,
            transcendentals=6 * length * width,
        ),
        name="rec_fwd",
    )(bx_own, bx_oth, by_own, by_oth, mask, prm, gates)


def rec_bwd(bx_own, bx_oth, by_own, by_oth, states, up_own, up_oth, mask, prm, gates, count):
    half, width = bx_own.shape
    length, lanes, heads = 2 * half, gates.shape[2], gates.shape[1]
    piece, whole, mask_spec, prm_spec, gate_spec = rec_specs(half, lanes, length)
    return pl.pallas_call(
        functools.partial(rec_bwd_kernel, count),
        grid=(heads,),
        in_specs=[piece] * 4 + [whole, piece, piece, mask_spec, prm_spec, gate_spec],
        out_specs=[piece] * 4 + [pl.BlockSpec((count, 1, 2 * lanes // count, lanes), lambda h: (0, h, 0, 0)), prm_spec],
        out_shape=[jax.ShapeDtypeStruct((half, width), BF16)] * 4
        + [
            jax.ShapeDtypeStruct((count, heads, 2 * lanes // count, lanes), BF16),
            jax.ShapeDtypeStruct((8, width), F32),
        ],
        scratch_shapes=rec_scratch(length, lanes)
        + [
            pltpu.VMEM((length, lanes), F32),
            pltpu.VMEM((length, lanes), BF16),
            pltpu.VMEM((length, lanes), BF16),
            pltpu.VMEM((2 * lanes, lanes), BF16),
            pltpu.VMEM((length, 2 * lanes), BF16),
            pltpu.VMEM((length + 8, lanes), F32),
        ],
        compiler_params=pltpu.CompilerParams(vmem_limit_bytes=48 << 20),
        cost_estimate=pl.CostEstimate(
            flops=12 * length * width * lanes + 250 * length * width,
            bytes_accessed=24 * length * width,
            transcendentals=8 * length * width,
        ),
        name="rec_bwd",
    )(bx_own, bx_oth, by_own, by_oth, states, up_own, up_oth, mask, prm, gates)


def stage_bits(count, crossed=False):
    bits = [1 << bit for bit in range(count.bit_length() - 1)]
    return [bits[0], bits[2], bits[1]] + bits[3:] if crossed else bits


def block_at(place, bits):
    return sum(bit for step, bit in enumerate(bits) if (place >> (len(bits) - 1 - step)) & 1)


def block_from(me, place, bits):
    relative = block_at(place, bits)
    block = 0
    for bit in bits:
        mine = lax.rem(me // bit, 2)
        block = block + bit * (1 - mine if relative & bit else mine)
    return block


def arrange_kernel(count, bits, steps, first, second, out):
    me = lax.axis_index("dp")
    cols = first.shape[1] // count

    def move(piece):
        for place in range(count):
            source = pl.ds(pl.multiple_of(block_from(me, place, bits) * cols, cols), cols)
            out[:, place * cols : (place + 1) * cols] = piece[:, source]

    @pl.when(pl.program_id(0) < steps)
    def _():
        move(first)

    @pl.when(pl.program_id(0) >= steps)
    def _():
        move(second)


def arrange(first, second, bits):
    half, width = first.shape
    steps = 2
    block = half // steps
    return pl.pallas_call(
        functools.partial(arrange_kernel, 1 << len(bits), bits, steps),
        grid=(2 * steps,),
        in_specs=[
            pl.BlockSpec((block, width), lambda i: (jnp.minimum(i, steps - 1), 0)),
            pl.BlockSpec((block, width), lambda i: (jnp.maximum(i - steps, 0), 0)),
        ],
        out_specs=pl.BlockSpec((block, width), lambda i: (i, 0)),
        out_shape=jax.ShapeDtypeStruct((2 * half, width), first.dtype),
        cost_estimate=pl.CostEstimate(flops=0, bytes_accessed=12 * half * width, transcendentals=0),
        name="arrange",
    )(first, second)


def tile_cols(step):
    return lax.rem((step + 1) // 2, 2)


def weight_grad_kernel(left_own, left_oth, right_own, right_oth, sent_next, kept, staged, landed, send_sem, recv_sem):
    step = pl.program_id(0)
    me = lax.axis_index("dp")
    partner = {"dp": me + 1 - 2 * lax.rem(me, 2)}

    @pl.when(step == 0)
    def _():
        barrier = pltpu.get_barrier_semaphore()
        pl.semaphore_signal(barrier, inc=1, device_id=partner, device_id_type=MESH)
        pl.semaphore_wait(barrier, 1)

    def copy(tile):
        return pltpu.make_async_remote_copy(
            src_ref=staged.at[tile],
            dst_ref=landed.at[tile],
            send_sem=send_sem.at[tile],
            recv_sem=recv_sem.at[tile],
            device_id=partner,
            device_id_type=MESH,
        )

    total = matmul_left(left_own[...], right_own[...]) + matmul_left(left_oth[...], right_oth[...])

    @pl.when(step < 4)
    def _():
        staged[step] = total.astype(BF16)
        copy(step).start()

    @pl.when(step >= 4)
    def _():
        copy(step - 4).wait_recv()
        value = (total + landed[step - 4].astype(F32)).astype(BF16)

        @pl.when(step < 6)
        def _():
            sent_next[...] = value

        @pl.when(step >= 6)
        def _():
            kept[...] = value

    @pl.when(step == 7)
    def _():
        for tile in range(4):
            copy(tile).wait_send()


def weight_grad(left, right_own, right_oth, ident):
    half, cols = right_own.shape
    rows = left.shape[1] // 4
    wide = cols // 2
    out = pltpu.HBM((rows, cols), BF16)
    return pl.pallas_call(
        weight_grad_kernel,
        grid=(8,),
        in_specs=[
            pl.BlockSpec((half, rows), lambda i: (0, 3 - i // 2)),
            pl.BlockSpec((half, rows), lambda i: (1, 3 - i // 2)),
            pl.BlockSpec((half, wide), lambda i: (0, tile_cols(i))),
            pl.BlockSpec((half, wide), lambda i: (0, tile_cols(i))),
        ],
        out_specs=[
            pl.BlockSpec((rows, wide), lambda i: (0, jnp.where(i < 5, 0, 1))),
            pl.BlockSpec((rows, wide), lambda i: (0, jnp.where(i < 7, 1, 0))),
        ],
        out_shape=[out, out],
        scratch_shapes=[
            pltpu.VMEM((4, rows, wide), BF16),
            pltpu.VMEM((4, rows, wide), BF16),
            pltpu.SemaphoreType.DMA((4,)),
            pltpu.SemaphoreType.DMA((4,)),
        ],
        compiler_params=pltpu.CompilerParams(
            collective_id=ident, has_side_effects=True, vmem_limit_bytes=48 << 20
        ),
        cost_estimate=pl.CostEstimate(
            flops=16 * half * rows * cols, bytes_accessed=16 * half * cols, transcendentals=0
        ),
        name="weight_grad",
    )(left, left, right_own, right_oth)


def two_back_kernel(first, first_w, second, second_w, out):
    out[...] = (matmul_right(first[...], first_w[...]) + matmul_right(second[...], second_w[...])).astype(BF16)


def two_back(first, first_w, second, second_w):
    rows, depth = first.shape
    cols = first_w.shape[0]
    step = 512
    left = pl.BlockSpec((rows, depth), lambda n: (0, 0))
    right = pl.BlockSpec((step, depth), lambda n: (n, 0))
    return pl.pallas_call(
        two_back_kernel,
        grid=(cols // step,),
        in_specs=[left, right, left, right],
        out_specs=pl.BlockSpec((rows, step), lambda n: (0, n)),
        out_shape=jax.ShapeDtypeStruct((rows, cols), BF16),
        compiler_params=pltpu.CompilerParams(vmem_limit_bytes=48 << 20),
        cost_estimate=pl.CostEstimate(
            flops=4 * rows * depth * cols, bytes_accessed=4 * depth * (rows + cols), transcendentals=0
        ),
        name="two_back",
    )(first, first_w, second, second_w)


def swap(value):
    return lax.ppermute(value, "tp", [(0, 1), (1, 0)])


def flip(value, bit):
    count = lax.axis_size("dp")
    return lax.ppermute(value, "dp", [(source, source ^ bit) for source in range(count)])


class Reduction:
    def __init__(self, left, right, bits, ident):
        self.bits = list(bits[1:])
        sent, self.keep = weight_grad(left, *right, ident)
        self.pass_on(sent)

    def pass_on(self, sent):
        self.received = flip(sent, self.bits.pop(0))

    def step(self, *others):
        received = after(self.received, *others)
        middle = received.shape[0] // 2
        sent = (self.keep[middle:].astype(F32) + received[middle:].astype(F32)).astype(BF16)
        keep = (self.keep[:middle].astype(F32) + received[:middle].astype(F32)).astype(BF16)
        sent, self.keep = lax.optimization_barrier((sent, keep))
        self.pass_on(sent)
        return sent

    def total(self, *others):
        while self.bits:
            self.step(*others)
        return self.keep.astype(F32) + after(self.received, *others).astype(F32)


def after(value, *others):
    return lax.optimization_barrier((value, *others))[0]


def norm_back(values, gain, grad):
    scale = lax.rsqrt(jnp.mean(values * values, axis=-1, keepdims=True) + EPS)
    lifted = gain * grad
    pull = jnp.mean(values * lifted, axis=-1, keepdims=True)
    return scale * lifted - values * (scale * scale * scale * pull)


def local_channels(
    layer_in, cotangent, resets, norm_gains, w_x, w_y, conv_w, lru_bias, a_param, gate_blocks, w_out, w_gate, w_up, w_down,
):
    place = lax.axis_index("tp")
    me = lax.axis_index("dp")
    count = lax.axis_size("dp")
    bits, crossed = stage_bits(count), stage_bits(count, True)
    width = w_x.shape[1]
    full_width = conv_w.shape[1]
    heads = gate_blocks.shape[1] // 2
    model = norm_gains.shape[1]

    own_in, own_cot = layer_in[0], cotangent[0]
    oth_in = swap(own_in)
    oth_resets = swap(resets[0])
    oth_cot = swap(own_cot)
    normed_own = rms_scale(own_in.astype(F32), norm_gains[0]).astype(BF16)
    bx_own = matmul(normed_own, w_x).astype(BF16)
    by_own = matmul(normed_own, w_y)

    first_place = place == 0
    in_time = jnp.where(first_place, resets[0], oth_resets), jnp.where(first_place, oth_resets, resets[0])
    keep = 1.0 - jnp.concatenate(in_time).astype(F32)
    keep_1 = jnp.concatenate([jnp.ones((1,), F32), keep[:-1]])
    keep_2 = jnp.concatenate([jnp.ones((1,), F32), keep_1[:-1]])
    valid = [keep, keep, keep * keep_1, keep * keep_1 * keep_2]
    mask = jnp.pad(jnp.stack(valid, axis=1), ((0, 8), (0, 4)))
    table = jnp.concatenate([conv_w, lru_bias, -8.0 * jax.nn.softplus(a_param)[None]], axis=0)
    prm = lax.dynamic_slice(table, (0, place * width), (8, width))
    gates = lax.dynamic_slice_in_dim(gate_blocks, place * heads, heads, axis=1)

    gh_own = matmul_right(after(own_cot, bx_own, by_own), w_down)
    normed_oth = rms_scale(after(oth_in, gh_own).astype(F32), norm_gains[0]).astype(BF16)
    bx_oth = matmul(normed_oth, w_x).astype(BF16)
    by_oth = matmul(normed_oth, w_y)
    gated_own, gated_oth, states = rec_fwd(bx_own, bx_oth, by_own, by_oth, mask, prm, gates)

    part_oth = matmul(gated_oth, w_out).astype(BF16)
    swap_own = swap(part_oth)
    part_own = matmul(after(gated_own, part_oth), w_out).astype(BF16)
    swap_oth = swap(part_own)
    gh_oth = matmul_right(after(oth_cot, part_own), w_down)
    cot_cols = arrange(after(own_cot, gh_oth), oth_cot, crossed)
    normed_cols = arrange(after(normed_own, cot_cols), normed_oth, bits)

    def feed_in(tokens, part, other):
        middle = tokens.astype(F32) + (part.astype(F32) + other.astype(F32))
        normed = rms_scale(middle, norm_gains[1]).astype(BF16)
        gate_val = matmul(normed, w_gate)
        up_val = matmul(normed, w_up)
        hidden = (jax.nn.gelu(gate_val, approximate=True) * up_val).astype(BF16)
        return middle, normed, gate_val, up_val, hidden

    def feed_grads(gate_val, up_val, grad_hidden):
        _, pull = jax.vjp(gelu_product, gate_val, up_val)
        grad_gate, grad_up = pull(grad_hidden)
        return grad_gate.astype(BF16), grad_up.astype(BF16)

    def norm_two_back(middle, back, cot):
        grad = cot.astype(F32) + norm_back(middle, norm_gains[1], back)
        return grad, grad.astype(BF16)

    middle_own, normed_two_own, gate_own, up_own, hidden_own = feed_in(own_in, part_own, after(swap_own, normed_cols))
    gg_own, gu_own = feed_grads(gate_own, up_own, after(gh_own, hidden_own))
    back_own = two_back(gg_own, w_gate, gu_own, w_up)
    back_own_swapped = swap(back_own)
    middle_oth, normed_two_oth, gate_oth, up_oth, hidden_oth = feed_in(oth_in, part_oth, after(swap_oth, back_own))
    down = Reduction(after(cot_cols, hidden_oth), (hidden_own, hidden_oth), crossed, 1)
    gg_oth, gu_oth = feed_grads(gate_oth, up_oth, after(gh_oth, down.keep))
    normed_two_cols = arrange(after(normed_two_own, gg_oth, gu_oth), normed_two_oth, bits)
    gate = Reduction(normed_two_cols, (gg_own, gg_oth), bits, 1)
    back_oth = two_back(after(gg_oth, gate.keep), w_gate, gu_oth, w_up)
    back_oth_swapped = swap(back_oth)
    oth_sum = (back_oth.astype(F32) + back_own_swapped.astype(F32)).astype(BF16)
    up = Reduction(after(normed_two_cols, oth_sum), (gu_own, gu_oth), bits, 1)
    done = down.step(up.keep)
    _, rec_oth = norm_two_back(middle_oth, after(oth_sum, done).astype(F32), oth_cot)
    into_oth = matmul_right(rec_oth, w_out)
    out_send = matmul(after(hidden_oth, into_oth), w_down).astype(BF16)
    out_swapped = swap(out_send)
    done = gate.step(out_send)
    own_sum = back_own.astype(F32) + after(back_oth_swapped, done).astype(F32)
    grad_own, rec_own = norm_two_back(middle_own, own_sum, own_cot)
    into_own = matmul_right(rec_own, w_out)
    rec_cols = arrange(after(rec_own, into_own), rec_oth, crossed)
    gx_own, gx_oth, gy_own, gy_oth, gate_sums, sums = rec_bwd(
        bx_own, bx_oth, by_own, by_oth, states, after(into_own, rec_cols), into_oth, mask, prm, gates, count
    )

    lanes = gate_sums.shape[-1]
    row = jnp.arange(8)[:, None] == 7
    slopes = -8.0 * lax.dynamic_slice(jax.nn.sigmoid(a_param), (place * width,), (width,))
    each = full_width // count
    sums = jnp.swapaxes(jnp.where(row, sums * slopes, sums).reshape(8, count // 2, each), 0, 1)
    sums = jnp.pad(jnp.concatenate([sums, sums], axis=0), ((0, 0), (0, 0), (0, lanes - each))).astype(BF16)
    blocks = jnp.concatenate([gate_sums.reshape(count, -1, lanes), sums], axis=1)
    blocks = lax.psum_scatter(blocks.reshape(-1, lanes), "dp", scatter_dimension=0, tiled=True)

    done = up.step(gx_own)
    done = down.step(done)
    done = gate.step(done)
    in_x = Reduction(after(normed_cols, done), (gx_own, gx_oth), bits, 2)
    out = Reduction(after(rec_cols, in_x.keep), (gated_own, gated_oth), crossed, 2)
    done = up.step(out.keep)
    in_y = Reduction(after(normed_cols, done), (gy_own, gy_oth), bits, 2)
    rec_send = two_back(after(gx_oth, in_y.keep), w_x, gy_oth, w_y)
    rec_swapped = swap(rec_send)
    down_grad = down.total(rec_send)
    gate_grad = gate.total(rec_send)
    done = in_x.step(down_grad, gate_grad)
    rec_keep = two_back(after(gx_own, done), w_x, gy_own, w_y)
    done = out.step(rec_keep)
    out_keep = matmul(after(hidden_own, done), w_down).astype(BF16)
    layer_out = (middle_own + out_keep.astype(F32) + after(out_swapped, out_keep).astype(F32)).astype(BF16)
    up_grad = up.total(layer_out)
    done = in_x.step(layer_out, up_grad)
    done = in_y.step(done)
    grad_normed = rec_keep.astype(F32) + after(rec_swapped, done).astype(F32)
    input_grad = grad_own + norm_back(own_in.astype(F32), norm_gains[0], grad_normed)
    done = out.step(input_grad)
    done = in_y.step(done)
    x_grad = in_x.total(done)
    others = swap(after(blocks, x_grad))
    out_grad = out.total(others)
    y_grad = in_y.total(out_grad)

    low, high = jnp.where(first_place, blocks, others), jnp.where(first_place, others, blocks)
    block_sums = jnp.stack([low[:-8], high[:-8]]).astype(F32).reshape(2 * heads, 2, -1, lanes)
    small = jnp.where(me < count // 2, low[-8:], high[-8:])[:, :each].astype(F32)

    block = model // count

    def gain_grad(gain, *pairs):
        weights = sum(
            jnp.sum(lax.dynamic_slice_in_dim(weight, me * block, block, axis=0).astype(F32) * grad, axis=1)
            for weight, grad in pairs
        )
        return weights / lax.dynamic_slice_in_dim(gain, me * block, block, axis=0)

    gains = jnp.stack(
        [
            gain_grad(norm_gains[0], (w_x, x_grad), (w_y, y_grad)),
            gain_grad(norm_gains[1], (w_gate, gate_grad), (w_up, up_grad)),
        ]
    )
    gains = gains + swap(gains)
    return (
        layer_out[None],
        input_grad[None],
        gains,
        x_grad,
        y_grad,
        small[0:4],
        small[4:7],
        small[7],
        jnp.swapaxes(block_sums, 0, 1),
        out_grad.T,
        gate_grad,
        up_grad,
        down_grad.T,
    )


def from_behind(value, axis, steps):
    count = lax.axis_size(axis)
    first, last = (max(0, -steps), min(count, count - steps))
    return lax.ppermute(value, axis, [(source, source + steps) for source in range(first, last)])


def rms_scale(values, gain_vec):
    return values * lax.rsqrt(jnp.mean(values * values, axis=-1, keepdims=True) + EPS) * gain_vec


def gelu_product(gate_val, up_val):
    return jax.nn.gelu(gate_val, approximate=True) * up_val


def lru_terms(conv_out, gate_in, gate_rate, a_param, starts):
    keep_mask = 1.0 - starts
    input_gate = jax.nn.sigmoid(gate_in)
    rate_gate = jax.nn.sigmoid(gate_rate)
    log_decay = -8.0 * rate_gate * jax.nn.softplus(a_param)
    scaling = starts + keep_mask * jnp.sqrt(-jnp.expm1(2.0 * log_decay))
    return (jnp.exp(log_decay) * keep_mask, conv_out * input_gate * scaling)


def matmul(first_mat, second_mat):
    return jnp.dot(first_mat, second_mat, preferred_element_type=jnp.float32)


def matmul_left(first_mat, second_mat):
    return lax.dot_general(
        first_mat, second_mat, (((0,), (0,)), ((), ())), preferred_element_type=jnp.float32
    )


def matmul_right(first_mat, second_mat):
    return lax.dot_general(
        first_mat, second_mat, (((1,), (1,)), ((), ())), preferred_element_type=jnp.float32
    )


def combine_state(first_item, second_item):
    return (first_item[0] * second_item[0], second_item[1] + second_item[0] * first_item[1])


def carry_across(coef_end, state_end, reverse):
    incoming = jnp.zeros_like(state_end)
    direction = -1 if reverse else 1
    for turn_index in range(lax.axis_size("tp") - 1):
        incoming = from_behind(state_end + coef_end * incoming, "tp", direction)
    return incoming


def local(
    layer_in,
    cotangent,
    resets,
    norm_gains,
    w_x,
    w_y,
    conv_w,
    lru_bias,
    a_param,
    gate_blocks,
    w_out,
    w_gate,
    w_up,
    w_down,
):
    inputs = layer_in[0].astype(jnp.float32)
    starts = resets[0].astype(jnp.float32)
    keep_mask = 1.0 - starts
    rim_size = conv_w.shape[0] - 1
    head_count = gate_blocks.shape[1]
    block_size = gate_blocks.shape[2]
    full_width = conv_w.shape[1]
    normed, norm_pull = jax.vjp(rms_scale, inputs, norm_gains[0])
    normed_low = normed.astype(jnp.bfloat16)
    proj_x, proj_y, proj_out = (
        lax.all_gather(w_x, "tp", axis=1, tiled=True),
        lax.all_gather(w_y, "tp", axis=1, tiled=True),
        lax.all_gather(w_out, "tp", axis=0, tiled=True),
    )
    rec_len = normed_low.shape[0]
    branch_x = matmul(normed_low, proj_x).astype(jnp.bfloat16)
    branch_y = matmul(normed_low, proj_y)
    rim_rows, rim_keep = from_behind(
        (branch_x[rec_len - rim_size :], keep_mask[rec_len - rim_size :].astype(jnp.bfloat16)),
        "tp",
        1,
    )
    padded_x = jnp.concatenate([rim_rows, branch_x], axis=0).astype(jnp.float32)
    padded_keep = jnp.concatenate([rim_keep.astype(jnp.float32), keep_mask])
    conv_sum = conv_w[0] * padded_x[rim_size:]
    valid_mask = keep_mask
    valid_list = []
    for offset in range(1, rim_size + 1):
        valid_list.append(valid_mask)
        conv_sum = (
            conv_sum
            + valid_mask[:, None]
            * conv_w[offset]
            * padded_x[rim_size - offset : rim_size - offset + rec_len]
        )
        valid_mask = valid_mask * padded_keep[rim_size - offset : rim_size - offset + rec_len]
    conv_out = (conv_sum + lru_bias[0]).astype(jnp.bfloat16)
    row_count = conv_out.shape[0]
    conv_blocks = conv_out.reshape(row_count, head_count, block_size)
    pre_rows = (
        jnp.einsum(
            "lhb,ghbc->glhc", conv_blocks, gate_blocks, preferred_element_type=jnp.float32
        ).reshape(2, row_count, full_width)
        + lru_bias[1:3][:, None, :]
    )
    gate_in = pre_rows[0]
    gate_rate = pre_rows[1]
    conv_float = conv_out.astype(jnp.float32)

    def lru_local(conv_in, in_pre, rate_pre, decay_in):
        return lru_terms(conv_in, in_pre, rate_pre, decay_in, starts[:, None])

    (decay_rate, pushed), lru_pull = jax.vjp(lru_local, conv_float, gate_in, gate_rate, a_param)
    decay_cum, local_states = lax.associative_scan(combine_state, (decay_rate, pushed), axis=0)
    incoming = carry_across(decay_cum[-1], local_states[-1], False)
    states = local_states + decay_cum * incoming
    gated_val, gated_pull = jax.vjp(gelu_product, branch_y, states)
    gated_low = gated_val.astype(jnp.bfloat16)
    recurrent = matmul(gated_low, proj_out)
    middle = inputs + recurrent
    normed_two, norm_two_pull = jax.vjp(rms_scale, middle, norm_gains[1])
    normed_two_low = normed_two.astype(jnp.bfloat16)
    group_rows = lax.all_gather(normed_two_low, "tp", axis=0, tiled=True)
    gate_val = matmul(group_rows, w_gate)
    up_val = matmul(group_rows, w_up)
    hidden_val, mlp_pull = jax.vjp(gelu_product, gate_val, up_val)
    hidden = hidden_val.astype(jnp.bfloat16)
    mlp_out = lax.psum_scatter(
        matmul(hidden, w_down).astype(jnp.bfloat16), "tp", scatter_dimension=0, tiled=True
    ).astype(jnp.float32)
    layer_out = (middle + mlp_out).astype(jnp.bfloat16)
    grad_out = cotangent[0].astype(jnp.float32)
    group_grad = lax.all_gather(cotangent[0], "tp", axis=0, tiled=True)
    w_down_grad = matmul_left(hidden, group_grad)
    grad_hidden = matmul_right(group_grad, w_down)
    grad_gate, grad_up = mlp_pull(grad_hidden)
    grad_gate = grad_gate.astype(jnp.bfloat16)
    grad_up = grad_up.astype(jnp.bfloat16)
    w_gate_grad = matmul_left(group_rows, grad_gate)
    w_up_grad = matmul_left(group_rows, grad_up)
    grad_normed_two = lax.psum_scatter(
        (matmul_right(grad_gate, w_gate) + matmul_right(grad_up, w_up)).astype(jnp.bfloat16),
        "tp",
        scatter_dimension=0,
        tiled=True,
    ).astype(jnp.float32)
    grad_middle, gain_two_grad = norm_two_pull(grad_normed_two)
    grad_middle = grad_middle + grad_out
    grad_rec = grad_middle.astype(jnp.bfloat16)
    grad_gated = matmul_right(grad_rec, proj_out)
    grad_branch_y, grad_direct = gated_pull(grad_gated)
    grad_branch_y = grad_branch_y.astype(jnp.bfloat16)
    decay_next = jnp.concatenate([decay_rate[1:], jnp.ones_like(decay_rate[:1])], axis=0)
    reach_back, local_grads = lax.associative_scan(
        combine_state, (decay_next, grad_direct), reverse=True, axis=0
    )
    outgoing = carry_across(decay_rate[0] * reach_back[0], decay_rate[0] * local_grads[0], True)
    state_grads = local_grads + reach_back * outgoing
    prior_states = jnp.concatenate([incoming[None], states[:-1]], axis=0)
    grad_conv, grad_in, grad_rate, a_local_grad = lru_pull(
        (state_grads * prior_states, state_grads)
    )
    grad_pre = jnp.stack([grad_in, grad_rate]).astype(jnp.bfloat16)
    pre_sums = jnp.sum(grad_pre.astype(jnp.float32), axis=1)
    pre_blocks = grad_pre.reshape(2, row_count, head_count, block_size)
    gate_blocks_grad = jnp.einsum(
        "lhb,glhc->ghbc", conv_blocks, pre_blocks, preferred_element_type=jnp.float32
    )
    gate_back = jnp.einsum(
        "glhc,ghbc->lhb", pre_blocks, gate_blocks, preferred_element_type=jnp.float32
    ).reshape(row_count, full_width)
    grad_conv = grad_conv + gate_back
    conv_w_rows = [jnp.sum(grad_conv * padded_x[rim_size:], axis=0)]
    grad_padded = (
        jnp.zeros((rec_len + rim_size, full_width), jnp.float32)
        .at[rim_size:]
        .add(conv_w[0] * grad_conv)
    )
    for offset in range(1, rim_size + 1):
        masked = valid_list[offset - 1][:, None] * grad_conv
        conv_w_rows.append(
            jnp.sum(masked * padded_x[rim_size - offset : rim_size - offset + rec_len], axis=0)
        )
        grad_padded = grad_padded.at[rim_size - offset : rim_size - offset + rec_len].add(
            conv_w[offset] * masked
        )
    returned = from_behind(grad_padded[:rim_size], "tp", -1)
    grad_x_branch = (
        grad_padded[rim_size:].at[rec_len - rim_size :].add(returned).astype(jnp.bfloat16)
    )
    conv_w_grad = jnp.stack(conv_w_rows)
    lru_bias_grad = jnp.concatenate([jnp.sum(grad_conv, axis=0)[None], pre_sums], axis=0)
    grad_normed = matmul_right(grad_x_branch, proj_x) + matmul_right(grad_branch_y, proj_y)
    grad_inputs, gain_one_grad = norm_pull(grad_normed)
    input_grad = grad_middle + grad_inputs
    w_x_grad, w_y_grad, w_out_grad = (
        lax.psum_scatter(
            matmul_left(normed_low, grad_x_branch).astype(jnp.bfloat16),
            "tp",
            scatter_dimension=1,
            tiled=True,
        ).astype(jnp.float32),
        lax.psum_scatter(
            matmul_left(normed_low, grad_branch_y).astype(jnp.bfloat16),
            "tp",
            scatter_dimension=1,
            tiled=True,
        ).astype(jnp.float32),
        lax.psum_scatter(
            matmul_left(gated_low, grad_rec).astype(jnp.bfloat16),
            "tp",
            scatter_dimension=0,
            tiled=True,
        ).astype(jnp.float32),
    )
    norm_gains_grad = jnp.stack([gain_one_grad, gain_two_grad])
    totals = (
        lax.psum_scatter(
            w_x_grad.astype(jnp.bfloat16), "dp", scatter_dimension=0, tiled=True
        ).astype(jnp.float32),
        lax.psum_scatter(
            w_y_grad.astype(jnp.bfloat16), "dp", scatter_dimension=0, tiled=True
        ).astype(jnp.float32),
        lax.psum_scatter(
            w_out_grad.astype(jnp.bfloat16), "dp", scatter_dimension=1, tiled=True
        ).astype(jnp.float32),
        lax.psum_scatter(
            w_gate_grad.astype(jnp.bfloat16), "dp", scatter_dimension=0, tiled=True
        ).astype(jnp.float32),
        lax.psum_scatter(
            w_up_grad.astype(jnp.bfloat16), "dp", scatter_dimension=0, tiled=True
        ).astype(jnp.float32),
        lax.psum_scatter(
            w_down_grad.astype(jnp.bfloat16), "dp", scatter_dimension=1, tiled=True
        ).astype(jnp.float32),
        lax.psum_scatter(
            norm_gains_grad.astype(jnp.bfloat16), "dp", scatter_dimension=1, tiled=True
        ).astype(jnp.float32),
        lax.psum_scatter(
            conv_w_grad.astype(jnp.bfloat16), "dp", scatter_dimension=1, tiled=True
        ).astype(jnp.float32),
        lax.psum_scatter(
            lru_bias_grad.astype(jnp.bfloat16), "dp", scatter_dimension=1, tiled=True
        ).astype(jnp.float32),
        lax.psum_scatter(
            a_local_grad.astype(jnp.bfloat16), "dp", scatter_dimension=0, tiled=True
        ).astype(jnp.float32),
        lax.psum_scatter(
            gate_blocks_grad.astype(jnp.bfloat16), "dp", scatter_dimension=2, tiled=True
        ).astype(jnp.float32),
    )
    reduced_small = (
        lax.psum(totals[6].astype(jnp.bfloat16), "tp").astype(jnp.float32),
        lax.psum(totals[7].astype(jnp.bfloat16), "tp").astype(jnp.float32),
        lax.psum(totals[8].astype(jnp.bfloat16), "tp").astype(jnp.float32),
        lax.psum(totals[9].astype(jnp.bfloat16), "tp").astype(jnp.float32),
        lax.psum(totals[10].astype(jnp.bfloat16), "tp").astype(jnp.float32),
    )
    return (
        layer_out[None],
        input_grad[None],
        reduced_small[0],
        totals[0],
        totals[1],
        reduced_small[1],
        reduced_small[2],
        reduced_small[3],
        reduced_small[4],
        totals[2],
        totals[3],
        totals[4],
        totals[5],
    )


def solution(mesh):
    rows, cols = mesh.shape["dp"], mesh.shape["tp"]
    by_channels = cols == 2 and rows >= 16 and rows & (rows - 1) == 0

    def step(*args):
        heads, model = args[9].shape[1], args[3].shape[1]
        fits = by_channels and heads % cols == 0 and model % (128 * rows) == 0
        return (local_channels if fits else local)(*args)

    return jax.shard_map(
        step,
        mesh=mesh,
        in_specs=(
            P("dp", "tp", None),
            P("dp", "tp", None),
            P("dp", "tp"),
            P(),
            P(None, "tp"),
            P(None, "tp"),
            P(),
            P(),
            P(),
            P(),
            P("tp", None),
            P(None, "tp"),
            P(None, "tp"),
            P("tp", None),
        ),
        out_specs=(
            P("dp", "tp", None),
            P("dp", "tp", None),
            P(None, "dp"),
            P("dp", "tp"),
            P("dp", "tp"),
            P(None, "dp"),
            P(None, "dp"),
            P("dp"),
            P(None, None, "dp", None),
            P("tp", "dp"),
            P("dp", "tp"),
            P("dp", "tp"),
            P("tp", "dp"),
        ),
        check_vma=False,
    )
```

```python
import functools

import jax
import jax.numpy as jnp
from jax import lax
from jax.experimental import pallas as pl
from jax.experimental.pallas import tpu as pltpu
from jax.sharding import PartitionSpec as P

EPS = 1e-06
F32, BF16 = jnp.float32, jnp.bfloat16
GELU_A, GELU_B = 0.7978845608028654, 0.044715
MESH = pl.DeviceIdType.MESH


AT_ONCE = 8
SEGMENTS = 8


def in_steps(own, other, into, first):
    steps = own.shape[0] // SEGMENTS
    for piece, spot in ((own, 0), (other, SEGMENTS)):
        rows = piece[...].astype(F32).reshape(SEGMENTS, steps, piece.shape[1])
        into[first : first + steps, spot : spot + SEGMENTS, :] = jnp.swapaxes(rows, 0, 1)


def in_rows(source, own, other):
    steps, _, lanes = source.shape
    for piece, spot in ((own, 0), (other, SEGMENTS)):
        rows = jnp.swapaxes(source[:, spot : spot + SEGMENTS, :], 0, 1)
        piece[...] = rows.reshape(SEGMENTS * steps, lanes).astype(piece.dtype)


def from_segment(value, place, later):
    segment = lax.broadcasted_iota(jnp.int32, value.shape, 1)
    if later:
        return jnp.where(segment == 2 * SEGMENTS - 1 - SEGMENTS * place, 0.0, pltpu.roll(value, 2 * SEGMENTS - 1, 1))
    return jnp.where(segment == SEGMENTS * place, 0.0, pltpu.roll(value, 1, 1))


def entering(added, factor, place, later):
    def turned(value):
        return jnp.where(place == 1, pltpu.roll(value, SEGMENTS, 0), value)

    added, factor = turned(added), turned(factor)
    state = jnp.zeros_like(added[0:1])
    rows = [None] * (2 * SEGMENTS)
    for index in reversed(range(2 * SEGMENTS)) if later else range(2 * SEGMENTS):
        rows[index] = state
        state = added[index : index + 1] + factor[index : index + 1] * state
    return turned(jnp.concatenate(rows, axis=0))


def wide_mask(mask_ref, index, first, count):
    mask = mask_ref[index, pl.ds(first, count)]
    return jnp.concatenate([mask, mask], axis=2)


def decay_terms(rate_gate, prm_ref):
    log_decay = prm_ref[7:8, :] * rate_gate
    decay = jnp.exp(log_decay)
    squared = decay * decay
    gap = jnp.maximum(-jnp.tanh(log_decay) * (1.0 + squared), 1e-37)
    return decay, squared, gap, lax.rsqrt(gap)


def rec_fwd_kernel(
    bx_own, bx_oth, by_own, by_oth, mask_ref, prm_ref, gate_ref,
    gated_own, gated_oth, state_ref, in_ref, rate_ref, conv_ref, xs, ys, pre, factor,
):
    place = lax.axis_index("tp")
    steps, both, lanes = state_ref.shape
    in_steps(bx_own, bx_oth, xs, 3)
    xs[0:3] = from_segment(xs[steps : steps + 3], place, False)
    in_steps(by_own, by_oth, ys, 0)
    taps = [prm_ref[k : k + 1, :] for k in range(4)]

    def conv_step(index, _):
        at = index * AT_ONCE
        total = taps[0] * xs[pl.ds(at + 3, AT_ONCE)] + prm_ref[4:5, :]
        for k in (1, 2, 3):
            total = total + taps[k] * (wide_mask(mask_ref, k - 1, at, AT_ONCE) * xs[pl.ds(at + 3 - k, AT_ONCE)])
        conv_ref[pl.ds(at, AT_ONCE)] = total.astype(BF16)
        return 0

    lax.fori_loop(0, steps // AT_ONCE, conv_step, 0)

    def gate_step(index, _):
        conv = conv_ref[pl.ds(index * 16, 16)].reshape(16 * both, lanes)
        rows = pl.ds(pl.multiple_of(index * 16 * both, 16 * both), 16 * both)
        pre[rows, 0:lanes] = jnp.dot(conv, gate_ref[0, 0], preferred_element_type=F32)
        pre[rows, lanes:] = jnp.dot(conv, gate_ref[1, 0], preferred_element_type=F32)
        return 0

    lax.fori_loop(0, steps // 16, gate_step, 0)

    def scan_step(index, carried):
        state, product = carried
        at = index * AT_ONCE
        block = pl.ds(at, AT_ONCE)
        rows = pl.ds(pl.multiple_of(at * both, AT_ONCE * both), AT_ONCE * both)
        shape = (AT_ONCE, both, lanes)
        in_gate = jax.nn.sigmoid(pre[rows, 0:lanes] + prm_ref[5:6, :]).reshape(shape)
        rate_gate = (1.0 / (1.0 + jnp.exp(-(pre[rows, lanes:] + prm_ref[6:7, :])))).reshape(shape)
        in_ref[block] = in_gate
        rate_ref[block] = rate_gate
        keep = wide_mask(mask_ref, 0, at, AT_ONCE)
        decay, _, gap, inverse = decay_terms(rate_gate, prm_ref)
        scaling = (1.0 - keep) + keep * (gap * inverse)
        pushed = conv_ref[block].astype(F32) * in_gate * scaling
        coef = decay * keep
        for one in range(AT_ONCE):
            state = coef[one] * state + pushed[one]
            product = coef[one] * product
            state_ref[at + one] = state
            factor[at + one] = product
        return state, product

    zero = jnp.zeros((both, lanes), F32)
    state, product = lax.fori_loop(0, steps // AT_ONCE, scan_step, (zero, zero + 1.0))
    enters = entering(state, product, place, False)

    def gated_step(index, _):
        block = pl.ds(index * AT_ONCE, AT_ONCE)
        state = state_ref[block] + factor[block] * enters
        state_ref[block] = state
        y = ys[block]
        tanh = jnp.tanh(GELU_A * y * (1.0 + GELU_B * (y * y)))
        ys[block] = state * (0.5 * y * (1.0 + tanh))
        return 0

    lax.fori_loop(0, steps // AT_ONCE, gated_step, 0)
    in_rows(ys, gated_own, gated_oth)


def fold(value):
    return jnp.sum(value, axis=0)


def rec_bwd_kernel(
    count, bx_own, bx_oth, by_own, by_oth, state_ref, in_ref, rate_ref, conv_ref, up_own, up_oth, mask_ref, prm_ref, gate_ref,
    gx_own, gx_oth, gy_own, gy_oth, gw_ref, sum_ref, xs, ys, us, gs, factor, to_log, to_in, to_rate, to_conv, gc, dg, gw,
):
    place = lax.axis_index("tp")
    steps, both, lanes = state_ref.shape
    length = steps * both
    in_steps(bx_own, bx_oth, xs, 3)
    xs[0:3] = from_segment(xs[steps : steps + 3], place, False)
    in_steps(by_own, by_oth, ys, 0)
    in_steps(up_own, up_oth, us, 0)

    def scan_step(index, carried):
        sent, product = carried
        at = steps - AT_ONCE - index * AT_ONCE
        block = pl.ds(at, AT_ONCE)
        in_gate, rate_gate = in_ref[block], rate_ref[block]
        keep = wide_mask(mask_ref, 0, at, AT_ONCE)
        decay, squared, gap, inverse = decay_terms(rate_gate, prm_ref)
        scaling = (1.0 - keep) + keep * (gap * inverse)
        y = ys[block]
        y2 = y * y
        tanh = jnp.tanh(GELU_A * y * (1.0 + GELU_B * y2))
        lift = 0.5 + 0.5 * tanh
        slope = lift + y * (1.0 - tanh * tanh) * (0.5 * GELU_A + (1.5 * GELU_A * GELU_B) * y2)
        up = us[block]
        state = state_ref[block]
        ys[block] = up * state * slope
        direct = up * (y * lift)
        coef = decay * keep
        entered = conv_ref[block].astype(F32) * in_gate
        pushed = entered * scaling
        to_log[block] = ((state - pushed) - entered * (keep * squared * inverse)) * rate_gate
        to_in[block] = pushed * (1.0 - in_gate)
        to_rate[block] = (1.0 - rate_gate) * prm_ref[7:8, :]
        to_conv[block] = in_gate * scaling
        for one in reversed(range(AT_ONCE)):
            grad = direct[one] + sent
            gs[at + one] = grad
            factor[at + one] = product
            sent = coef[one] * grad
            product = coef[one] * product
        return sent, product

    zero = jnp.zeros((both, lanes), F32)
    sent, product = lax.fori_loop(0, steps // AT_ONCE, scan_step, (zero, zero + 1.0))
    enters = entering(sent, product, place, True)

    def grad_step(index, sum_log):
        at = index * AT_ONCE
        block = pl.ds(at, AT_ONCE)
        rows = pl.ds(pl.multiple_of(at * both, AT_ONCE * both), AT_ONCE * both)
        grad = gs[block] + factor[block] * enters
        through = grad * to_log[block]
        dg[rows, 0:lanes] = (grad * to_in[block]).astype(BF16).reshape(AT_ONCE * both, lanes)
        dg[rows, lanes:] = (through * to_rate[block]).astype(BF16).reshape(AT_ONCE * both, lanes)
        gc[block] = grad * to_conv[block]
        return sum_log + fold(through)

    sum_log = lax.fori_loop(0, steps // AT_ONCE, grad_step, zero)

    def back_step(index, _):
        rows = pl.ds(pl.multiple_of(index * 16 * both, 16 * both), 16 * both)
        more = matmul_right(dg[rows, 0:lanes], gate_ref[0, 0]) + matmul_right(dg[rows, lanes:], gate_ref[1, 0])
        gc[pl.ds(index * 16, 16)] += more.reshape(16, both, lanes)
        return 0

    lax.fori_loop(0, steps // 16, back_step, 0)
    conv = conv_ref[...].reshape(length, lanes)
    gw[0:lanes, :] = matmul_left(conv, dg[:, 0:lanes]).astype(BF16)
    gw[lanes:, :] = matmul_left(conv, dg[:, lanes:]).astype(BF16)
    gate_sums = jnp.dot(jnp.ones((8, length), BF16), dg[...], preferred_element_type=F32)
    rows_each = lanes // count
    for block in range(count):
        for gate in (0, 1):
            source = gate * lanes + block * rows_each
            gw_ref[block, 0, gate * rows_each : (gate + 1) * rows_each, :] = gw[source : source + rows_each, :]
    gc[steps : steps + 3] = from_segment(gc[0:3], place, True)
    taps = [prm_ref[k : k + 1, :] for k in range(4)]

    def conv_step(index, sums):
        at = index * AT_ONCE
        here = gc[pl.ds(at, AT_ONCE)]
        total = taps[0] * here
        sums = [sums[0] + fold(here), sums[1] + fold(here * xs[pl.ds(at + 3, AT_ONCE)])] + list(sums[2:])
        for k in (1, 2, 3):
            total = total + taps[k] * (gc[pl.ds(at + k, AT_ONCE)] * wide_mask(mask_ref, k - 1, at + k, AT_ONCE))
            masked = here * wide_mask(mask_ref, k - 1, at, AT_ONCE)
            sums[k + 1] = sums[k + 1] + fold(masked * xs[pl.ds(at + 3 - k, AT_ONCE)])
        us[pl.ds(at, AT_ONCE)] = total
        return tuple(sums)

    sums = lax.fori_loop(0, steps // AT_ONCE, conv_step, (zero,) * 5)
    for index, value in ((0, sums[1]), (1, sums[2]), (2, sums[3]), (3, sums[4]), (4, sums[0]), (7, sum_log)):
        sum_ref[index : index + 1, :] = jnp.sum(value, axis=0, keepdims=True)
    sum_ref[5:6, :] = gate_sums[0:1, 0:lanes]
    sum_ref[6:7, :] = gate_sums[0:1, lanes:]
    in_rows(us, gx_own, gx_oth)
    in_rows(ys, gy_own, gy_oth)


def rec_specs(half, lanes):
    steps = half // SEGMENTS
    piece = pl.BlockSpec((half, lanes), lambda h: (0, h))
    stepped = pl.BlockSpec((steps, 2 * SEGMENTS, lanes), lambda h: (0, 0, h))
    mask = pl.BlockSpec((3, steps + 3, 2 * SEGMENTS, 128), lambda h: (0, 0, 0, 0))
    prm = pl.BlockSpec((8, lanes), lambda h: (0, h))
    gate = pl.BlockSpec((2, 1, lanes, lanes), lambda h: (0, h, 0, 0))
    return piece, stepped, mask, prm, gate


def rec_fwd(bx_own, bx_oth, by_own, by_oth, mask, prm, gates):
    half, width = bx_own.shape
    length, lanes, heads = 2 * half, gates.shape[2], gates.shape[1]
    steps, both = half // SEGMENTS, 2 * SEGMENTS
    piece, stepped, mask_spec, prm_spec, gate_spec = rec_specs(half, lanes)
    out = jax.ShapeDtypeStruct((half, width), BF16)
    kept = jax.ShapeDtypeStruct((steps, both, width), F32)
    return pl.pallas_call(
        rec_fwd_kernel,
        grid=(heads,),
        in_specs=[piece] * 4 + [mask_spec, prm_spec, gate_spec],
        out_specs=[piece] * 2 + [stepped] * 4,
        out_shape=[out, out, kept, kept, kept, jax.ShapeDtypeStruct((steps, both, width), BF16)],
        scratch_shapes=[
            pltpu.VMEM((steps + 3, both, lanes), F32),
            pltpu.VMEM((steps, both, lanes), F32),
            pltpu.VMEM((length, 2 * lanes), F32),
            pltpu.VMEM((steps, both, lanes), F32),
        ],
        compiler_params=pltpu.CompilerParams(vmem_limit_bytes=40 << 20),
        cost_estimate=pl.CostEstimate(
            flops=4 * length * width * lanes + 100 * length * width,
            bytes_accessed=26 * length * width,
            transcendentals=6 * length * width,
        ),
        name="rec_fwd",
    )(bx_own, bx_oth, by_own, by_oth, mask, prm, gates)


def rec_bwd(bx_own, bx_oth, by_own, by_oth, kept, up_own, up_oth, mask, prm, gates, count):
    half, width = bx_own.shape
    length, lanes, heads = 2 * half, gates.shape[2], gates.shape[1]
    steps, both = half // SEGMENTS, 2 * SEGMENTS
    piece, stepped, mask_spec, prm_spec, gate_spec = rec_specs(half, lanes)
    block = pltpu.VMEM((steps, both, lanes), F32)
    padded = pltpu.VMEM((steps + 3, both, lanes), F32)
    return pl.pallas_call(
        functools.partial(rec_bwd_kernel, count),
        grid=(heads,),
        in_specs=[piece] * 4 + [stepped] * 4 + [piece] * 2 + [mask_spec, prm_spec, gate_spec],
        out_specs=[piece] * 4 + [pl.BlockSpec((count, 1, 2 * lanes // count, lanes), lambda h: (0, h, 0, 0)), prm_spec],
        out_shape=[jax.ShapeDtypeStruct((half, width), BF16)] * 4
        + [
            jax.ShapeDtypeStruct((count, heads, 2 * lanes // count, lanes), BF16),
            jax.ShapeDtypeStruct((8, width), F32),
        ],
        scratch_shapes=[padded]
        + [block] * 8
        + [padded, pltpu.VMEM((length, 2 * lanes), BF16), pltpu.VMEM((2 * lanes, lanes), BF16)],
        compiler_params=pltpu.CompilerParams(vmem_limit_bytes=52 << 20),
        cost_estimate=pl.CostEstimate(
            flops=8 * length * width * lanes + 150 * length * width,
            bytes_accessed=34 * length * width,
            transcendentals=4 * length * width,
        ),
        name="rec_bwd",
    )(bx_own, bx_oth, by_own, by_oth, *kept, up_own, up_oth, mask, prm, gates)


def stage_bits(count, crossed=False):
    bits = [1 << bit for bit in range(count.bit_length() - 1)]
    return [bits[0], bits[2], bits[1]] + bits[3:] if crossed else bits


def block_at(place, bits):
    return sum(bit for step, bit in enumerate(bits) if (place >> (len(bits) - 1 - step)) & 1)


def block_from(me, place, bits):
    relative = block_at(place, bits)
    block = 0
    for bit in bits:
        mine = lax.rem(me // bit, 2)
        block = block + bit * (1 - mine if relative & bit else mine)
    return block


def arrange_kernel(bits, first, second, first_out, second_out):
    @pl.when(pl.program_id(0) == 0)
    def _():
        arranged(first, first_out, bits)

    @pl.when(pl.program_id(0) == 1)
    def _():
        arranged(second, second_out, bits)


def arrange(first, second, bits):
    whole = pl.BlockSpec(first.shape, lambda i: (0, 0))
    shape = jax.ShapeDtypeStruct(first.shape, first.dtype)
    return pl.pallas_call(
        functools.partial(arrange_kernel, bits),
        grid=(2,),
        in_specs=[whole, whole],
        out_specs=[whole, whole],
        out_shape=[shape, shape],
        compiler_params=pltpu.CompilerParams(vmem_limit_bytes=24 << 20),
        cost_estimate=pl.CostEstimate(flops=0, bytes_accessed=12 * first.size, transcendentals=0),
        name="arrange",
    )(first, second)


def weight_grad_kernel(splits, own_a, own_b, oth_a, oth_b, right_own, right_oth, sent_next, kept, staged, landed, send_sem, recv_sem):
    step = pl.program_id(0)
    half = 2 * splits
    me = lax.axis_index("dp")
    partner = {"dp": me + 1 - 2 * lax.rem(me, 2)}

    @pl.when(step == 0)
    def _():
        barrier = pltpu.get_barrier_semaphore()
        pl.semaphore_signal(barrier, inc=1, device_id=partner, device_id_type=MESH)
        pl.semaphore_wait(barrier, 1)

    def copy(tile):
        return pltpu.make_async_remote_copy(
            src_ref=staged.at[tile],
            dst_ref=landed.at[tile],
            send_sem=send_sem.at[tile],
            recv_sem=recv_sem.at[tile],
            device_id=partner,
            device_id_type=MESH,
        )

    left_own = jnp.concatenate([own_a[...], own_b[...]], axis=1)
    left_oth = jnp.concatenate([oth_a[...], oth_b[...]], axis=1)
    total = matmul_left(left_own, right_own[...]) + matmul_left(left_oth, right_oth[...])

    @pl.when(step < half)
    def _():
        staged[step] = total.astype(BF16)
        copy(step).start()

    @pl.when(step >= half)
    def _():
        copy(step - half).wait_recv()
        value = (total + landed[step - half].astype(F32)).astype(BF16)

        @pl.when(step < half + splits)
        def _():
            sent_next[...] = value

        @pl.when(step >= half + splits)
        def _():
            kept[...] = value

    @pl.when(step == 2 * half - 1)
    def _():
        for tile in range(half):
            copy(tile).wait_send()


def weight_grad(left_own, left_oth, right_own, right_oth, crossed, cost):
    half, cols = right_own.shape
    rows = left_own.shape[1] // 4
    splits = 2 if cols > 2048 else 1
    wide = cols // splits
    out = pltpu.HBM((rows, cols), BF16)

    def tile(i):
        return lax.rem((i + 1) // 2, 2) if splits == 2 else 0

    def columns(part):
        def index(i):
            quarter = 3 - i // splits
            return 0, (quarter // 2 * 4 + part * 2 + lax.rem(quarter, 2) if crossed else quarter * 2 + part)

        return pl.BlockSpec((half, rows // 2), index)

    last = 4 * splits - 1
    return pl.pallas_call(
        functools.partial(weight_grad_kernel, splits),
        grid=(4 * splits,),
        in_specs=[
            columns(0),
            columns(1),
            columns(0),
            columns(1),
            pl.BlockSpec((half, wide), lambda i: (0, tile(i))),
            pl.BlockSpec((half, wide), lambda i: (0, tile(i))),
        ],
        out_specs=[
            pl.BlockSpec((rows, wide), lambda i: (0, jnp.where(i < last - 2, 0, 1) if splits == 2 else 0)),
            pl.BlockSpec((rows, wide), lambda i: (0, jnp.where(i < last, 1, 0) if splits == 2 else 0)),
        ],
        out_shape=[out, out],
        scratch_shapes=[
            pltpu.VMEM((2 * splits, rows, wide), BF16),
            pltpu.VMEM((2 * splits, rows, wide), BF16),
            pltpu.SemaphoreType.DMA((2 * splits,)),
            pltpu.SemaphoreType.DMA((2 * splits,)),
        ],
        compiler_params=pltpu.CompilerParams(
            collective_id=2 * splits + crossed, has_side_effects=True, vmem_limit_bytes=48 << 20
        ),
        cost_estimate=pl.CostEstimate(
            flops=int(cost * 16 * half * rows * cols), bytes_accessed=int(cost * 16 * half * cols), transcendentals=0
        ),
        name="weight_grad",
    )(left_own, left_own, left_oth, left_oth, right_own, right_oth)


ROWS = 64


def arranged(source, into, bits):
    me = lax.axis_index("dp")
    count = 1 << len(bits)
    cols = source.shape[1] // count
    for place in range(count):
        block = pl.ds(pl.multiple_of(block_from(me, place, bits) * cols, cols), cols)
        into[:, place * cols : (place + 1) * cols] = source[:, block]


def feed_kernel(bits, sub, tokens, part, other, gain, grad_hidden, w_gate, w_up, middle, cols, hidden, grad_gate, grad_up, normed):
    @pl.when(pl.program_id(0) == 0)
    def _():
        def rows_step(index, _):
            rows = pl.ds(pl.multiple_of(index * ROWS, ROWS), ROWS)
            total = tokens[rows, :].astype(F32) + (part[rows, :].astype(F32) + other[rows, :].astype(F32))
            middle[rows, :] = total
            scale = lax.rsqrt(jnp.mean(total * total, axis=-1, keepdims=True) + EPS)
            normed[rows, :] = (total * scale * gain[...]).astype(BF16)
            return 0

        lax.fori_loop(0, tokens.shape[0] // ROWS, rows_step, 0)
        arranged(normed, cols, bits)

    for start in range(0, w_gate.shape[1], sub):
        part_cols = slice(start, start + sub)
        gate = jnp.dot(normed[...], w_gate[:, part_cols], preferred_element_type=F32)
        up = jnp.dot(normed[...], w_up[:, part_cols], preferred_element_type=F32)
        squared = gate * gate
        tanh = jnp.tanh(GELU_A * gate * (1.0 + GELU_B * squared))
        lift = 0.5 + 0.5 * tanh
        slope = lift + gate * (1.0 - tanh * tanh) * (0.5 * GELU_A + (1.5 * GELU_A * GELU_B) * squared)
        gelu = gate * lift
        back = grad_hidden[:, part_cols].astype(F32)
        hidden[:, part_cols] = (gelu * up).astype(BF16)
        grad_gate[:, part_cols] = (back * up * slope).astype(BF16)
        grad_up[:, part_cols] = (back * gelu).astype(BF16)


def feed(tokens, part, other, gain, grad_hidden, w_gate, w_up, bits, wide=512, sub=256):
    rows, model = tokens.shape
    cols = w_gate.shape[1]
    whole = pl.BlockSpec((rows, model), lambda n: (0, 0))
    piece = pl.BlockSpec((rows, wide), lambda n: (0, n))
    weight = pl.BlockSpec((model, wide), lambda n: (0, n))
    out = jax.ShapeDtypeStruct((rows, cols), BF16)
    return pl.pallas_call(
        functools.partial(feed_kernel, bits, sub),
        grid=(cols // wide,),
        in_specs=[whole] * 3 + [pl.BlockSpec((1, model), lambda n: (0, 0)), piece, weight, weight],
        out_specs=[whole, whole, piece, piece, piece],
        out_shape=[jax.ShapeDtypeStruct((rows, model), F32), jax.ShapeDtypeStruct((rows, model), BF16), out, out, out],
        scratch_shapes=[pltpu.VMEM((rows, model), BF16)],
        compiler_params=pltpu.CompilerParams(vmem_limit_bytes=56 << 20),
        cost_estimate=pl.CostEstimate(
            flops=4 * rows * model * cols, bytes_accessed=4 * model * cols + 12 * rows * cols, transcendentals=rows * cols
        ),
        name="feed",
    )(tokens, part, other, gain, grad_hidden, w_gate, w_up)


def pull_kernel(bits, middle, back, other, cot, gain, weight, grad, cols, into, rec):
    @pl.when(pl.program_id(0) == 0)
    def _():
        def rows_step(index, _):
            rows = pl.ds(pl.multiple_of(index * ROWS, ROWS), ROWS)
            values = middle[rows, :]
            scale = lax.rsqrt(jnp.mean(values * values, axis=-1, keepdims=True) + EPS)
            lifted = gain[...] * (back[rows, :].astype(F32) + other[rows, :].astype(F32))
            pulled = jnp.mean(values * lifted, axis=-1, keepdims=True)
            total = cot[rows, :].astype(F32) + (scale * lifted - values * (scale * scale * scale * pulled))
            grad[rows, :] = total
            rec[rows, :] = total.astype(BF16)
            return 0

        lax.fori_loop(0, middle.shape[0] // ROWS, rows_step, 0)
        arranged(rec, cols, bits)

    into[...] = matmul_right(rec[...], weight[...])


def pull(middle, back, other, cot, gain, weight, bits, wide=640):
    rows, model = middle.shape
    cols = weight.shape[0]
    wide = wide if cols % wide == 0 else cols
    whole = pl.BlockSpec((rows, model), lambda n: (0, 0))
    return pl.pallas_call(
        functools.partial(pull_kernel, bits),
        grid=(cols // wide,),
        in_specs=[whole] * 4 + [pl.BlockSpec((1, model), lambda n: (0, 0)), pl.BlockSpec((wide, model), lambda n: (n, 0))],
        out_specs=[whole, whole, pl.BlockSpec((rows, wide), lambda n: (0, n))],
        out_shape=[
            jax.ShapeDtypeStruct((rows, model), F32),
            jax.ShapeDtypeStruct((rows, model), BF16),
            jax.ShapeDtypeStruct((rows, cols), F32),
        ],
        scratch_shapes=[pltpu.VMEM((rows, model), BF16)],
        compiler_params=pltpu.CompilerParams(vmem_limit_bytes=56 << 20),
        cost_estimate=pl.CostEstimate(
            flops=2 * rows * model * cols, bytes_accessed=16 * rows * model + 4 * rows * cols, transcendentals=0
        ),
        name="pull",
    )(middle, back, other, cot, gain, weight)


def two_back_kernel(first, first_w, second, second_w, out):
    out[...] = (matmul_right(first[...], first_w[...]) + matmul_right(second[...], second_w[...])).astype(BF16)


def two_back(first, first_w, second, second_w, cost=1.0):
    rows, depth = first.shape
    cols = first_w.shape[0]
    step = 512
    left = pl.BlockSpec((rows, depth), lambda n: (0, 0))
    right = pl.BlockSpec((step, depth), lambda n: (n, 0))
    return pl.pallas_call(
        two_back_kernel,
        grid=(cols // step,),
        in_specs=[left, right, left, right],
        out_specs=pl.BlockSpec((rows, step), lambda n: (0, n)),
        out_shape=jax.ShapeDtypeStruct((rows, cols), BF16),
        compiler_params=pltpu.CompilerParams(vmem_limit_bytes=48 << 20),
        cost_estimate=pl.CostEstimate(
            flops=int(cost * 4 * rows * depth * cols), bytes_accessed=int(cost * 4 * depth * (rows + cols)), transcendentals=0
        ),
        name="two_back",
    )(first, first_w, second, second_w)


def swap(value):
    return lax.ppermute(value, "tp", [(0, 1), (1, 0)])


def flip(value, bit):
    count = lax.axis_size("dp")
    return lax.ppermute(value, "dp", [(source, source ^ bit) for source in range(count)])


class Reduction:
    def __init__(self, left, right, count, crossed=False, cost=1.0):
        self.bits = stage_bits(count, crossed)[1:]
        sent, self.keep = weight_grad(*left, *right, crossed, cost)
        self.pass_on(sent)

    def pass_on(self, sent):
        self.received = flip(sent, self.bits.pop(0))

    def step(self, *others):
        received = after(self.received, *others)
        middle = received.shape[0] // 2
        sent = (self.keep[middle:].astype(F32) + received[middle:].astype(F32)).astype(BF16)
        keep = (self.keep[:middle].astype(F32) + received[:middle].astype(F32)).astype(BF16)
        sent, self.keep = lax.optimization_barrier((sent, keep))
        self.pass_on(sent)
        return sent

    def total(self, *others):
        while self.bits:
            self.step(*others)
        return self.keep.astype(F32) + after(self.received, *others).astype(F32)


def after(value, *others):
    return lax.optimization_barrier((value, *others))[0]


def norm_back(values, gain, grad):
    scale = lax.rsqrt(jnp.mean(values * values, axis=-1, keepdims=True) + EPS)
    lifted = gain * grad
    pull = jnp.mean(values * lifted, axis=-1, keepdims=True)
    return scale * lifted - values * (scale * scale * scale * pull)


def local_channels(
    layer_in, cotangent, resets, norm_gains, w_x, w_y, conv_w, lru_bias, a_param, gate_blocks, w_out, w_gate, w_up, w_down,
):
    place = lax.axis_index("tp")
    me = lax.axis_index("dp")
    count = lax.axis_size("dp")
    bits = stage_bits(count)
    width = w_x.shape[1]
    full_width = conv_w.shape[1]
    heads = gate_blocks.shape[1] // 2
    model = norm_gains.shape[1]

    own_in, own_cot = layer_in[0], cotangent[0]
    oth_in = swap(own_in)
    oth_resets = swap(resets[0])
    oth_cot = swap(own_cot)
    normed_own = rms_scale(own_in.astype(F32), norm_gains[0]).astype(BF16)
    bx_own = matmul(normed_own, w_x).astype(BF16)
    by_own = matmul(normed_own, w_y)

    first_place = place == 0
    in_time = jnp.where(first_place, resets[0], oth_resets), jnp.where(first_place, oth_resets, resets[0])
    keep = 1.0 - jnp.concatenate(in_time).astype(F32)
    keep_1 = jnp.concatenate([jnp.ones((1,), F32), keep[:-1]])
    keep_2 = jnp.concatenate([jnp.ones((1,), F32), keep_1[:-1]])
    valid = jnp.stack([keep, keep * keep_1, keep * keep_1 * keep_2]).reshape(3, 2, SEGMENTS, -1)
    valid = jnp.where(first_place, valid, valid[:, ::-1]).reshape(3, 2 * SEGMENTS, -1)
    later = jnp.concatenate([valid[:, 1:, :3], valid[:, :1, :3]], axis=1)
    mask = jnp.swapaxes(jnp.concatenate([valid, later], axis=2), 1, 2)
    mask = jnp.broadcast_to(mask[..., None], mask.shape + (128,))
    table = jnp.concatenate([conv_w, lru_bias, -8.0 * jax.nn.softplus(a_param)[None]], axis=0)
    prm = lax.dynamic_slice(table, (0, place * width), (8, width))
    gates = lax.dynamic_slice_in_dim(gate_blocks, place * heads, heads, axis=1)

    gh_own = matmul_right(after(own_cot, bx_own, by_own), w_down)
    normed_oth = rms_scale(after(oth_in, gh_own).astype(F32), norm_gains[0]).astype(BF16)
    bx_oth = matmul(normed_oth, w_x).astype(BF16)
    by_oth = matmul(normed_oth, w_y)
    gated_own, gated_oth, *kept = rec_fwd(bx_own, bx_oth, by_own, by_oth, mask, prm, gates)

    part_oth = matmul(gated_oth, w_out).astype(BF16)
    swap_own = swap(part_oth)
    part_own = matmul(after(gated_own, part_oth), w_out).astype(BF16)
    swap_oth = swap(part_own)
    gh_oth = matmul_right(after(oth_cot, part_own), w_down)
    cot_cols = arrange(after(own_cot, gh_oth), oth_cot, bits)
    normed_cols = arrange(after(normed_own, cot_cols[0]), normed_oth, bits)
    gains = norm_gains[1:2]

    middle_own, two_own, hidden_own, gg_own, gu_own = feed(
        own_in, part_own, after(swap_own, normed_cols[0]), gains, gh_own, w_gate, w_up, bits
    )
    back_own = two_back(gg_own, w_gate, gu_own, w_up)
    back_own_swapped = swap(back_own)
    middle_oth, two_oth, hidden_oth, gg_oth, gu_oth = feed(
        oth_in, part_oth, after(swap_oth, back_own), gains, gh_oth, w_gate, w_up, bits
    )
    down = Reduction((after(cot_cols[0], hidden_oth), cot_cols[1]), (hidden_own, hidden_oth), count)
    gate = Reduction((after(two_own, down.keep), two_oth), (gg_own, gg_oth), count, True)
    back_oth = two_back(after(gg_oth, gate.keep), w_gate, gu_oth, w_up)
    back_oth_swapped = swap(back_oth)
    _, rec_oth, into_oth = pull(middle_oth, back_oth, back_own_swapped, oth_cot, gains, w_out, bits)
    up = Reduction((after(two_own, into_oth), two_oth), (gu_own, gu_oth), count)
    done = down.step(up.keep)
    done = gate.step(done)
    grad_own, rec_own, into_own = pull(middle_own, back_own, after(back_oth_swapped, done), own_cot, gains, w_out, bits)
    out = Reduction((rec_own, rec_oth), (gated_own, gated_oth), count)
    done = down.step(out.keep)
    gx_own, gx_oth, gy_own, gy_oth, gate_sums, sums = rec_bwd(
        bx_own, bx_oth, by_own, by_oth, kept, after(into_own, done), into_oth, mask, prm, gates, count
    )

    lanes = gate_sums.shape[-1]
    row = jnp.arange(8)[:, None] == 7
    slopes = -8.0 * lax.dynamic_slice(jax.nn.sigmoid(a_param), (place * width,), (width,))
    each = full_width // count
    sums = jnp.swapaxes(jnp.where(row, sums * slopes, sums).reshape(8, count // 2, each), 0, 1)
    sums = jnp.pad(jnp.concatenate([sums, sums], axis=0), ((0, 0), (0, 0), (0, lanes - each))).astype(BF16)
    blocks = jnp.concatenate([gate_sums.reshape(count, -1, lanes), sums], axis=1)
    blocks = lax.psum_scatter(blocks.reshape(-1, lanes), "dp", scatter_dimension=0, tiled=True)

    small_cost = 0.1
    done = up.step(gx_own)
    in_x = Reduction((after(normed_cols[0], done), normed_cols[1]), (gx_own, gx_oth), count, cost=small_cost)
    done = gate.step(in_x.keep)
    in_y = Reduction((after(normed_cols[0], done), normed_cols[1]), (gy_own, gy_oth), count, cost=small_cost)
    out_send = matmul(after(hidden_oth, in_y.keep), w_down).astype(BF16)
    out_swapped = swap(out_send)
    rec_send = two_back(after(gx_oth, out_send), w_x, gy_oth, w_y, small_cost)
    rec_swapped = swap(rec_send)
    down_grad = down.total(rec_send).T
    done = out.step(down_grad)
    rec_keep = two_back(after(gx_own, done), w_x, gy_own, w_y, small_cost)
    done = up.step(rec_keep)
    gate_grad = gate.total(done)
    done = in_x.step(gate_grad)
    done = out.step(done)
    out_keep = matmul(after(hidden_own, done), w_down).astype(BF16)
    done = in_y.step(out_keep)
    layer_out = (middle_own + out_keep.astype(F32) + after(out_swapped, done).astype(F32)).astype(BF16)
    done = in_x.step(layer_out)
    up_grad = up.total(done)
    grad_normed = rec_keep.astype(F32) + after(rec_swapped, up_grad).astype(F32)
    input_grad = grad_own + norm_back(own_in.astype(F32), norm_gains[0], grad_normed)
    out_grad = out.total(input_grad).T
    done = in_y.step(out_grad)
    others = swap(after(blocks, done))
    x_grad = in_x.total(others)
    y_grad = in_y.total(x_grad)

    low, high = jnp.where(first_place, blocks, others), jnp.where(first_place, others, blocks)
    block_sums = jnp.stack([low[:-8], high[:-8]]).astype(F32).reshape(2 * heads, 2, -1, lanes)
    small = jnp.where(me < count // 2, low[-8:], high[-8:])[:, :each].astype(F32)

    block = model // count

    def gain_grad(gain, *pairs):
        weights = sum(
            jnp.sum(lax.dynamic_slice_in_dim(weight, me * block, block, axis=0).astype(F32) * grad, axis=1)
            for weight, grad in pairs
        )
        return weights / lax.dynamic_slice_in_dim(gain, me * block, block, axis=0)

    gains = jnp.stack(
        [
            gain_grad(norm_gains[0], (w_x, x_grad), (w_y, y_grad)),
            gain_grad(norm_gains[1], (w_gate, gate_grad), (w_up, up_grad)),
        ]
    )
    gains = gains + swap(gains)
    return (
        layer_out[None],
        input_grad[None],
        gains,
        x_grad,
        y_grad,
        small[0:4],
        small[4:7],
        small[7],
        jnp.swapaxes(block_sums, 0, 1),
        out_grad,
        gate_grad,
        up_grad,
        down_grad,
    )


def from_behind(value, axis, steps):
    count = lax.axis_size(axis)
    first, last = (max(0, -steps), min(count, count - steps))
    return lax.ppermute(value, axis, [(source, source + steps) for source in range(first, last)])


def rms_scale(values, gain_vec):
    return values * lax.rsqrt(jnp.mean(values * values, axis=-1, keepdims=True) + EPS) * gain_vec


def gelu_product(gate_val, up_val):
    return jax.nn.gelu(gate_val, approximate=True) * up_val


def lru_terms(conv_out, gate_in, gate_rate, a_param, starts):
    keep_mask = 1.0 - starts
    input_gate = jax.nn.sigmoid(gate_in)
    rate_gate = jax.nn.sigmoid(gate_rate)
    log_decay = -8.0 * rate_gate * jax.nn.softplus(a_param)
    scaling = starts + keep_mask * jnp.sqrt(-jnp.expm1(2.0 * log_decay))
    return (jnp.exp(log_decay) * keep_mask, conv_out * input_gate * scaling)


def matmul(first_mat, second_mat):
    return jnp.dot(first_mat, second_mat, preferred_element_type=jnp.float32)


def matmul_left(first_mat, second_mat):
    return lax.dot_general(
        first_mat, second_mat, (((0,), (0,)), ((), ())), preferred_element_type=jnp.float32
    )


def matmul_right(first_mat, second_mat):
    return lax.dot_general(
        first_mat, second_mat, (((1,), (1,)), ((), ())), preferred_element_type=jnp.float32
    )


def combine_state(first_item, second_item):
    return (first_item[0] * second_item[0], second_item[1] + second_item[0] * first_item[1])


def carry_across(coef_end, state_end, reverse):
    incoming = jnp.zeros_like(state_end)
    direction = -1 if reverse else 1
    for turn_index in range(lax.axis_size("tp") - 1):
        incoming = from_behind(state_end + coef_end * incoming, "tp", direction)
    return incoming


def local(
    layer_in,
    cotangent,
    resets,
    norm_gains,
    w_x,
    w_y,
    conv_w,
    lru_bias,
    a_param,
    gate_blocks,
    w_out,
    w_gate,
    w_up,
    w_down,
):
    inputs = layer_in[0].astype(jnp.float32)
    starts = resets[0].astype(jnp.float32)
    keep_mask = 1.0 - starts
    rim_size = conv_w.shape[0] - 1
    head_count = gate_blocks.shape[1]
    block_size = gate_blocks.shape[2]
    full_width = conv_w.shape[1]
    normed, norm_pull = jax.vjp(rms_scale, inputs, norm_gains[0])
    normed_low = normed.astype(jnp.bfloat16)
    proj_x, proj_y, proj_out = (
        lax.all_gather(w_x, "tp", axis=1, tiled=True),
        lax.all_gather(w_y, "tp", axis=1, tiled=True),
        lax.all_gather(w_out, "tp", axis=0, tiled=True),
    )
    rec_len = normed_low.shape[0]
    branch_x = matmul(normed_low, proj_x).astype(jnp.bfloat16)
    branch_y = matmul(normed_low, proj_y)
    rim_rows, rim_keep = from_behind(
        (branch_x[rec_len - rim_size :], keep_mask[rec_len - rim_size :].astype(jnp.bfloat16)),
        "tp",
        1,
    )
    padded_x = jnp.concatenate([rim_rows, branch_x], axis=0).astype(jnp.float32)
    padded_keep = jnp.concatenate([rim_keep.astype(jnp.float32), keep_mask])
    conv_sum = conv_w[0] * padded_x[rim_size:]
    valid_mask = keep_mask
    valid_list = []
    for offset in range(1, rim_size + 1):
        valid_list.append(valid_mask)
        conv_sum = (
            conv_sum
            + valid_mask[:, None]
            * conv_w[offset]
            * padded_x[rim_size - offset : rim_size - offset + rec_len]
        )
        valid_mask = valid_mask * padded_keep[rim_size - offset : rim_size - offset + rec_len]
    conv_out = (conv_sum + lru_bias[0]).astype(jnp.bfloat16)
    row_count = conv_out.shape[0]
    conv_blocks = conv_out.reshape(row_count, head_count, block_size)
    pre_rows = (
        jnp.einsum(
            "lhb,ghbc->glhc", conv_blocks, gate_blocks, preferred_element_type=jnp.float32
        ).reshape(2, row_count, full_width)
        + lru_bias[1:3][:, None, :]
    )
    gate_in = pre_rows[0]
    gate_rate = pre_rows[1]
    conv_float = conv_out.astype(jnp.float32)

    def lru_local(conv_in, in_pre, rate_pre, decay_in):
        return lru_terms(conv_in, in_pre, rate_pre, decay_in, starts[:, None])

    (decay_rate, pushed), lru_pull = jax.vjp(lru_local, conv_float, gate_in, gate_rate, a_param)
    decay_cum, local_states = lax.associative_scan(combine_state, (decay_rate, pushed), axis=0)
    incoming = carry_across(decay_cum[-1], local_states[-1], False)
    states = local_states + decay_cum * incoming
    gated_val, gated_pull = jax.vjp(gelu_product, branch_y, states)
    gated_low = gated_val.astype(jnp.bfloat16)
    recurrent = matmul(gated_low, proj_out)
    middle = inputs + recurrent
    normed_two, norm_two_pull = jax.vjp(rms_scale, middle, norm_gains[1])
    normed_two_low = normed_two.astype(jnp.bfloat16)
    group_rows = lax.all_gather(normed_two_low, "tp", axis=0, tiled=True)
    gate_val = matmul(group_rows, w_gate)
    up_val = matmul(group_rows, w_up)
    hidden_val, mlp_pull = jax.vjp(gelu_product, gate_val, up_val)
    hidden = hidden_val.astype(jnp.bfloat16)
    mlp_out = lax.psum_scatter(
        matmul(hidden, w_down).astype(jnp.bfloat16), "tp", scatter_dimension=0, tiled=True
    ).astype(jnp.float32)
    layer_out = (middle + mlp_out).astype(jnp.bfloat16)
    grad_out = cotangent[0].astype(jnp.float32)
    group_grad = lax.all_gather(cotangent[0], "tp", axis=0, tiled=True)
    w_down_grad = matmul_left(hidden, group_grad)
    grad_hidden = matmul_right(group_grad, w_down)
    grad_gate, grad_up = mlp_pull(grad_hidden)
    grad_gate = grad_gate.astype(jnp.bfloat16)
    grad_up = grad_up.astype(jnp.bfloat16)
    w_gate_grad = matmul_left(group_rows, grad_gate)
    w_up_grad = matmul_left(group_rows, grad_up)
    grad_normed_two = lax.psum_scatter(
        (matmul_right(grad_gate, w_gate) + matmul_right(grad_up, w_up)).astype(jnp.bfloat16),
        "tp",
        scatter_dimension=0,
        tiled=True,
    ).astype(jnp.float32)
    grad_middle, gain_two_grad = norm_two_pull(grad_normed_two)
    grad_middle = grad_middle + grad_out
    grad_rec = grad_middle.astype(jnp.bfloat16)
    grad_gated = matmul_right(grad_rec, proj_out)
    grad_branch_y, grad_direct = gated_pull(grad_gated)
    grad_branch_y = grad_branch_y.astype(jnp.bfloat16)
    decay_next = jnp.concatenate([decay_rate[1:], jnp.ones_like(decay_rate[:1])], axis=0)
    reach_back, local_grads = lax.associative_scan(
        combine_state, (decay_next, grad_direct), reverse=True, axis=0
    )
    outgoing = carry_across(decay_rate[0] * reach_back[0], decay_rate[0] * local_grads[0], True)
    state_grads = local_grads + reach_back * outgoing
    prior_states = jnp.concatenate([incoming[None], states[:-1]], axis=0)
    grad_conv, grad_in, grad_rate, a_local_grad = lru_pull(
        (state_grads * prior_states, state_grads)
    )
    grad_pre = jnp.stack([grad_in, grad_rate]).astype(jnp.bfloat16)
    pre_sums = jnp.sum(grad_pre.astype(jnp.float32), axis=1)
    pre_blocks = grad_pre.reshape(2, row_count, head_count, block_size)
    gate_blocks_grad = jnp.einsum(
        "lhb,glhc->ghbc", conv_blocks, pre_blocks, preferred_element_type=jnp.float32
    )
    gate_back = jnp.einsum(
        "glhc,ghbc->lhb", pre_blocks, gate_blocks, preferred_element_type=jnp.float32
    ).reshape(row_count, full_width)
    grad_conv = grad_conv + gate_back
    conv_w_rows = [jnp.sum(grad_conv * padded_x[rim_size:], axis=0)]
    grad_padded = (
        jnp.zeros((rec_len + rim_size, full_width), jnp.float32)
        .at[rim_size:]
        .add(conv_w[0] * grad_conv)
    )
    for offset in range(1, rim_size + 1):
        masked = valid_list[offset - 1][:, None] * grad_conv
        conv_w_rows.append(
            jnp.sum(masked * padded_x[rim_size - offset : rim_size - offset + rec_len], axis=0)
        )
        grad_padded = grad_padded.at[rim_size - offset : rim_size - offset + rec_len].add(
            conv_w[offset] * masked
        )
    returned = from_behind(grad_padded[:rim_size], "tp", -1)
    grad_x_branch = (
        grad_padded[rim_size:].at[rec_len - rim_size :].add(returned).astype(jnp.bfloat16)
    )
    conv_w_grad = jnp.stack(conv_w_rows)
    lru_bias_grad = jnp.concatenate([jnp.sum(grad_conv, axis=0)[None], pre_sums], axis=0)
    grad_normed = matmul_right(grad_x_branch, proj_x) + matmul_right(grad_branch_y, proj_y)
    grad_inputs, gain_one_grad = norm_pull(grad_normed)
    input_grad = grad_middle + grad_inputs
    w_x_grad, w_y_grad, w_out_grad = (
        lax.psum_scatter(
            matmul_left(normed_low, grad_x_branch).astype(jnp.bfloat16),
            "tp",
            scatter_dimension=1,
            tiled=True,
        ).astype(jnp.float32),
        lax.psum_scatter(
            matmul_left(normed_low, grad_branch_y).astype(jnp.bfloat16),
            "tp",
            scatter_dimension=1,
            tiled=True,
        ).astype(jnp.float32),
        lax.psum_scatter(
            matmul_left(gated_low, grad_rec).astype(jnp.bfloat16),
            "tp",
            scatter_dimension=0,
            tiled=True,
        ).astype(jnp.float32),
    )
    norm_gains_grad = jnp.stack([gain_one_grad, gain_two_grad])
    totals = (
        lax.psum_scatter(
            w_x_grad.astype(jnp.bfloat16), "dp", scatter_dimension=0, tiled=True
        ).astype(jnp.float32),
        lax.psum_scatter(
            w_y_grad.astype(jnp.bfloat16), "dp", scatter_dimension=0, tiled=True
        ).astype(jnp.float32),
        lax.psum_scatter(
            w_out_grad.astype(jnp.bfloat16), "dp", scatter_dimension=1, tiled=True
        ).astype(jnp.float32),
        lax.psum_scatter(
            w_gate_grad.astype(jnp.bfloat16), "dp", scatter_dimension=0, tiled=True
        ).astype(jnp.float32),
        lax.psum_scatter(
            w_up_grad.astype(jnp.bfloat16), "dp", scatter_dimension=0, tiled=True
        ).astype(jnp.float32),
        lax.psum_scatter(
            w_down_grad.astype(jnp.bfloat16), "dp", scatter_dimension=1, tiled=True
        ).astype(jnp.float32),
        lax.psum_scatter(
            norm_gains_grad.astype(jnp.bfloat16), "dp", scatter_dimension=1, tiled=True
        ).astype(jnp.float32),
        lax.psum_scatter(
            conv_w_grad.astype(jnp.bfloat16), "dp", scatter_dimension=1, tiled=True
        ).astype(jnp.float32),
        lax.psum_scatter(
            lru_bias_grad.astype(jnp.bfloat16), "dp", scatter_dimension=1, tiled=True
        ).astype(jnp.float32),
        lax.psum_scatter(
            a_local_grad.astype(jnp.bfloat16), "dp", scatter_dimension=0, tiled=True
        ).astype(jnp.float32),
        lax.psum_scatter(
            gate_blocks_grad.astype(jnp.bfloat16), "dp", scatter_dimension=2, tiled=True
        ).astype(jnp.float32),
    )
    reduced_small = (
        lax.psum(totals[6].astype(jnp.bfloat16), "tp").astype(jnp.float32),
        lax.psum(totals[7].astype(jnp.bfloat16), "tp").astype(jnp.float32),
        lax.psum(totals[8].astype(jnp.bfloat16), "tp").astype(jnp.float32),
        lax.psum(totals[9].astype(jnp.bfloat16), "tp").astype(jnp.float32),
        lax.psum(totals[10].astype(jnp.bfloat16), "tp").astype(jnp.float32),
    )
    return (
        layer_out[None],
        input_grad[None],
        reduced_small[0],
        totals[0],
        totals[1],
        reduced_small[1],
        reduced_small[2],
        reduced_small[3],
        reduced_small[4],
        totals[2],
        totals[3],
        totals[4],
        totals[5],
    )


def solution(mesh):
    rows, cols = mesh.shape["dp"], mesh.shape["tp"]
    by_channels = cols == 2 and rows >= 16 and rows & (rows - 1) == 0

    def step(*args):
        heads, model = args[9].shape[1], args[3].shape[1]
        fits = by_channels and heads % cols == 0 and model % (128 * rows) == 0
        return (local_channels if fits else local)(*args)

    return jax.shard_map(
        step,
        mesh=mesh,
        in_specs=(
            P("dp", "tp", None),
            P("dp", "tp", None),
            P("dp", "tp"),
            P(),
            P(None, "tp"),
            P(None, "tp"),
            P(),
            P(),
            P(),
            P(),
            P("tp", None),
            P(None, "tp"),
            P(None, "tp"),
            P("tp", None),
        ),
        out_specs=(
            P("dp", "tp", None),
            P("dp", "tp", None),
            P(None, "dp"),
            P("dp", "tp"),
            P("dp", "tp"),
            P(None, "dp"),
            P(None, "dp"),
            P("dp"),
            P(None, None, "dp", None),
            P("tp", "dp"),
            P("dp", "tp"),
            P("dp", "tp"),
            P("tp", "dp"),
        ),
        check_vma=False,
    )
```

```python
import functools

import jax
import jax.numpy as jnp
from jax import lax
from jax.experimental import pallas as pl
from jax.experimental.pallas import tpu as pltpu
from jax.sharding import PartitionSpec as P

EPS = 1e-06
F32, BF16 = jnp.float32, jnp.bfloat16
GELU_A, GELU_B = 0.7978845608028654, 0.044715
ORDER = (
    "DK", "GK", "B2", "UK", "OK", "P2", "D1", "G1", "P1", "OUT", "D2", "U1",
    "RB", "G2", "X", "Dt", "O1", "RS", "U2", "Gt", "Y", "O2", "X1", "OS",
    "RK", "IG", "Y1", "Ut", "Ot", "X2", "Y2", "LO", "Xt", "SW", "Yt",
)
CROSSED = "G"
COSTS = {}
MESH = pl.DeviceIdType.MESH


AT_ONCE = 8
SEGMENTS = 8


def in_steps(own, other, into, first):
    steps = own.shape[0] // SEGMENTS
    for piece, spot in ((own, 0), (other, SEGMENTS)):
        rows = piece[...].astype(F32).reshape(SEGMENTS, steps, piece.shape[1])
        into[first : first + steps, spot : spot + SEGMENTS, :] = jnp.swapaxes(rows, 0, 1)


def in_rows(source, own, other):
    steps, _, lanes = source.shape
    for piece, spot in ((own, 0), (other, SEGMENTS)):
        rows = jnp.swapaxes(source[:, spot : spot + SEGMENTS, :], 0, 1)
        piece[...] = rows.reshape(SEGMENTS * steps, lanes).astype(piece.dtype)


def from_segment(value, place, later):
    segment = lax.broadcasted_iota(jnp.int32, value.shape, 1)
    if later:
        return jnp.where(segment == 2 * SEGMENTS - 1 - SEGMENTS * place, 0.0, pltpu.roll(value, 2 * SEGMENTS - 1, 1))
    return jnp.where(segment == SEGMENTS * place, 0.0, pltpu.roll(value, 1, 1))


def entering(added, factor, place, later):
    def turned(value):
        return jnp.where(place == 1, pltpu.roll(value, SEGMENTS, 0), value)

    added, factor = turned(added), turned(factor)
    state = jnp.zeros_like(added[0:1])
    rows = [None] * (2 * SEGMENTS)
    for index in reversed(range(2 * SEGMENTS)) if later else range(2 * SEGMENTS):
        rows[index] = state
        state = added[index : index + 1] + factor[index : index + 1] * state
    return turned(jnp.concatenate(rows, axis=0))


def wide_mask(mask_ref, index, first, count):
    mask = mask_ref[index, pl.ds(first, count)]
    return jnp.concatenate([mask, mask], axis=2)


def decay_terms(rate_gate, prm_ref):
    log_decay = prm_ref[7:8, :] * rate_gate
    decay = jnp.exp(log_decay)
    squared = decay * decay
    gap = jnp.maximum(-jnp.tanh(log_decay) * (1.0 + squared), 1e-37)
    return decay, squared, gap, lax.rsqrt(gap)


def rec_fwd_kernel(
    bx_own, bx_oth, by_own, by_oth, mask_ref, prm_ref, gate_ref,
    gated_own, gated_oth, state_ref, in_ref, rate_ref, conv_ref, xs, ys, pre, factor,
):
    place = lax.axis_index("tp")
    steps, both, lanes = state_ref.shape
    in_steps(bx_own, bx_oth, xs, 3)
    xs[0:3] = from_segment(xs[steps : steps + 3], place, False)
    in_steps(by_own, by_oth, ys, 0)
    taps = [prm_ref[k : k + 1, :] for k in range(4)]

    def conv_step(index, _):
        at = index * AT_ONCE
        total = taps[0] * xs[pl.ds(at + 3, AT_ONCE)] + prm_ref[4:5, :]
        for k in (1, 2, 3):
            total = total + taps[k] * (wide_mask(mask_ref, k - 1, at, AT_ONCE) * xs[pl.ds(at + 3 - k, AT_ONCE)])
        conv_ref[pl.ds(at, AT_ONCE)] = total.astype(BF16)
        return 0

    lax.fori_loop(0, steps // AT_ONCE, conv_step, 0)

    def gate_step(index, _):
        conv = conv_ref[pl.ds(index * 16, 16)].reshape(16 * both, lanes)
        rows = pl.ds(pl.multiple_of(index * 16 * both, 16 * both), 16 * both)
        pre[rows, 0:lanes] = jnp.dot(conv, gate_ref[0, 0], preferred_element_type=F32)
        pre[rows, lanes:] = jnp.dot(conv, gate_ref[1, 0], preferred_element_type=F32)
        return 0

    lax.fori_loop(0, steps // 16, gate_step, 0)

    def scan_step(index, carried):
        state, product = carried
        at = index * AT_ONCE
        block = pl.ds(at, AT_ONCE)
        rows = pl.ds(pl.multiple_of(at * both, AT_ONCE * both), AT_ONCE * both)
        shape = (AT_ONCE, both, lanes)
        in_gate = jax.nn.sigmoid(pre[rows, 0:lanes] + prm_ref[5:6, :]).reshape(shape)
        rate_gate = (1.0 / (1.0 + jnp.exp(-(pre[rows, lanes:] + prm_ref[6:7, :])))).reshape(shape)
        in_ref[block] = in_gate
        rate_ref[block] = rate_gate
        keep = wide_mask(mask_ref, 0, at, AT_ONCE)
        decay, _, gap, inverse = decay_terms(rate_gate, prm_ref)
        scaling = (1.0 - keep) + keep * (gap * inverse)
        pushed = conv_ref[block].astype(F32) * in_gate * scaling
        coef = decay * keep
        for one in range(AT_ONCE):
            state = coef[one] * state + pushed[one]
            product = coef[one] * product
            state_ref[at + one] = state
            factor[at + one] = product
        return state, product

    zero = jnp.zeros((both, lanes), F32)
    state, product = lax.fori_loop(0, steps // AT_ONCE, scan_step, (zero, zero + 1.0))
    enters = entering(state, product, place, False)

    def gated_step(index, _):
        block = pl.ds(index * AT_ONCE, AT_ONCE)
        state = state_ref[block] + factor[block] * enters
        state_ref[block] = state
        y = ys[block]
        tanh = jnp.tanh(GELU_A * y * (1.0 + GELU_B * (y * y)))
        ys[block] = state * (0.5 * y * (1.0 + tanh))
        return 0

    lax.fori_loop(0, steps // AT_ONCE, gated_step, 0)
    in_rows(ys, gated_own, gated_oth)


def fold(value):
    return jnp.sum(value, axis=0)


def rec_bwd_kernel(
    count, bits, bx_own, bx_oth, by_own, by_oth, state_ref, in_ref, rate_ref, conv_ref, up_own, up_oth, mask_ref, prm_ref, gate_ref,
    gx_own, gx_oth, gy_own, gy_oth, gw_ref, sum_ref, xs, ys, us, gs, factor, to_log, to_in, to_rate, to_conv, gc, dg, gw,
):
    place = lax.axis_index("tp")
    steps, both, lanes = state_ref.shape
    length = steps * both
    in_steps(bx_own, bx_oth, xs, 3)
    xs[0:3] = from_segment(xs[steps : steps + 3], place, False)
    in_steps(by_own, by_oth, ys, 0)
    in_steps(up_own, up_oth, us, 0)

    def scan_step(index, carried):
        sent, product = carried
        at = steps - AT_ONCE - index * AT_ONCE
        block = pl.ds(at, AT_ONCE)
        in_gate, rate_gate = in_ref[block], rate_ref[block]
        keep = wide_mask(mask_ref, 0, at, AT_ONCE)
        decay, squared, gap, inverse = decay_terms(rate_gate, prm_ref)
        scaling = (1.0 - keep) + keep * (gap * inverse)
        y = ys[block]
        y2 = y * y
        tanh = jnp.tanh(GELU_A * y * (1.0 + GELU_B * y2))
        lift = 0.5 + 0.5 * tanh
        slope = lift + y * (1.0 - tanh * tanh) * (0.5 * GELU_A + (1.5 * GELU_A * GELU_B) * y2)
        up = us[block]
        state = state_ref[block]
        ys[block] = up * state * slope
        direct = up * (y * lift)
        coef = decay * keep
        entered = conv_ref[block].astype(F32) * in_gate
        pushed = entered * scaling
        to_log[block] = ((state - pushed) - entered * (keep * squared * inverse)) * rate_gate
        to_in[block] = pushed * (1.0 - in_gate)
        to_rate[block] = (1.0 - rate_gate) * prm_ref[7:8, :]
        to_conv[block] = in_gate * scaling
        for one in reversed(range(AT_ONCE)):
            grad = direct[one] + sent
            gs[at + one] = grad
            factor[at + one] = product
            sent = coef[one] * grad
            product = coef[one] * product
        return sent, product

    zero = jnp.zeros((both, lanes), F32)
    sent, product = lax.fori_loop(0, steps // AT_ONCE, scan_step, (zero, zero + 1.0))
    enters = entering(sent, product, place, True)

    def grad_step(index, sum_log):
        at = index * AT_ONCE
        block = pl.ds(at, AT_ONCE)
        rows = pl.ds(pl.multiple_of(at * both, AT_ONCE * both), AT_ONCE * both)
        grad = gs[block] + factor[block] * enters
        through = grad * to_log[block]
        dg[rows, 0:lanes] = (grad * to_in[block]).astype(BF16).reshape(AT_ONCE * both, lanes)
        dg[rows, lanes:] = (through * to_rate[block]).astype(BF16).reshape(AT_ONCE * both, lanes)
        gc[block] = grad * to_conv[block]
        return sum_log + fold(through)

    sum_log = lax.fori_loop(0, steps // AT_ONCE, grad_step, zero)

    def back_step(index, _):
        rows = pl.ds(pl.multiple_of(index * 16 * both, 16 * both), 16 * both)
        more = matmul_right(dg[rows, 0:lanes], gate_ref[0, 0]) + matmul_right(dg[rows, lanes:], gate_ref[1, 0])
        gc[pl.ds(index * 16, 16)] += more.reshape(16, both, lanes)
        return 0

    lax.fori_loop(0, steps // 16, back_step, 0)
    conv = conv_ref[...].reshape(length, lanes)
    gw[0:lanes, :] = matmul_left(conv, dg[:, 0:lanes]).astype(BF16)
    gw[lanes:, :] = matmul_left(conv, dg[:, lanes:]).astype(BF16)
    gate_sums = jnp.dot(jnp.ones((8, length), BF16), dg[...], preferred_element_type=F32)
    rows_each = lanes // count
    me = lax.axis_index("dp")
    for spot in range(count):
        block = block_from(me, spot, bits)
        for gate in (0, 1):
            source = pl.ds(pl.multiple_of(gate * lanes + block * rows_each, rows_each), rows_each)
            gw_ref[spot, gate * rows_each : (gate + 1) * rows_each, :] = gw[source, :]
    gc[steps : steps + 3] = from_segment(gc[0:3], place, True)
    taps = [prm_ref[k : k + 1, :] for k in range(4)]

    def conv_step(index, sums):
        at = index * AT_ONCE
        here = gc[pl.ds(at, AT_ONCE)]
        total = taps[0] * here
        sums = [sums[0] + fold(here), sums[1] + fold(here * xs[pl.ds(at + 3, AT_ONCE)])] + list(sums[2:])
        for k in (1, 2, 3):
            total = total + taps[k] * (gc[pl.ds(at + k, AT_ONCE)] * wide_mask(mask_ref, k - 1, at + k, AT_ONCE))
            masked = here * wide_mask(mask_ref, k - 1, at, AT_ONCE)
            sums[k + 1] = sums[k + 1] + fold(masked * xs[pl.ds(at + 3 - k, AT_ONCE)])
        us[pl.ds(at, AT_ONCE)] = total
        return tuple(sums)

    sums = lax.fori_loop(0, steps // AT_ONCE, conv_step, (zero,) * 5)
    for index, value in ((0, sums[1]), (1, sums[2]), (2, sums[3]), (3, sums[4]), (4, sums[0]), (7, sum_log)):
        sum_ref[index : index + 1, :] = jnp.sum(value, axis=0, keepdims=True)
    sum_ref[5:6, :] = gate_sums[0:1, 0:lanes]
    sum_ref[6:7, :] = gate_sums[0:1, lanes:]
    in_rows(us, gx_own, gx_oth)
    in_rows(ys, gy_own, gy_oth)


def rec_specs(half, lanes):
    steps = half // SEGMENTS
    piece = pl.BlockSpec((half, lanes), lambda h: (0, h))
    stepped = pl.BlockSpec((steps, 2 * SEGMENTS, lanes), lambda h: (0, 0, h))
    mask = pl.BlockSpec((3, steps + 3, 2 * SEGMENTS, 128), lambda h: (0, 0, 0, 0))
    prm = pl.BlockSpec((8, lanes), lambda h: (0, h))
    gate = pl.BlockSpec((2, 1, lanes, lanes), lambda h: (0, h, 0, 0))
    return piece, stepped, mask, prm, gate


def rec_fwd(bx_own, bx_oth, by_own, by_oth, mask, prm, gates):
    half, width = bx_own.shape
    length, lanes, heads = 2 * half, gates.shape[2], gates.shape[1]
    steps, both = half // SEGMENTS, 2 * SEGMENTS
    piece, stepped, mask_spec, prm_spec, gate_spec = rec_specs(half, lanes)
    out = jax.ShapeDtypeStruct((half, width), BF16)
    kept = jax.ShapeDtypeStruct((steps, both, width), F32)
    return pl.pallas_call(
        rec_fwd_kernel,
        grid=(heads,),
        in_specs=[piece] * 4 + [mask_spec, prm_spec, gate_spec],
        out_specs=[piece] * 2 + [stepped] * 4,
        out_shape=[out, out, kept, kept, kept, jax.ShapeDtypeStruct((steps, both, width), BF16)],
        scratch_shapes=[
            pltpu.VMEM((steps + 3, both, lanes), F32),
            pltpu.VMEM((steps, both, lanes), F32),
            pltpu.VMEM((length, 2 * lanes), F32),
            pltpu.VMEM((steps, both, lanes), F32),
        ],
        compiler_params=pltpu.CompilerParams(vmem_limit_bytes=40 << 20),
        cost_estimate=pl.CostEstimate(
            flops=4 * length * width * lanes + 100 * length * width,
            bytes_accessed=26 * length * width,
            transcendentals=6 * length * width,
        ),
        name="rec_fwd",
    )(bx_own, bx_oth, by_own, by_oth, mask, prm, gates)


def rec_bwd(bx_own, bx_oth, by_own, by_oth, kept, up_own, up_oth, mask, prm, gates, count, cost):
    half, width = bx_own.shape
    length, lanes, heads = 2 * half, gates.shape[2], gates.shape[1]
    steps, both = half // SEGMENTS, 2 * SEGMENTS
    piece, stepped, mask_spec, prm_spec, gate_spec = rec_specs(half, lanes)
    block = pltpu.VMEM((steps, both, lanes), F32)
    padded = pltpu.VMEM((steps + 3, both, lanes), F32)
    return pl.pallas_call(
        functools.partial(rec_bwd_kernel, count, stage_bits(count, "X" in CROSSED)),
        grid=(heads,),
        in_specs=[piece] * 4 + [stepped] * 4 + [piece] * 2 + [mask_spec, prm_spec, gate_spec],
        out_specs=[piece] * 4 + [pl.BlockSpec((count, 2 * lanes // count, lanes), lambda h: (0, 0, h)), prm_spec],
        out_shape=[jax.ShapeDtypeStruct((half, width), BF16)] * 4
        + [
            jax.ShapeDtypeStruct((count, 2 * lanes // count, width), BF16),
            jax.ShapeDtypeStruct((8, width), F32),
        ],
        scratch_shapes=[padded]
        + [block] * 8
        + [padded, pltpu.VMEM((length, 2 * lanes), BF16), pltpu.VMEM((2 * lanes, lanes), BF16)],
        compiler_params=pltpu.CompilerParams(vmem_limit_bytes=52 << 20),
        cost_estimate=pl.CostEstimate(
            flops=int(cost * (8 * length * width * lanes + 150 * length * width)),
            bytes_accessed=int(cost * 34 * length * width),
            transcendentals=int(cost * 4 * length * width),
        ),
        name="rec_bwd",
    )(bx_own, bx_oth, by_own, by_oth, *kept, up_own, up_oth, mask, prm, gates)


def stage_bits(count, crossed=False):
    bits = [1 << bit for bit in range(count.bit_length() - 1)]
    return [bits[0], bits[2], bits[1]] + bits[3:] if crossed else bits


def block_at(place, bits):
    return sum(bit for step, bit in enumerate(bits) if (place >> (len(bits) - 1 - step)) & 1)


def block_from(me, place, bits):
    relative = block_at(place, bits)
    block = 0
    for bit in bits:
        mine = lax.rem(me // bit, 2)
        block = block + bit * (1 - mine if relative & bit else mine)
    return block


def arrange_kernel(bits, first, second, first_out, second_out):
    @pl.when(pl.program_id(0) == 0)
    def _():
        arranged(first, first_out, bits)

    @pl.when(pl.program_id(0) == 1)
    def _():
        arranged(second, second_out, bits)


def arrange(first, second, bits):
    whole = pl.BlockSpec(first.shape, lambda i: (0, 0))
    shape = jax.ShapeDtypeStruct(first.shape, first.dtype)
    return pl.pallas_call(
        functools.partial(arrange_kernel, bits),
        grid=(2,),
        in_specs=[whole, whole],
        out_specs=[whole, whole],
        out_shape=[shape, shape],
        compiler_params=pltpu.CompilerParams(vmem_limit_bytes=24 << 20),
        cost_estimate=pl.CostEstimate(flops=0, bytes_accessed=12 * first.size, transcendentals=0),
        name="arrange",
    )(first, second)


def weight_grad_kernel(more, own_a, own_b, oth_a, oth_b, right_own, right_oth, *rest):
    extra, (sent_next, kept, staged, landed, send_sem, recv_sem) = rest[:-6], rest[-6:]
    step = pl.program_id(0)
    me = lax.axis_index("dp")
    partner = {"dp": me + 1 - 2 * lax.rem(me, 2)}

    @pl.when(step == 0)
    def _():
        barrier = pltpu.get_barrier_semaphore()
        pl.semaphore_signal(barrier, inc=1, device_id=partner, device_id_type=MESH)
        pl.semaphore_wait(barrier, 1)

    def copy(tile):
        return pltpu.make_async_remote_copy(
            src_ref=staged.at[tile],
            dst_ref=landed.at[tile],
            send_sem=send_sem.at[tile],
            recv_sem=recv_sem.at[tile],
            device_id=partner,
            device_id_type=MESH,
        )

    left_own = jnp.concatenate([own_a[...], own_b[...]], axis=1)
    left_oth = jnp.concatenate([oth_a[...], oth_b[...]], axis=1)
    total = matmul_left(left_own, right_own[...]) + matmul_left(left_oth, right_oth[...])

    def pieces():
        if not more:
            return [(slice(0, total.shape[0]), total)]
        out = []
        for block in range(total.shape[0] // 128):
            first = block * (128 + more)
            out.append((slice(first, first + 128), total[block * 128 : (block + 1) * 128]))
            out.append((slice(first + 128, first + 128 + more), extra[0][block].astype(F32)))
        return out

    @pl.when(step < 2)
    def _():
        for rows, value in pieces():
            staged[step, rows, :] = value.astype(BF16)
        copy(step).start()

    def finish(tile, into):
        copy(tile).wait_recv()
        for rows, value in pieces():
            into[rows, :] = (value + landed[tile, rows, :].astype(F32)).astype(BF16)

    @pl.when(step == 2)
    def _():
        finish(0, sent_next)

    @pl.when(step == 3)
    def _():
        finish(1, kept)
        for tile in range(2):
            copy(tile).wait_send()


def weight_grad(left_own, left_oth, right_own, right_oth, crossed, cost, extra=None):
    half, cols = right_own.shape
    rows = left_own.shape[1] // 4
    more = 0 if extra is None else extra.shape[1]
    height = rows + rows // 128 * more
    out = pltpu.HBM((height, cols), BF16)

    def columns(part):
        def index(i):
            quarter = 3 - i
            return 0, (quarter // 2 * 4 + part * 2 + lax.rem(quarter, 2) if crossed else quarter * 2 + part)

        return pl.BlockSpec((half, rows // 2), index)

    right = pl.BlockSpec((half, cols), lambda i: (0, 0))
    whole = pl.BlockSpec((height, cols), lambda i: (0, 0))
    specs = [columns(0), columns(1), columns(0), columns(1), right, right]
    args = [left_own, left_own, left_oth, left_oth, right_own, right_oth]
    if more:
        specs.append(pl.BlockSpec((rows // 128, more, cols), lambda i: (3 - i, 0, 0)))
        args.append(extra)
    return pl.pallas_call(
        functools.partial(weight_grad_kernel, more),
        grid=(4,),
        in_specs=specs,
        out_specs=[whole, whole],
        out_shape=[out, out],
        scratch_shapes=[
            pltpu.VMEM((2, height, cols), BF16),
            pltpu.VMEM((2, height, cols), BF16),
            pltpu.SemaphoreType.DMA((2,)),
            pltpu.SemaphoreType.DMA((2,)),
        ],
        compiler_params=pltpu.CompilerParams(
            collective_id=4 * bool(more) + 2 * (cols > 2048) + crossed, has_side_effects=True, vmem_limit_bytes=60 << 20
        ),
        cost_estimate=pl.CostEstimate(
            flops=int(cost * 16 * half * rows * cols), bytes_accessed=int(cost * 16 * half * cols), transcendentals=0
        ),
        name="weight_grad",
    )(*args)


ROWS = 64


def arranged(source, into, bits):
    me = lax.axis_index("dp")
    count = 1 << len(bits)
    cols = source.shape[1] // count
    for place in range(count):
        block = pl.ds(pl.multiple_of(block_from(me, place, bits) * cols, cols), cols)
        into[:, place * cols : (place + 1) * cols] = source[:, block]


def feed_kernel(bits, sub, tokens, part, other, gain, grad_hidden, w_gate, w_up, middle, cols, hidden, grad_gate, grad_up, normed):
    @pl.when(pl.program_id(0) == 0)
    def _():
        def rows_step(index, _):
            rows = pl.ds(pl.multiple_of(index * ROWS, ROWS), ROWS)
            total = tokens[rows, :].astype(F32) + (part[rows, :].astype(F32) + other[rows, :].astype(F32))
            middle[rows, :] = total
            scale = lax.rsqrt(jnp.mean(total * total, axis=-1, keepdims=True) + EPS)
            normed[rows, :] = (total * scale * gain[...]).astype(BF16)
            return 0

        lax.fori_loop(0, tokens.shape[0] // ROWS, rows_step, 0)
        arranged(normed, cols, bits)

    for start in range(0, w_gate.shape[1], sub):
        part_cols = slice(start, start + sub)
        gate = jnp.dot(normed[...], w_gate[:, part_cols], preferred_element_type=F32)
        up = jnp.dot(normed[...], w_up[:, part_cols], preferred_element_type=F32)
        squared = gate * gate
        tanh = jnp.tanh(GELU_A * gate * (1.0 + GELU_B * squared))
        lift = 0.5 + 0.5 * tanh
        slope = lift + gate * (1.0 - tanh * tanh) * (0.5 * GELU_A + (1.5 * GELU_A * GELU_B) * squared)
        gelu = gate * lift
        back = grad_hidden[:, part_cols].astype(F32)
        hidden[:, part_cols] = (gelu * up).astype(BF16)
        grad_gate[:, part_cols] = (back * up * slope).astype(BF16)
        grad_up[:, part_cols] = (back * gelu).astype(BF16)


def feed(tokens, part, other, gain, grad_hidden, w_gate, w_up, bits, wide=768, sub=768):
    rows, model = tokens.shape
    cols = w_gate.shape[1]
    whole = pl.BlockSpec((rows, model), lambda n: (0, 0))
    piece = pl.BlockSpec((rows, wide), lambda n: (0, n))
    weight = pl.BlockSpec((model, wide), lambda n: (0, n))
    out = jax.ShapeDtypeStruct((rows, cols), BF16)
    return pl.pallas_call(
        functools.partial(feed_kernel, bits, sub),
        grid=(cols // wide,),
        in_specs=[whole] * 3 + [pl.BlockSpec((1, model), lambda n: (0, 0)), piece, weight, weight],
        out_specs=[whole, whole, piece, piece, piece],
        out_shape=[jax.ShapeDtypeStruct((rows, model), F32), jax.ShapeDtypeStruct((rows, model), BF16), out, out, out],
        scratch_shapes=[pltpu.VMEM((rows, model), BF16)],
        compiler_params=pltpu.CompilerParams(vmem_limit_bytes=56 << 20),
        cost_estimate=pl.CostEstimate(
            flops=4 * rows * model * cols, bytes_accessed=4 * model * cols + 12 * rows * cols, transcendentals=rows * cols
        ),
        name="feed",
    )(tokens, part, other, gain, grad_hidden, w_gate, w_up)


def pull_kernel(bits, middle, back, other, cot, gain, weight, grad, cols, into, rec):
    @pl.when(pl.program_id(0) == 0)
    def _():
        def rows_step(index, _):
            rows = pl.ds(pl.multiple_of(index * ROWS, ROWS), ROWS)
            values = middle[rows, :]
            scale = lax.rsqrt(jnp.mean(values * values, axis=-1, keepdims=True) + EPS)
            lifted = gain[...] * (back[rows, :].astype(F32) + other[rows, :].astype(F32))
            pulled = jnp.mean(values * lifted, axis=-1, keepdims=True)
            total = cot[rows, :].astype(F32) + (scale * lifted - values * (scale * scale * scale * pulled))
            grad[rows, :] = total
            rec[rows, :] = total.astype(BF16)
            return 0

        lax.fori_loop(0, middle.shape[0] // ROWS, rows_step, 0)
        arranged(rec, cols, bits)

    into[...] = matmul_right(rec[...], weight[...])


def pull(middle, back, other, cot, gain, weight, bits, cost, wide=640):
    rows, model = middle.shape
    cols = weight.shape[0]
    wide = wide if cols % wide == 0 else cols
    whole = pl.BlockSpec((rows, model), lambda n: (0, 0))
    return pl.pallas_call(
        functools.partial(pull_kernel, bits),
        grid=(cols // wide,),
        in_specs=[whole] * 4 + [pl.BlockSpec((1, model), lambda n: (0, 0)), pl.BlockSpec((wide, model), lambda n: (n, 0))],
        out_specs=[whole, whole, pl.BlockSpec((rows, wide), lambda n: (0, n))],
        out_shape=[
            jax.ShapeDtypeStruct((rows, model), F32),
            jax.ShapeDtypeStruct((rows, model), BF16),
            jax.ShapeDtypeStruct((rows, cols), F32),
        ],
        scratch_shapes=[pltpu.VMEM((rows, model), BF16)],
        compiler_params=pltpu.CompilerParams(vmem_limit_bytes=56 << 20),
        cost_estimate=pl.CostEstimate(
            flops=int(cost * 2 * rows * model * cols),
            bytes_accessed=int(cost * (16 * rows * model + 4 * rows * cols)),
            transcendentals=0,
        ),
        name="pull",
    )(middle, back, other, cot, gain, weight)


def two_back_kernel(first, first_w, second, second_w, out):
    out[...] = (matmul_right(first[...], first_w[...]) + matmul_right(second[...], second_w[...])).astype(BF16)


def two_back(first, first_w, second, second_w, cost=1.0):
    rows, depth = first.shape
    cols = first_w.shape[0]
    step = 512
    left = pl.BlockSpec((rows, depth), lambda n: (0, 0))
    right = pl.BlockSpec((step, depth), lambda n: (n, 0))
    return pl.pallas_call(
        two_back_kernel,
        grid=(cols // step,),
        in_specs=[left, right, left, right],
        out_specs=pl.BlockSpec((rows, step), lambda n: (0, n)),
        out_shape=jax.ShapeDtypeStruct((rows, cols), BF16),
        compiler_params=pltpu.CompilerParams(vmem_limit_bytes=48 << 20),
        cost_estimate=pl.CostEstimate(
            flops=int(cost * 4 * rows * depth * cols), bytes_accessed=int(cost * 4 * depth * (rows + cols)), transcendentals=0
        ),
        name="two_back",
    )(first, first_w, second, second_w)


def swap(value):
    return lax.ppermute(value, "tp", [(0, 1), (1, 0)])


def flip(value, bit):
    count = lax.axis_size("dp")
    return lax.ppermute(value, "dp", [(source, source ^ bit) for source in range(count)])


def halve_kernel(keep_low, keep_high, received_low, received_high, kept, sent):
    kept[...] = (keep_low[...].astype(F32) + received_low[...].astype(F32)).astype(BF16)
    sent[...] = (keep_high[...].astype(F32) + received_high[...].astype(F32)).astype(BF16)


def halve(keep, received, cost):
    rows, cols = keep.shape
    block = rows // 4 if rows > 512 else rows // 2
    steps = rows // 2 // block
    low = pl.BlockSpec((block, cols), lambda i: (i, 0))
    high = pl.BlockSpec((block, cols), lambda i: (i + steps, 0))
    return pl.pallas_call(
        halve_kernel,
        grid=(steps,),
        in_specs=[low, high, low, high],
        out_specs=[low, low],
        out_shape=[pltpu.HBM((rows // 2, cols), BF16)] * 2,
        compiler_params=pltpu.CompilerParams(vmem_limit_bytes=32 << 20),
        cost_estimate=pl.CostEstimate(flops=0, bytes_accessed=int(cost * 6 * rows * cols), transcendentals=0),
        name="halve",
    )(keep, keep, received, received)


class Reduction:
    def __init__(self, left, right, count, crossed, cost, extra=None):
        self.bits = stage_bits(count, crossed)[1:]
        sent, self.keep = weight_grad(*left, *right, crossed, cost, extra)
        self.pass_on(sent)

    def pass_on(self, sent):
        self.received = flip(sent, self.bits.pop(0))

    def step(self, cost, *others):
        self.keep, sent = halve(self.keep, after(self.received, *others), cost)
        self.pass_on(sent)
        return sent

    def total(self, *others):
        while self.bits:
            self.step(1.0, *others)
        return self.keep.astype(F32) + after(self.received, *others).astype(F32)


def after(value, *others):
    return lax.optimization_barrier((value, *others))[0]


def norm_back(values, gain, grad):
    scale = lax.rsqrt(jnp.mean(values * values, axis=-1, keepdims=True) + EPS)
    lifted = gain * grad
    pull = jnp.mean(values * lifted, axis=-1, keepdims=True)
    return scale * lifted - values * (scale * scale * scale * pull)


def local_channels(
    layer_in, cotangent, resets, norm_gains, w_x, w_y, conv_w, lru_bias, a_param, gate_blocks, w_out, w_gate, w_up, w_down,
):
    place = lax.axis_index("tp")
    me = lax.axis_index("dp")
    count = lax.axis_size("dp")
    bits = stage_bits(count)
    width = w_x.shape[1]
    full_width = conv_w.shape[1]
    heads = gate_blocks.shape[1] // 2
    model = norm_gains.shape[1]

    own_in, own_cot = layer_in[0], cotangent[0]
    oth_in = swap(own_in)
    oth_resets = swap(resets[0])
    oth_cot = swap(own_cot)
    normed_own = rms_scale(own_in.astype(F32), norm_gains[0]).astype(BF16)
    bx_own = matmul(normed_own, w_x).astype(BF16)
    by_own = matmul(normed_own, w_y)

    first_place = place == 0
    in_time = jnp.where(first_place, resets[0], oth_resets), jnp.where(first_place, oth_resets, resets[0])
    keep = 1.0 - jnp.concatenate(in_time).astype(F32)
    keep_1 = jnp.concatenate([jnp.ones((1,), F32), keep[:-1]])
    keep_2 = jnp.concatenate([jnp.ones((1,), F32), keep_1[:-1]])
    valid = jnp.stack([keep, keep * keep_1, keep * keep_1 * keep_2]).reshape(3, 2, SEGMENTS, -1)
    valid = jnp.where(first_place, valid, valid[:, ::-1]).reshape(3, 2 * SEGMENTS, -1)
    later = jnp.concatenate([valid[:, 1:, :3], valid[:, :1, :3]], axis=1)
    mask = jnp.swapaxes(jnp.concatenate([valid, later], axis=2), 1, 2)
    mask = jnp.broadcast_to(mask[..., None], mask.shape + (128,))
    table = jnp.concatenate([conv_w, lru_bias, -8.0 * jax.nn.softplus(a_param)[None]], axis=0)
    prm = lax.dynamic_slice(table, (0, place * width), (8, width))
    gates = lax.dynamic_slice_in_dim(gate_blocks, place * heads, heads, axis=1)

    gh_own = matmul_right(after(own_cot, bx_own, by_own), w_down)
    normed_oth = rms_scale(after(oth_in, gh_own).astype(F32), norm_gains[0]).astype(BF16)
    bx_oth = matmul(normed_oth, w_x).astype(BF16)
    by_oth = matmul(normed_oth, w_y)
    gated_own, gated_oth, *kept = rec_fwd(bx_own, bx_oth, by_own, by_oth, mask, prm, gates)

    part_oth = matmul(gated_oth, w_out).astype(BF16)
    swap_own = swap(part_oth)
    part_own = matmul(after(gated_own, part_oth), w_out).astype(BF16)
    swap_oth = swap(part_own)
    gh_oth = matmul_right(after(oth_cot, part_own), w_down)
    cot_cols = arrange(after(own_cot, gh_oth), oth_cot, bits)
    normed_cols = arrange(after(normed_own, cot_cols[0]), normed_oth, bits)
    gains = norm_gains[1:2]

    middle_own, two_own, hidden_own, gg_own, gu_own = feed(
        own_in, part_own, after(swap_own, normed_cols[0]), gains, gh_own, w_gate, w_up, bits
    )
    back_own = two_back(gg_own, w_gate, gu_own, w_up)
    back_own_swapped = swap(back_own)
    middle_oth, two_oth, hidden_oth, gg_oth, gu_oth = feed(
        oth_in, part_oth, after(swap_oth, back_own), gains, gh_oth, w_gate, w_up, bits
    )
    sums_over = {}
    at = {"done": hidden_oth}

    def reduce_kernel(name, letter, left, right, extra=None):
        left = (after(left[0], at["done"]), left[1])
        sums_over[letter] = Reduction(left, right, count, letter in CROSSED, COSTS.get(name, 1.0), extra)
        return sums_over[letter].keep

    def back_other(cost):
        at["back"] = two_back(after(gg_oth, at["done"]), w_gate, gu_oth, w_up, cost)
        at["back_swapped"] = swap(at["back"])
        return at["back"]

    def pull_other(cost):
        other = after(back_own_swapped, at["done"])
        _, at["rec_oth"], at["into_oth"] = pull(middle_oth, at["back"], other, oth_cot, gains, w_out, bits, cost)
        return at["into_oth"]

    def pull_own(cost):
        other = after(at["back_swapped"], at["done"])
        at["grad_own"], at["rec_own"], at["into_own"] = pull(middle_own, back_own, other, own_cot, gains, w_out, bits, cost)
        return at["into_own"]

    def recurrence(cost):
        into = after(at["into_own"], at["done"]), at["into_oth"]
        *grads, gate_sums, sums = rec_bwd(bx_own, bx_oth, by_own, by_oth, kept, *into, mask, prm, gates, count, cost)
        at["gx"], at["gy"] = grads[0:2], grads[2:4]
        row = jnp.arange(8)[:, None] == 7
        slopes = -8.0 * lax.dynamic_slice(jax.nn.sigmoid(a_param), (place * width,), (width,))
        sums = jnp.swapaxes(jnp.where(row, sums * slopes, sums).reshape(8, count // 2, each), 0, 1)
        order = [block_at(spot, stage_bits(count, "X" in CROSSED)) for spot in range(count)]
        chosen = jnp.bitwise_xor(jnp.array(order), me)[:, None] % (count // 2) == jnp.arange(count // 2)[None, :]
        sums = matmul(chosen.astype(BF16), sums.astype(BF16).reshape(count // 2, -1)).reshape(count, 8, each)
        sums = jnp.pad(sums.astype(BF16), ((0, 0), (0, 8), (0, width - each)))
        at["extra"] = jnp.concatenate([gate_sums, sums], axis=1)
        return grads[0]

    def rec_rows(index):
        def run(cost):
            name = ("rec_keep", "rec_send")[index]
            at[name] = two_back(after(at["gx"][index], at["done"]), w_x, at["gy"][index], w_y, cost)
            if index == 1:
                at["rec_swapped"] = swap(at[name])
            return at[name]

        return run

    def out_other(cost):
        sent = matmul(after(hidden_oth, at["done"]), w_down).astype(BF16)
        at["out_swapped"] = swap(sent)
        return sent

    def out_own(cost):
        at["out_keep"] = matmul(after(hidden_own, at["done"]), w_down).astype(BF16)
        return at["out_keep"]

    def to_inputs(cost):
        grad_normed = at["rec_keep"].astype(F32) + after(at["rec_swapped"], at["done"]).astype(F32)
        at["input_grad"] = at["grad_own"] + norm_back(own_in.astype(F32), norm_gains[0], grad_normed)
        return at["input_grad"]

    def to_outputs(cost):
        total = middle_own + at["out_keep"].astype(F32) + after(at["out_swapped"], at["done"]).astype(F32)
        at["layer_out"] = total.astype(BF16)
        return at["layer_out"]

    def swap_blocks(cost):
        at["mine"] = after(grads["X"][block:], at["done"]).astype(BF16)
        at["others"] = swap(at["mine"])
        return at["others"]

    each = full_width // count
    block = model // count
    steps = {
        "DK": lambda cost: reduce_kernel("DK", "D", cot_cols, (hidden_own, hidden_oth)),
        "GK": lambda cost: reduce_kernel("GK", "G", (two_own, two_oth), (gg_own, gg_oth)),
        "UK": lambda cost: reduce_kernel("UK", "U", (two_own, two_oth), (gu_own, gu_oth)),
        "OUT": lambda cost: reduce_kernel("OUT", "O", (at["rec_own"], at["rec_oth"]), (gated_own, gated_oth)),
        "X": lambda cost: reduce_kernel("X", "X", normed_cols, at["gx"], at["extra"]),
        "Y": lambda cost: reduce_kernel("Y", "Y", normed_cols, at["gy"]),
        "B2": back_other,
        "P2": pull_other,
        "P1": pull_own,
        "RB": recurrence,
        "RS": rec_rows(1),
        "RK": rec_rows(0),
        "OS": out_other,
        "OK": out_own,
        "IG": to_inputs,
        "LO": to_outputs,
        "SW": swap_blocks,
    }
    grads = {}
    for name in ORDER:
        if name in steps:
            at["done"] = steps[name](COSTS.get(name, 1.0))
        elif name[1] == "t":
            total = sums_over[name[0]].total(at["done"])
            at["done"] = grads[name[0]] = total.T if name[0] in "DO" else total
        else:
            at["done"] = sums_over[name[0]].step(COSTS.get(name, 1.0), at["done"])
    mine, others, layer_out, input_grad = (at[name] for name in ("mine", "others", "layer_out", "input_grad"))
    down_grad, gate_grad, up_grad, out_grad, x_grad, y_grad = (grads[letter] for letter in "DGUOXY")
    x_grad = x_grad[:block]
    low, high = jnp.where(first_place, mine, others), jnp.where(first_place, others, mine)
    both = jnp.stack([low[:-16], high[:-16]]).astype(F32).reshape(2, 2, -1, heads, gates.shape[-1])
    block_sums = jnp.transpose(both, (1, 0, 3, 2, 4)).reshape(2, 2 * heads, -1, gates.shape[-1])
    small = jnp.where(me < count // 2, low[-16:-8], high[-16:-8])[:, :each].astype(F32)

    def gain_grad(gain, *pairs):
        weights = sum(
            jnp.sum(lax.dynamic_slice_in_dim(weight, me * block, block, axis=0).astype(F32) * grad, axis=1)
            for weight, grad in pairs
        )
        return weights / lax.dynamic_slice_in_dim(gain, me * block, block, axis=0)

    gains = jnp.stack(
        [
            gain_grad(norm_gains[0], (w_x, x_grad), (w_y, y_grad)),
            gain_grad(norm_gains[1], (w_gate, gate_grad), (w_up, up_grad)),
        ]
    )
    gains = gains + swap(gains)
    return (
        layer_out[None],
        input_grad[None],
        gains,
        x_grad,
        y_grad,
        small[0:4],
        small[4:7],
        small[7],
        block_sums,
        out_grad,
        gate_grad,
        up_grad,
        down_grad,
    )


def from_behind(value, axis, steps):
    count = lax.axis_size(axis)
    first, last = (max(0, -steps), min(count, count - steps))
    return lax.ppermute(value, axis, [(source, source + steps) for source in range(first, last)])


def rms_scale(values, gain_vec):
    return values * lax.rsqrt(jnp.mean(values * values, axis=-1, keepdims=True) + EPS) * gain_vec


def gelu_product(gate_val, up_val):
    return jax.nn.gelu(gate_val, approximate=True) * up_val


def lru_terms(conv_out, gate_in, gate_rate, a_param, starts):
    keep_mask = 1.0 - starts
    input_gate = jax.nn.sigmoid(gate_in)
    rate_gate = jax.nn.sigmoid(gate_rate)
    log_decay = -8.0 * rate_gate * jax.nn.softplus(a_param)
    scaling = starts + keep_mask * jnp.sqrt(-jnp.expm1(2.0 * log_decay))
    return (jnp.exp(log_decay) * keep_mask, conv_out * input_gate * scaling)


def matmul(first_mat, second_mat):
    return jnp.dot(first_mat, second_mat, preferred_element_type=jnp.float32)


def matmul_left(first_mat, second_mat):
    return lax.dot_general(
        first_mat, second_mat, (((0,), (0,)), ((), ())), preferred_element_type=jnp.float32
    )


def matmul_right(first_mat, second_mat):
    return lax.dot_general(
        first_mat, second_mat, (((1,), (1,)), ((), ())), preferred_element_type=jnp.float32
    )


def combine_state(first_item, second_item):
    return (first_item[0] * second_item[0], second_item[1] + second_item[0] * first_item[1])


def carry_across(coef_end, state_end, reverse):
    incoming = jnp.zeros_like(state_end)
    direction = -1 if reverse else 1
    for turn_index in range(lax.axis_size("tp") - 1):
        incoming = from_behind(state_end + coef_end * incoming, "tp", direction)
    return incoming


def local(
    layer_in,
    cotangent,
    resets,
    norm_gains,
    w_x,
    w_y,
    conv_w,
    lru_bias,
    a_param,
    gate_blocks,
    w_out,
    w_gate,
    w_up,
    w_down,
):
    inputs = layer_in[0].astype(jnp.float32)
    starts = resets[0].astype(jnp.float32)
    keep_mask = 1.0 - starts
    rim_size = conv_w.shape[0] - 1
    head_count = gate_blocks.shape[1]
    block_size = gate_blocks.shape[2]
    full_width = conv_w.shape[1]
    normed, norm_pull = jax.vjp(rms_scale, inputs, norm_gains[0])
    normed_low = normed.astype(jnp.bfloat16)
    proj_x, proj_y, proj_out = (
        lax.all_gather(w_x, "tp", axis=1, tiled=True),
        lax.all_gather(w_y, "tp", axis=1, tiled=True),
        lax.all_gather(w_out, "tp", axis=0, tiled=True),
    )
    rec_len = normed_low.shape[0]
    branch_x = matmul(normed_low, proj_x).astype(jnp.bfloat16)
    branch_y = matmul(normed_low, proj_y)
    rim_rows, rim_keep = from_behind(
        (branch_x[rec_len - rim_size :], keep_mask[rec_len - rim_size :].astype(jnp.bfloat16)),
        "tp",
        1,
    )
    padded_x = jnp.concatenate([rim_rows, branch_x], axis=0).astype(jnp.float32)
    padded_keep = jnp.concatenate([rim_keep.astype(jnp.float32), keep_mask])
    conv_sum = conv_w[0] * padded_x[rim_size:]
    valid_mask = keep_mask
    valid_list = []
    for offset in range(1, rim_size + 1):
        valid_list.append(valid_mask)
        conv_sum = (
            conv_sum
            + valid_mask[:, None]
            * conv_w[offset]
            * padded_x[rim_size - offset : rim_size - offset + rec_len]
        )
        valid_mask = valid_mask * padded_keep[rim_size - offset : rim_size - offset + rec_len]
    conv_out = (conv_sum + lru_bias[0]).astype(jnp.bfloat16)
    row_count = conv_out.shape[0]
    conv_blocks = conv_out.reshape(row_count, head_count, block_size)
    pre_rows = (
        jnp.einsum(
            "lhb,ghbc->glhc", conv_blocks, gate_blocks, preferred_element_type=jnp.float32
        ).reshape(2, row_count, full_width)
        + lru_bias[1:3][:, None, :]
    )
    gate_in = pre_rows[0]
    gate_rate = pre_rows[1]
    conv_float = conv_out.astype(jnp.float32)

    def lru_local(conv_in, in_pre, rate_pre, decay_in):
        return lru_terms(conv_in, in_pre, rate_pre, decay_in, starts[:, None])

    (decay_rate, pushed), lru_pull = jax.vjp(lru_local, conv_float, gate_in, gate_rate, a_param)
    decay_cum, local_states = lax.associative_scan(combine_state, (decay_rate, pushed), axis=0)
    incoming = carry_across(decay_cum[-1], local_states[-1], False)
    states = local_states + decay_cum * incoming
    gated_val, gated_pull = jax.vjp(gelu_product, branch_y, states)
    gated_low = gated_val.astype(jnp.bfloat16)
    recurrent = matmul(gated_low, proj_out)
    middle = inputs + recurrent
    normed_two, norm_two_pull = jax.vjp(rms_scale, middle, norm_gains[1])
    normed_two_low = normed_two.astype(jnp.bfloat16)
    group_rows = lax.all_gather(normed_two_low, "tp", axis=0, tiled=True)
    gate_val = matmul(group_rows, w_gate)
    up_val = matmul(group_rows, w_up)
    hidden_val, mlp_pull = jax.vjp(gelu_product, gate_val, up_val)
    hidden = hidden_val.astype(jnp.bfloat16)
    mlp_out = lax.psum_scatter(
        matmul(hidden, w_down).astype(jnp.bfloat16), "tp", scatter_dimension=0, tiled=True
    ).astype(jnp.float32)
    layer_out = (middle + mlp_out).astype(jnp.bfloat16)
    grad_out = cotangent[0].astype(jnp.float32)
    group_grad = lax.all_gather(cotangent[0], "tp", axis=0, tiled=True)
    w_down_grad = matmul_left(hidden, group_grad)
    grad_hidden = matmul_right(group_grad, w_down)
    grad_gate, grad_up = mlp_pull(grad_hidden)
    grad_gate = grad_gate.astype(jnp.bfloat16)
    grad_up = grad_up.astype(jnp.bfloat16)
    w_gate_grad = matmul_left(group_rows, grad_gate)
    w_up_grad = matmul_left(group_rows, grad_up)
    grad_normed_two = lax.psum_scatter(
        (matmul_right(grad_gate, w_gate) + matmul_right(grad_up, w_up)).astype(jnp.bfloat16),
        "tp",
        scatter_dimension=0,
        tiled=True,
    ).astype(jnp.float32)
    grad_middle, gain_two_grad = norm_two_pull(grad_normed_two)
    grad_middle = grad_middle + grad_out
    grad_rec = grad_middle.astype(jnp.bfloat16)
    grad_gated = matmul_right(grad_rec, proj_out)
    grad_branch_y, grad_direct = gated_pull(grad_gated)
    grad_branch_y = grad_branch_y.astype(jnp.bfloat16)
    decay_next = jnp.concatenate([decay_rate[1:], jnp.ones_like(decay_rate[:1])], axis=0)
    reach_back, local_grads = lax.associative_scan(
        combine_state, (decay_next, grad_direct), reverse=True, axis=0
    )
    outgoing = carry_across(decay_rate[0] * reach_back[0], decay_rate[0] * local_grads[0], True)
    state_grads = local_grads + reach_back * outgoing
    prior_states = jnp.concatenate([incoming[None], states[:-1]], axis=0)
    grad_conv, grad_in, grad_rate, a_local_grad = lru_pull(
        (state_grads * prior_states, state_grads)
    )
    grad_pre = jnp.stack([grad_in, grad_rate]).astype(jnp.bfloat16)
    pre_sums = jnp.sum(grad_pre.astype(jnp.float32), axis=1)
    pre_blocks = grad_pre.reshape(2, row_count, head_count, block_size)
    gate_blocks_grad = jnp.einsum(
        "lhb,glhc->ghbc", conv_blocks, pre_blocks, preferred_element_type=jnp.float32
    )
    gate_back = jnp.einsum(
        "glhc,ghbc->lhb", pre_blocks, gate_blocks, preferred_element_type=jnp.float32
    ).reshape(row_count, full_width)
    grad_conv = grad_conv + gate_back
    conv_w_rows = [jnp.sum(grad_conv * padded_x[rim_size:], axis=0)]
    grad_padded = (
        jnp.zeros((rec_len + rim_size, full_width), jnp.float32)
        .at[rim_size:]
        .add(conv_w[0] * grad_conv)
    )
    for offset in range(1, rim_size + 1):
        masked = valid_list[offset - 1][:, None] * grad_conv
        conv_w_rows.append(
            jnp.sum(masked * padded_x[rim_size - offset : rim_size - offset + rec_len], axis=0)
        )
        grad_padded = grad_padded.at[rim_size - offset : rim_size - offset + rec_len].add(
            conv_w[offset] * masked
        )
    returned = from_behind(grad_padded[:rim_size], "tp", -1)
    grad_x_branch = (
        grad_padded[rim_size:].at[rec_len - rim_size :].add(returned).astype(jnp.bfloat16)
    )
    conv_w_grad = jnp.stack(conv_w_rows)
    lru_bias_grad = jnp.concatenate([jnp.sum(grad_conv, axis=0)[None], pre_sums], axis=0)
    grad_normed = matmul_right(grad_x_branch, proj_x) + matmul_right(grad_branch_y, proj_y)
    grad_inputs, gain_one_grad = norm_pull(grad_normed)
    input_grad = grad_middle + grad_inputs
    w_x_grad, w_y_grad, w_out_grad = (
        lax.psum_scatter(
            matmul_left(normed_low, grad_x_branch).astype(jnp.bfloat16),
            "tp",
            scatter_dimension=1,
            tiled=True,
        ).astype(jnp.float32),
        lax.psum_scatter(
            matmul_left(normed_low, grad_branch_y).astype(jnp.bfloat16),
            "tp",
            scatter_dimension=1,
            tiled=True,
        ).astype(jnp.float32),
        lax.psum_scatter(
            matmul_left(gated_low, grad_rec).astype(jnp.bfloat16),
            "tp",
            scatter_dimension=0,
            tiled=True,
        ).astype(jnp.float32),
    )
    norm_gains_grad = jnp.stack([gain_one_grad, gain_two_grad])
    totals = (
        lax.psum_scatter(
            w_x_grad.astype(jnp.bfloat16), "dp", scatter_dimension=0, tiled=True
        ).astype(jnp.float32),
        lax.psum_scatter(
            w_y_grad.astype(jnp.bfloat16), "dp", scatter_dimension=0, tiled=True
        ).astype(jnp.float32),
        lax.psum_scatter(
            w_out_grad.astype(jnp.bfloat16), "dp", scatter_dimension=1, tiled=True
        ).astype(jnp.float32),
        lax.psum_scatter(
            w_gate_grad.astype(jnp.bfloat16), "dp", scatter_dimension=0, tiled=True
        ).astype(jnp.float32),
        lax.psum_scatter(
            w_up_grad.astype(jnp.bfloat16), "dp", scatter_dimension=0, tiled=True
        ).astype(jnp.float32),
        lax.psum_scatter(
            w_down_grad.astype(jnp.bfloat16), "dp", scatter_dimension=1, tiled=True
        ).astype(jnp.float32),
        lax.psum_scatter(
            norm_gains_grad.astype(jnp.bfloat16), "dp", scatter_dimension=1, tiled=True
        ).astype(jnp.float32),
        lax.psum_scatter(
            conv_w_grad.astype(jnp.bfloat16), "dp", scatter_dimension=1, tiled=True
        ).astype(jnp.float32),
        lax.psum_scatter(
            lru_bias_grad.astype(jnp.bfloat16), "dp", scatter_dimension=1, tiled=True
        ).astype(jnp.float32),
        lax.psum_scatter(
            a_local_grad.astype(jnp.bfloat16), "dp", scatter_dimension=0, tiled=True
        ).astype(jnp.float32),
        lax.psum_scatter(
            gate_blocks_grad.astype(jnp.bfloat16), "dp", scatter_dimension=2, tiled=True
        ).astype(jnp.float32),
    )
    reduced_small = (
        lax.psum(totals[6].astype(jnp.bfloat16), "tp").astype(jnp.float32),
        lax.psum(totals[7].astype(jnp.bfloat16), "tp").astype(jnp.float32),
        lax.psum(totals[8].astype(jnp.bfloat16), "tp").astype(jnp.float32),
        lax.psum(totals[9].astype(jnp.bfloat16), "tp").astype(jnp.float32),
        lax.psum(totals[10].astype(jnp.bfloat16), "tp").astype(jnp.float32),
    )
    return (
        layer_out[None],
        input_grad[None],
        reduced_small[0],
        totals[0],
        totals[1],
        reduced_small[1],
        reduced_small[2],
        reduced_small[3],
        reduced_small[4],
        totals[2],
        totals[3],
        totals[4],
        totals[5],
    )


def solution(mesh):
    rows, cols = mesh.shape["dp"], mesh.shape["tp"]
    by_channels = cols == 2 and rows >= 16 and rows & (rows - 1) == 0

    def step(*args):
        heads, model = args[9].shape[1], args[3].shape[1]
        fits = by_channels and heads % cols == 0 and model % (128 * rows) == 0
        return (local_channels if fits else local)(*args)

    return jax.shard_map(
        step,
        mesh=mesh,
        in_specs=(
            P("dp", "tp", None),
            P("dp", "tp", None),
            P("dp", "tp"),
            P(),
            P(None, "tp"),
            P(None, "tp"),
            P(),
            P(),
            P(),
            P(),
            P("tp", None),
            P(None, "tp"),
            P(None, "tp"),
            P("tp", None),
        ),
        out_specs=(
            P("dp", "tp", None),
            P("dp", "tp", None),
            P(None, "dp"),
            P("dp", "tp"),
            P("dp", "tp"),
            P(None, "dp"),
            P(None, "dp"),
            P("dp"),
            P(None, None, "dp", None),
            P("tp", "dp"),
            P("dp", "tp"),
            P("dp", "tp"),
            P("tp", "dp"),
        ),
        check_vma=False,
    )
```

```python
import functools

import jax
import jax.numpy as jnp
from jax import lax
from jax.experimental import pallas as pl
from jax.experimental.pallas import tpu as pltpu
from jax.sharding import PartitionSpec as P

EPS = 1e-06
F32, BF16 = jnp.float32, jnp.bfloat16
GELU_A, GELU_B = 0.7978845608028654, 0.044715
ORDER = (
    "DK", "GK", "UK", "B2", "P2", "D1", "G1", "P1", "OUT", "D2", "U1", "RB",
    "G2", "X", "Dt", "O1", "RS", "U2", "Gt", "Y", "O2", "X1", "OS", "RK",
    "IG", "Y1", "Ut", "Ot", "X2", "Y2", "OK", "LO", "Xt", "SW", "Yt", "GN",
)
CROSSED = "G"
COSTS = {"B2": 0.6, "GK": 0.6, "P2": 6, "UK": 0.6}
MESH = pl.DeviceIdType.MESH


AT_ONCE = 8
SEGMENTS = 8


def in_steps(own, other, into, first):
    steps = own.shape[0] // SEGMENTS
    for piece, spot in ((own, 0), (other, SEGMENTS)):
        rows = piece[...].astype(F32).reshape(SEGMENTS, steps, piece.shape[1])
        into[first : first + steps, spot : spot + SEGMENTS, :] = jnp.swapaxes(rows, 0, 1)


def in_rows(source, own, other):
    steps, _, lanes = source.shape
    for piece, spot in ((own, 0), (other, SEGMENTS)):
        rows = jnp.swapaxes(source[:, spot : spot + SEGMENTS, :], 0, 1)
        piece[...] = rows.reshape(SEGMENTS * steps, lanes).astype(piece.dtype)


def from_segment(value, place, later):
    segment = lax.broadcasted_iota(jnp.int32, value.shape, 1)
    if later:
        return jnp.where(segment == 2 * SEGMENTS - 1 - SEGMENTS * place, 0.0, pltpu.roll(value, 2 * SEGMENTS - 1, 1))
    return jnp.where(segment == SEGMENTS * place, 0.0, pltpu.roll(value, 1, 1))


def entering(added, factor, place, later):
    def turned(value):
        return jnp.where(place == 1, pltpu.roll(value, SEGMENTS, 0), value)

    added, factor = turned(added), turned(factor)
    state = jnp.zeros_like(added[0:1])
    rows = [None] * (2 * SEGMENTS)
    for index in reversed(range(2 * SEGMENTS)) if later else range(2 * SEGMENTS):
        rows[index] = state
        state = added[index : index + 1] + factor[index : index + 1] * state
    return turned(jnp.concatenate(rows, axis=0))


def wide_mask(mask_ref, index, first, count):
    mask = mask_ref[index, pl.ds(first, count)]
    return jnp.concatenate([mask, mask], axis=2)


def decay_terms(rate_gate, prm_ref):
    log_decay = prm_ref[7:8, :] * rate_gate
    decay = jnp.exp(log_decay)
    squared = decay * decay
    gap = jnp.maximum(-jnp.tanh(log_decay) * (1.0 + squared), 1e-37)
    return decay, squared, gap, lax.rsqrt(gap)


def rec_fwd_kernel(
    bx_own, bx_oth, by_own, by_oth, mask_ref, prm_ref, gate_ref,
    gated_own, gated_oth, state_ref, in_ref, rate_ref, conv_ref, xs, ys, pre, factor,
):
    place = lax.axis_index("tp")
    steps, both, lanes = state_ref.shape
    in_steps(bx_own, bx_oth, xs, 3)
    xs[0:3] = from_segment(xs[steps : steps + 3], place, False)
    in_steps(by_own, by_oth, ys, 0)
    taps = [prm_ref[k : k + 1, :] for k in range(4)]

    def conv_step(index, _):
        at = index * AT_ONCE
        total = taps[0] * xs[pl.ds(at + 3, AT_ONCE)] + prm_ref[4:5, :]
        for k in (1, 2, 3):
            total = total + taps[k] * (wide_mask(mask_ref, k - 1, at, AT_ONCE) * xs[pl.ds(at + 3 - k, AT_ONCE)])
        conv_ref[pl.ds(at, AT_ONCE)] = total.astype(BF16)
        return 0

    lax.fori_loop(0, steps // AT_ONCE, conv_step, 0)

    def gate_step(index, _):
        conv = conv_ref[pl.ds(index * 16, 16)].reshape(16 * both, lanes)
        rows = pl.ds(pl.multiple_of(index * 16 * both, 16 * both), 16 * both)
        pre[rows, 0:lanes] = jnp.dot(conv, gate_ref[0, 0], preferred_element_type=F32)
        pre[rows, lanes:] = jnp.dot(conv, gate_ref[1, 0], preferred_element_type=F32)
        return 0

    lax.fori_loop(0, steps // 16, gate_step, 0)

    def scan_step(index, carried):
        state, product = carried
        at = index * AT_ONCE
        block = pl.ds(at, AT_ONCE)
        rows = pl.ds(pl.multiple_of(at * both, AT_ONCE * both), AT_ONCE * both)
        shape = (AT_ONCE, both, lanes)
        in_gate = jax.nn.sigmoid(pre[rows, 0:lanes] + prm_ref[5:6, :]).reshape(shape)
        rate_gate = (1.0 / (1.0 + jnp.exp(-(pre[rows, lanes:] + prm_ref[6:7, :])))).reshape(shape)
        in_ref[block] = in_gate
        rate_ref[block] = rate_gate
        keep = wide_mask(mask_ref, 0, at, AT_ONCE)
        decay, _, gap, inverse = decay_terms(rate_gate, prm_ref)
        scaling = (1.0 - keep) + keep * (gap * inverse)
        pushed = conv_ref[block].astype(F32) * in_gate * scaling
        coef = decay * keep
        for one in range(AT_ONCE):
            state = coef[one] * state + pushed[one]
            product = coef[one] * product
            state_ref[at + one] = state
            factor[at + one] = product
        return state, product

    zero = jnp.zeros((both, lanes), F32)
    state, product = lax.fori_loop(0, steps // AT_ONCE, scan_step, (zero, zero + 1.0))
    enters = entering(state, product, place, False)

    def gated_step(index, _):
        block = pl.ds(index * AT_ONCE, AT_ONCE)
        state = state_ref[block] + factor[block] * enters
        state_ref[block] = state
        y = ys[block]
        tanh = jnp.tanh(GELU_A * y * (1.0 + GELU_B * (y * y)))
        ys[block] = state * (0.5 * y * (1.0 + tanh))
        return 0

    lax.fori_loop(0, steps // AT_ONCE, gated_step, 0)
    in_rows(ys, gated_own, gated_oth)


def fold(value):
    return jnp.sum(value, axis=0)


def rec_bwd_kernel(
    count, bits, bx_own, bx_oth, by_own, by_oth, state_ref, in_ref, rate_ref, conv_ref, up_own, up_oth, mask_ref, prm_ref, gate_ref,
    gx_own, gx_oth, gy_own, gy_oth, gw_ref, sum_ref, xs, ys, us, gs, factor, to_log, to_in, to_rate, to_conv, gc, dg, gw,
):
    place = lax.axis_index("tp")
    steps, both, lanes = state_ref.shape
    length = steps * both
    in_steps(bx_own, bx_oth, xs, 3)
    xs[0:3] = from_segment(xs[steps : steps + 3], place, False)
    in_steps(by_own, by_oth, ys, 0)
    in_steps(up_own, up_oth, us, 0)

    def scan_step(index, carried):
        sent, product = carried
        at = steps - AT_ONCE - index * AT_ONCE
        block = pl.ds(at, AT_ONCE)
        in_gate, rate_gate = in_ref[block], rate_ref[block]
        keep = wide_mask(mask_ref, 0, at, AT_ONCE)
        decay, squared, gap, inverse = decay_terms(rate_gate, prm_ref)
        scaling = (1.0 - keep) + keep * (gap * inverse)
        y = ys[block]
        y2 = y * y
        tanh = jnp.tanh(GELU_A * y * (1.0 + GELU_B * y2))
        lift = 0.5 + 0.5 * tanh
        slope = lift + y * (1.0 - tanh * tanh) * (0.5 * GELU_A + (1.5 * GELU_A * GELU_B) * y2)
        up = us[block]
        state = state_ref[block]
        ys[block] = up * state * slope
        direct = up * (y * lift)
        coef = decay * keep
        entered = conv_ref[block].astype(F32) * in_gate
        pushed = entered * scaling
        to_log[block] = ((state - pushed) - entered * (keep * squared * inverse)) * rate_gate
        to_in[block] = pushed * (1.0 - in_gate)
        to_rate[block] = (1.0 - rate_gate) * prm_ref[7:8, :]
        to_conv[block] = in_gate * scaling
        for one in reversed(range(AT_ONCE)):
            grad = direct[one] + sent
            gs[at + one] = grad
            factor[at + one] = product
            sent = coef[one] * grad
            product = coef[one] * product
        return sent, product

    zero = jnp.zeros((both, lanes), F32)
    sent, product = lax.fori_loop(0, steps // AT_ONCE, scan_step, (zero, zero + 1.0))
    enters = entering(sent, product, place, True)

    def grad_step(index, sum_log):
        at = index * AT_ONCE
        block = pl.ds(at, AT_ONCE)
        rows = pl.ds(pl.multiple_of(at * both, AT_ONCE * both), AT_ONCE * both)
        grad = gs[block] + factor[block] * enters
        through = grad * to_log[block]
        dg[rows, 0:lanes] = (grad * to_in[block]).astype(BF16).reshape(AT_ONCE * both, lanes)
        dg[rows, lanes:] = (through * to_rate[block]).astype(BF16).reshape(AT_ONCE * both, lanes)
        gc[block] = grad * to_conv[block]
        return sum_log + fold(through)

    sum_log = lax.fori_loop(0, steps // AT_ONCE, grad_step, zero)

    def back_step(index, _):
        rows = pl.ds(pl.multiple_of(index * 16 * both, 16 * both), 16 * both)
        more = matmul_right(dg[rows, 0:lanes], gate_ref[0, 0]) + matmul_right(dg[rows, lanes:], gate_ref[1, 0])
        gc[pl.ds(index * 16, 16)] += more.reshape(16, both, lanes)
        return 0

    lax.fori_loop(0, steps // 16, back_step, 0)
    conv = conv_ref[...].reshape(length, lanes)
    gw[0:lanes, :] = matmul_left(conv, dg[:, 0:lanes]).astype(BF16)
    gw[lanes:, :] = matmul_left(conv, dg[:, lanes:]).astype(BF16)
    gate_sums = jnp.dot(jnp.ones((8, length), BF16), dg[...], preferred_element_type=F32)
    rows_each = lanes // count
    me = lax.axis_index("dp")
    for spot in range(count):
        block = block_from(me, spot, bits)
        for gate in (0, 1):
            source = pl.ds(pl.multiple_of(gate * lanes + block * rows_each, rows_each), rows_each)
            gw_ref[spot, gate * rows_each : (gate + 1) * rows_each, :] = gw[source, :]
    gc[steps : steps + 3] = from_segment(gc[0:3], place, True)
    taps = [prm_ref[k : k + 1, :] for k in range(4)]

    def conv_step(index, sums):
        at = index * AT_ONCE
        here = gc[pl.ds(at, AT_ONCE)]
        total = taps[0] * here
        sums = [sums[0] + fold(here), sums[1] + fold(here * xs[pl.ds(at + 3, AT_ONCE)])] + list(sums[2:])
        for k in (1, 2, 3):
            total = total + taps[k] * (gc[pl.ds(at + k, AT_ONCE)] * wide_mask(mask_ref, k - 1, at + k, AT_ONCE))
            masked = here * wide_mask(mask_ref, k - 1, at, AT_ONCE)
            sums[k + 1] = sums[k + 1] + fold(masked * xs[pl.ds(at + 3 - k, AT_ONCE)])
        us[pl.ds(at, AT_ONCE)] = total
        return tuple(sums)

    sums = lax.fori_loop(0, steps // AT_ONCE, conv_step, (zero,) * 5)
    for index, value in ((0, sums[1]), (1, sums[2]), (2, sums[3]), (3, sums[4]), (4, sums[0]), (7, sum_log)):
        sum_ref[index : index + 1, :] = jnp.sum(value, axis=0, keepdims=True)
    sum_ref[5:6, :] = gate_sums[0:1, 0:lanes]
    sum_ref[6:7, :] = gate_sums[0:1, lanes:]
    in_rows(us, gx_own, gx_oth)
    in_rows(ys, gy_own, gy_oth)


def rec_specs(half, lanes):
    steps = half // SEGMENTS
    piece = pl.BlockSpec((half, lanes), lambda h: (0, h))
    stepped = pl.BlockSpec((steps, 2 * SEGMENTS, lanes), lambda h: (0, 0, h))
    mask = pl.BlockSpec((3, steps + 3, 2 * SEGMENTS, 128), lambda h: (0, 0, 0, 0))
    prm = pl.BlockSpec((8, lanes), lambda h: (0, h))
    gate = pl.BlockSpec((2, 1, lanes, lanes), lambda h: (0, h, 0, 0))
    return piece, stepped, mask, prm, gate


def rec_fwd(bx_own, bx_oth, by_own, by_oth, mask, prm, gates):
    half, width = bx_own.shape
    length, lanes, heads = 2 * half, gates.shape[2], gates.shape[1]
    steps, both = half // SEGMENTS, 2 * SEGMENTS
    piece, stepped, mask_spec, prm_spec, gate_spec = rec_specs(half, lanes)
    out = jax.ShapeDtypeStruct((half, width), BF16)
    kept = jax.ShapeDtypeStruct((steps, both, width), F32)
    return pl.pallas_call(
        rec_fwd_kernel,
        grid=(heads,),
        in_specs=[piece] * 4 + [mask_spec, prm_spec, gate_spec],
        out_specs=[piece] * 2 + [stepped] * 4,
        out_shape=[out, out, kept, kept, kept, jax.ShapeDtypeStruct((steps, both, width), BF16)],
        scratch_shapes=[
            pltpu.VMEM((steps + 3, both, lanes), F32),
            pltpu.VMEM((steps, both, lanes), F32),
            pltpu.VMEM((length, 2 * lanes), F32),
            pltpu.VMEM((steps, both, lanes), F32),
        ],
        compiler_params=pltpu.CompilerParams(vmem_limit_bytes=40 << 20),
        cost_estimate=pl.CostEstimate(
            flops=4 * length * width * lanes + 100 * length * width,
            bytes_accessed=26 * length * width,
            transcendentals=6 * length * width,
        ),
        name="rec_fwd",
    )(bx_own, bx_oth, by_own, by_oth, mask, prm, gates)


def rec_bwd(bx_own, bx_oth, by_own, by_oth, kept, up_own, up_oth, mask, prm, gates, count, cost):
    half, width = bx_own.shape
    length, lanes, heads = 2 * half, gates.shape[2], gates.shape[1]
    steps, both = half // SEGMENTS, 2 * SEGMENTS
    piece, stepped, mask_spec, prm_spec, gate_spec = rec_specs(half, lanes)
    block = pltpu.VMEM((steps, both, lanes), F32)
    padded = pltpu.VMEM((steps + 3, both, lanes), F32)
    return pl.pallas_call(
        functools.partial(rec_bwd_kernel, count, stage_bits(count, "X" in CROSSED)),
        grid=(heads,),
        in_specs=[piece] * 4 + [stepped] * 4 + [piece] * 2 + [mask_spec, prm_spec, gate_spec],
        out_specs=[piece] * 4 + [pl.BlockSpec((count, 2 * lanes // count, lanes), lambda h: (0, 0, h)), prm_spec],
        out_shape=[jax.ShapeDtypeStruct((half, width), BF16)] * 4
        + [
            jax.ShapeDtypeStruct((count, 2 * lanes // count, width), BF16),
            jax.ShapeDtypeStruct((8, width), F32),
        ],
        scratch_shapes=[padded]
        + [block] * 8
        + [padded, pltpu.VMEM((length, 2 * lanes), BF16), pltpu.VMEM((2 * lanes, lanes), BF16)],
        compiler_params=pltpu.CompilerParams(vmem_limit_bytes=52 << 20),
        cost_estimate=pl.CostEstimate(
            flops=int(cost * (8 * length * width * lanes + 150 * length * width)),
            bytes_accessed=int(cost * 34 * length * width),
            transcendentals=int(cost * 4 * length * width),
        ),
        name="rec_bwd",
    )(bx_own, bx_oth, by_own, by_oth, *kept, up_own, up_oth, mask, prm, gates)


def stage_bits(count, crossed=False):
    bits = [1 << bit for bit in range(count.bit_length() - 1)]
    return [bits[0], bits[2], bits[1]] + bits[3:] if crossed else bits


def block_at(place, bits):
    return sum(bit for step, bit in enumerate(bits) if (place >> (len(bits) - 1 - step)) & 1)


def block_from(me, place, bits):
    relative = block_at(place, bits)
    block = 0
    for bit in bits:
        mine = lax.rem(me // bit, 2)
        block = block + bit * (1 - mine if relative & bit else mine)
    return block


def arrange_kernel(bits, first, second, first_out, second_out):
    @pl.when(pl.program_id(0) == 0)
    def _():
        arranged(first, first_out, bits)

    @pl.when(pl.program_id(0) == 1)
    def _():
        arranged(second, second_out, bits)


def arrange(first, second, bits):
    whole = pl.BlockSpec(first.shape, lambda i: (0, 0))
    shape = jax.ShapeDtypeStruct(first.shape, first.dtype)
    return pl.pallas_call(
        functools.partial(arrange_kernel, bits),
        grid=(2,),
        in_specs=[whole, whole],
        out_specs=[whole, whole],
        out_shape=[shape, shape],
        compiler_params=pltpu.CompilerParams(vmem_limit_bytes=24 << 20),
        cost_estimate=pl.CostEstimate(flops=0, bytes_accessed=12 * first.size, transcendentals=0),
        name="arrange",
    )(first, second)


def weight_grad_kernel(more, own_a, own_b, oth_a, oth_b, right_own, right_oth, *rest):
    extra, (sent_next, kept, staged, landed, send_sem, recv_sem) = rest[:-6], rest[-6:]
    step = pl.program_id(0)
    me = lax.axis_index("dp")
    partner = {"dp": me + 1 - 2 * lax.rem(me, 2)}

    @pl.when(step == 0)
    def _():
        barrier = pltpu.get_barrier_semaphore()
        pl.semaphore_signal(barrier, inc=1, device_id=partner, device_id_type=MESH)
        pl.semaphore_wait(barrier, 1)

    def copy(tile):
        return pltpu.make_async_remote_copy(
            src_ref=staged.at[tile],
            dst_ref=landed.at[tile],
            send_sem=send_sem.at[tile],
            recv_sem=recv_sem.at[tile],
            device_id=partner,
            device_id_type=MESH,
        )

    left_own = jnp.concatenate([own_a[...], own_b[...]], axis=1)
    left_oth = jnp.concatenate([oth_a[...], oth_b[...]], axis=1)
    total = matmul_left(left_own, right_own[...]) + matmul_left(left_oth, right_oth[...])

    def pieces():
        if not more:
            return [(slice(0, total.shape[0]), total)]
        out = []
        for block in range(total.shape[0] // 128):
            first = block * (128 + more)
            out.append((slice(first, first + 128), total[block * 128 : (block + 1) * 128]))
            out.append((slice(first + 128, first + 128 + more), extra[0][block].astype(F32)))
        return out

    @pl.when(step < 2)
    def _():
        for rows, value in pieces():
            staged[step, rows, :] = value.astype(BF16)
        copy(step).start()

    def finish(tile, into):
        copy(tile).wait_recv()
        for rows, value in pieces():
            into[rows, :] = (value + landed[tile, rows, :].astype(F32)).astype(BF16)

    @pl.when(step == 2)
    def _():
        finish(0, sent_next)

    @pl.when(step == 3)
    def _():
        finish(1, kept)
        for tile in range(2):
            copy(tile).wait_send()


def weight_grad(left_own, left_oth, right_own, right_oth, crossed, cost, extra=None):
    half, cols = right_own.shape
    rows = left_own.shape[1] // 4
    more = 0 if extra is None else extra.shape[1]
    height = rows + rows // 128 * more
    out = pltpu.HBM((height, cols), BF16)

    def columns(part):
        def index(i):
            quarter = 3 - i
            return 0, (quarter // 2 * 4 + part * 2 + lax.rem(quarter, 2) if crossed else quarter * 2 + part)

        return pl.BlockSpec((half, rows // 2), index)

    right = pl.BlockSpec((half, cols), lambda i: (0, 0))
    whole = pl.BlockSpec((height, cols), lambda i: (0, 0))
    specs = [columns(0), columns(1), columns(0), columns(1), right, right]
    args = [left_own, left_own, left_oth, left_oth, right_own, right_oth]
    if more:
        specs.append(pl.BlockSpec((rows // 128, more, cols), lambda i: (3 - i, 0, 0)))
        args.append(extra)
    return pl.pallas_call(
        functools.partial(weight_grad_kernel, more),
        grid=(4,),
        in_specs=specs,
        out_specs=[whole, whole],
        out_shape=[out, out],
        scratch_shapes=[
            pltpu.VMEM((2, height, cols), BF16),
            pltpu.VMEM((2, height, cols), BF16),
            pltpu.SemaphoreType.DMA((2,)),
            pltpu.SemaphoreType.DMA((2,)),
        ],
        compiler_params=pltpu.CompilerParams(
            collective_id=4 * bool(more) + 2 * (cols > 2048) + crossed, has_side_effects=True, vmem_limit_bytes=60 << 20
        ),
        cost_estimate=pl.CostEstimate(
            flops=int(cost * 16 * half * rows * cols), bytes_accessed=int(cost * 16 * half * cols), transcendentals=0
        ),
        name="weight_grad",
    )(*args)


ROWS = 64


def arranged(source, into, bits):
    me = lax.axis_index("dp")
    count = 1 << len(bits)
    cols = source.shape[1] // count
    for place in range(count):
        block = pl.ds(pl.multiple_of(block_from(me, place, bits) * cols, cols), cols)
        into[:, place * cols : (place + 1) * cols] = source[:, block]


def feed_kernel(bits, sub, tokens, part, other, gain, grad_hidden, w_gate, w_up, middle, cols, hidden, grad_gate, grad_up, normed):
    @pl.when(pl.program_id(0) == 0)
    def _():
        def rows_step(index, _):
            rows = pl.ds(pl.multiple_of(index * ROWS, ROWS), ROWS)
            total = tokens[rows, :].astype(F32) + (part[rows, :].astype(F32) + other[rows, :].astype(F32))
            middle[rows, :] = total
            scale = lax.rsqrt(jnp.mean(total * total, axis=-1, keepdims=True) + EPS)
            normed[rows, :] = (total * scale * gain[...]).astype(BF16)
            return 0

        lax.fori_loop(0, tokens.shape[0] // ROWS, rows_step, 0)
        arranged(normed, cols, bits)

    for start in range(0, w_gate.shape[1], sub):
        part_cols = slice(start, start + sub)
        gate = jnp.dot(normed[...], w_gate[:, part_cols], preferred_element_type=F32)
        up = jnp.dot(normed[...], w_up[:, part_cols], preferred_element_type=F32)
        squared = gate * gate
        tanh = jnp.tanh(GELU_A * gate * (1.0 + GELU_B * squared))
        lift = 0.5 + 0.5 * tanh
        slope = lift + gate * (1.0 - tanh * tanh) * (0.5 * GELU_A + (1.5 * GELU_A * GELU_B) * squared)
        gelu = gate * lift
        back = grad_hidden[:, part_cols].astype(F32)
        hidden[:, part_cols] = (gelu * up).astype(BF16)
        grad_gate[:, part_cols] = (back * up * slope).astype(BF16)
        grad_up[:, part_cols] = (back * gelu).astype(BF16)


def feed(tokens, part, other, gain, grad_hidden, w_gate, w_up, bits, wide=768, sub=768):
    rows, model = tokens.shape
    cols = w_gate.shape[1]
    whole = pl.BlockSpec((rows, model), lambda n: (0, 0))
    piece = pl.BlockSpec((rows, wide), lambda n: (0, n))
    weight = pl.BlockSpec((model, wide), lambda n: (0, n))
    out = jax.ShapeDtypeStruct((rows, cols), BF16)
    return pl.pallas_call(
        functools.partial(feed_kernel, bits, sub),
        grid=(cols // wide,),
        in_specs=[whole] * 3 + [pl.BlockSpec((1, model), lambda n: (0, 0)), piece, weight, weight],
        out_specs=[whole, whole, piece, piece, piece],
        out_shape=[jax.ShapeDtypeStruct((rows, model), F32), jax.ShapeDtypeStruct((rows, model), BF16), out, out, out],
        scratch_shapes=[pltpu.VMEM((rows, model), BF16)],
        compiler_params=pltpu.CompilerParams(vmem_limit_bytes=56 << 20),
        cost_estimate=pl.CostEstimate(
            flops=4 * rows * model * cols, bytes_accessed=4 * model * cols + 12 * rows * cols, transcendentals=rows * cols
        ),
        name="feed",
    )(tokens, part, other, gain, grad_hidden, w_gate, w_up)


def pull_kernel(bits, middle, back, other, cot, gain, weight, grad, cols, into, rec):
    @pl.when(pl.program_id(0) == 0)
    def _():
        def rows_step(index, _):
            rows = pl.ds(pl.multiple_of(index * ROWS, ROWS), ROWS)
            values = middle[rows, :]
            scale = lax.rsqrt(jnp.mean(values * values, axis=-1, keepdims=True) + EPS)
            lifted = gain[...] * (back[rows, :].astype(F32) + other[rows, :].astype(F32))
            pulled = jnp.mean(values * lifted, axis=-1, keepdims=True)
            total = cot[rows, :].astype(F32) + (scale * lifted - values * (scale * scale * scale * pulled))
            grad[rows, :] = total
            rec[rows, :] = total.astype(BF16)
            return 0

        lax.fori_loop(0, middle.shape[0] // ROWS, rows_step, 0)
        arranged(rec, cols, bits)

    into[...] = matmul_right(rec[...], weight[...])


def pull(middle, back, other, cot, gain, weight, bits, cost, wide=640):
    rows, model = middle.shape
    cols = weight.shape[0]
    wide = wide if cols % wide == 0 else cols
    whole = pl.BlockSpec((rows, model), lambda n: (0, 0))
    return pl.pallas_call(
        functools.partial(pull_kernel, bits),
        grid=(cols // wide,),
        in_specs=[whole] * 4 + [pl.BlockSpec((1, model), lambda n: (0, 0)), pl.BlockSpec((wide, model), lambda n: (n, 0))],
        out_specs=[whole, whole, pl.BlockSpec((rows, wide), lambda n: (0, n))],
        out_shape=[
            jax.ShapeDtypeStruct((rows, model), F32),
            jax.ShapeDtypeStruct((rows, model), BF16),
            jax.ShapeDtypeStruct((rows, cols), F32),
        ],
        scratch_shapes=[pltpu.VMEM((rows, model), BF16)],
        compiler_params=pltpu.CompilerParams(vmem_limit_bytes=56 << 20),
        cost_estimate=pl.CostEstimate(
            flops=int(cost * 2 * rows * model * cols),
            bytes_accessed=int(cost * (16 * rows * model + 4 * rows * cols)),
            transcendentals=0,
        ),
        name="pull",
    )(middle, back, other, cot, gain, weight)


def two_back_kernel(first, first_w, second, second_w, out):
    out[...] = (matmul_right(first[...], first_w[...]) + matmul_right(second[...], second_w[...])).astype(BF16)


def two_back(first, first_w, second, second_w, cost=1.0):
    rows, depth = first.shape
    cols = first_w.shape[0]
    step = 512
    left = pl.BlockSpec((rows, depth), lambda n: (0, 0))
    right = pl.BlockSpec((step, depth), lambda n: (n, 0))
    return pl.pallas_call(
        two_back_kernel,
        grid=(cols // step,),
        in_specs=[left, right, left, right],
        out_specs=pl.BlockSpec((rows, step), lambda n: (0, n)),
        out_shape=jax.ShapeDtypeStruct((rows, cols), BF16),
        compiler_params=pltpu.CompilerParams(vmem_limit_bytes=48 << 20),
        cost_estimate=pl.CostEstimate(
            flops=int(cost * 4 * rows * depth * cols), bytes_accessed=int(cost * 4 * depth * (rows + cols)), transcendentals=0
        ),
        name="two_back",
    )(first, first_w, second, second_w)


def swap(value):
    return lax.ppermute(value, "tp", [(0, 1), (1, 0)])


def flip(value, bit):
    count = lax.axis_size("dp")
    return lax.ppermute(value, "dp", [(source, source ^ bit) for source in range(count)])


def halve_kernel(keep_low, keep_high, received_low, received_high, kept, sent):
    kept[...] = (keep_low[...].astype(F32) + received_low[...].astype(F32)).astype(BF16)
    sent[...] = (keep_high[...].astype(F32) + received_high[...].astype(F32)).astype(BF16)


def halve(keep, received, cost):
    rows, cols = keep.shape
    block = rows // 4 if rows > 512 else rows // 2
    steps = rows // 2 // block
    low = pl.BlockSpec((block, cols), lambda i: (i, 0))
    high = pl.BlockSpec((block, cols), lambda i: (i + steps, 0))
    return pl.pallas_call(
        halve_kernel,
        grid=(steps,),
        in_specs=[low, high, low, high],
        out_specs=[low, low],
        out_shape=[pltpu.HBM((rows // 2, cols), BF16)] * 2,
        compiler_params=pltpu.CompilerParams(vmem_limit_bytes=32 << 20),
        cost_estimate=pl.CostEstimate(flops=0, bytes_accessed=int(cost * 6 * rows * cols), transcendentals=0),
        name="halve",
    )(keep, keep, received, received)


class Reduction:
    def __init__(self, left, right, count, crossed, cost, extra=None):
        self.bits = stage_bits(count, crossed)[1:]
        sent, self.keep = weight_grad(*left, *right, crossed, cost, extra)
        self.pass_on(sent)

    def pass_on(self, sent):
        self.received = flip(sent, self.bits.pop(0))

    def step(self, cost, *others):
        self.keep, sent = halve(self.keep, after(self.received, *others), cost)
        self.pass_on(sent)
        return sent

    def total(self, *others):
        while self.bits:
            self.step(1.0, *others)
        return self.keep.astype(F32) + after(self.received, *others).astype(F32)


def after(value, *others):
    return lax.optimization_barrier((value, *others))[0]


def norm_back(values, gain, grad):
    scale = lax.rsqrt(jnp.mean(values * values, axis=-1, keepdims=True) + EPS)
    lifted = gain * grad
    pull = jnp.mean(values * lifted, axis=-1, keepdims=True)
    return scale * lifted - values * (scale * scale * scale * pull)


def local_channels(
    layer_in, cotangent, resets, norm_gains, w_x, w_y, conv_w, lru_bias, a_param, gate_blocks, w_out, w_gate, w_up, w_down,
):
    place = lax.axis_index("tp")
    me = lax.axis_index("dp")
    count = lax.axis_size("dp")
    bits = stage_bits(count)
    width = w_x.shape[1]
    full_width = conv_w.shape[1]
    heads = gate_blocks.shape[1] // 2
    model = norm_gains.shape[1]

    own_in, own_cot = layer_in[0], cotangent[0]
    oth_in = swap(own_in)
    oth_resets = swap(resets[0])
    oth_cot = swap(own_cot)
    normed_own = rms_scale(own_in.astype(F32), norm_gains[0]).astype(BF16)
    bx_own = matmul(normed_own, w_x).astype(BF16)
    by_own = matmul(normed_own, w_y)

    first_place = place == 0
    in_time = jnp.where(first_place, resets[0], oth_resets), jnp.where(first_place, oth_resets, resets[0])
    keep = 1.0 - jnp.concatenate(in_time).astype(F32)
    keep_1 = jnp.concatenate([jnp.ones((1,), F32), keep[:-1]])
    keep_2 = jnp.concatenate([jnp.ones((1,), F32), keep_1[:-1]])
    valid = jnp.stack([keep, keep * keep_1, keep * keep_1 * keep_2]).reshape(3, 2, SEGMENTS, -1)
    valid = jnp.where(first_place, valid, valid[:, ::-1]).reshape(3, 2 * SEGMENTS, -1)
    later = jnp.concatenate([valid[:, 1:, :3], valid[:, :1, :3]], axis=1)
    mask = jnp.swapaxes(jnp.concatenate([valid, later], axis=2), 1, 2)
    mask = jnp.broadcast_to(mask[..., None], mask.shape + (128,))
    table = jnp.concatenate([conv_w, lru_bias, -8.0 * jax.nn.softplus(a_param)[None]], axis=0)
    prm = lax.dynamic_slice(table, (0, place * width), (8, width))
    gates = lax.dynamic_slice_in_dim(gate_blocks, place * heads, heads, axis=1)

    gh_own = matmul_right(after(own_cot, bx_own, by_own), w_down)
    normed_oth = rms_scale(after(oth_in, gh_own).astype(F32), norm_gains[0]).astype(BF16)
    bx_oth = matmul(normed_oth, w_x).astype(BF16)
    by_oth = matmul(normed_oth, w_y)
    gated_own, gated_oth, *kept = rec_fwd(bx_own, bx_oth, by_own, by_oth, mask, prm, gates)

    part_oth = matmul(gated_oth, w_out).astype(BF16)
    swap_own = swap(part_oth)
    part_own = matmul(after(gated_own, part_oth), w_out).astype(BF16)
    swap_oth = swap(part_own)
    gh_oth = matmul_right(after(oth_cot, part_own), w_down)
    cot_cols = arrange(after(own_cot, gh_oth), oth_cot, bits)
    normed_cols = arrange(after(normed_own, cot_cols[0]), normed_oth, bits)
    gains = norm_gains[1:2]

    middle_own, two_own, hidden_own, gg_own, gu_own = feed(
        own_in, part_own, after(swap_own, normed_cols[0]), gains, gh_own, w_gate, w_up, bits
    )
    back_own = two_back(gg_own, w_gate, gu_own, w_up)
    back_own_swapped = swap(back_own)
    middle_oth, two_oth, hidden_oth, gg_oth, gu_oth = feed(
        oth_in, part_oth, after(swap_oth, back_own), gains, gh_oth, w_gate, w_up, bits
    )
    sums_over = {}
    at = {"done": hidden_oth}

    def reduce_kernel(name, letter, left, right, extra=None):
        left = (after(left[0], at["done"]), left[1])
        sums_over[letter] = Reduction(left, right, count, letter in CROSSED, COSTS.get(name, 1.0), extra)
        return sums_over[letter].keep

    def back_other(cost):
        at["back"] = two_back(after(gg_oth, at["done"]), w_gate, gu_oth, w_up, cost)
        at["back_swapped"] = swap(at["back"])
        return at["back"]

    def pull_other(cost):
        other = after(back_own_swapped, at["done"])
        _, at["rec_oth"], at["into_oth"] = pull(middle_oth, at["back"], other, oth_cot, gains, w_out, bits, cost)
        return at["into_oth"]

    def pull_own(cost):
        other = after(at["back_swapped"], at["done"])
        at["grad_own"], at["rec_own"], at["into_own"] = pull(middle_own, back_own, other, own_cot, gains, w_out, bits, cost)
        return at["into_own"]

    def recurrence(cost):
        into = after(at["into_own"], at["done"]), at["into_oth"]
        *grads, gate_sums, sums = rec_bwd(bx_own, bx_oth, by_own, by_oth, kept, *into, mask, prm, gates, count, cost)
        at["gx"], at["gy"] = grads[0:2], grads[2:4]
        row = jnp.arange(8)[:, None] == 7
        slopes = -8.0 * lax.dynamic_slice(jax.nn.sigmoid(a_param), (place * width,), (width,))
        sums = jnp.swapaxes(jnp.where(row, sums * slopes, sums).reshape(8, count // 2, each), 0, 1)
        order = [block_at(spot, stage_bits(count, "X" in CROSSED)) for spot in range(count)]
        chosen = jnp.bitwise_xor(jnp.array(order), me)[:, None] % (count // 2) == jnp.arange(count // 2)[None, :]
        sums = matmul(chosen.astype(BF16), sums.astype(BF16).reshape(count // 2, -1)).reshape(count, 8, each)
        sums = jnp.pad(sums.astype(BF16), ((0, 0), (0, 8), (0, width - each)))
        at["extra"] = jnp.concatenate([gate_sums, sums], axis=1)
        return grads[0]

    def rec_rows(index):
        def run(cost):
            name = ("rec_keep", "rec_send")[index]
            at[name] = two_back(after(at["gx"][index], at["done"]), w_x, at["gy"][index], w_y, cost)
            if index == 1:
                at["rec_swapped"] = swap(at[name])
            return at[name]

        return run

    def out_other(cost):
        sent = matmul(after(hidden_oth, at["done"]), w_down).astype(BF16)
        at["out_swapped"] = swap(sent)
        return sent

    def out_own(cost):
        at["out_keep"] = matmul(after(hidden_own, at["done"]), w_down).astype(BF16)
        return at["out_keep"]

    def to_inputs(cost):
        grad_normed = at["rec_keep"].astype(F32) + after(at["rec_swapped"], at["done"]).astype(F32)
        at["input_grad"] = at["grad_own"] + norm_back(own_in.astype(F32), norm_gains[0], grad_normed)
        return at["input_grad"]

    def to_outputs(cost):
        total = middle_own + at["out_keep"].astype(F32) + after(at["out_swapped"], at["done"]).astype(F32)
        at["layer_out"] = total.astype(BF16)
        return at["layer_out"]

    def swap_blocks(cost):
        at["mine"] = after(grads["X"][block:], at["done"]).astype(BF16)
        at["others"] = swap(at["mine"])
        return at["others"]

    each = full_width // count
    block = model // count

    def gain_grad(gain, *pairs):
        weights = sum(
            jnp.sum(lax.dynamic_slice_in_dim(weight, me * block, block, axis=0).astype(F32) * grad, axis=1)
            for weight, grad in pairs
        )
        return weights / lax.dynamic_slice_in_dim(gain, me * block, block, axis=0)

    def sum_gains(cost):
        first = gain_grad(norm_gains[0], (w_x, grads["X"][:block]), (w_y, grads["Y"]))
        second = gain_grad(norm_gains[1], (w_gate, grads["G"]), (w_up, grads["U"]))
        gains = after(jnp.stack([first, second]), at["done"])
        at["gains"] = gains + swap(gains)
        return gains

    steps = {
        "DK": lambda cost: reduce_kernel("DK", "D", cot_cols, (hidden_own, hidden_oth)),
        "GK": lambda cost: reduce_kernel("GK", "G", (two_own, two_oth), (gg_own, gg_oth)),
        "UK": lambda cost: reduce_kernel("UK", "U", (two_own, two_oth), (gu_own, gu_oth)),
        "OUT": lambda cost: reduce_kernel("OUT", "O", (at["rec_own"], at["rec_oth"]), (gated_own, gated_oth)),
        "X": lambda cost: reduce_kernel("X", "X", normed_cols, at["gx"], at["extra"]),
        "Y": lambda cost: reduce_kernel("Y", "Y", normed_cols, at["gy"]),
        "B2": back_other,
        "P2": pull_other,
        "P1": pull_own,
        "RB": recurrence,
        "RS": rec_rows(1),
        "RK": rec_rows(0),
        "OS": out_other,
        "OK": out_own,
        "IG": to_inputs,
        "LO": to_outputs,
        "SW": swap_blocks,
        "GN": sum_gains,
    }
    grads = {}
    for name in ORDER:
        if name in steps:
            at["done"] = steps[name](COSTS.get(name, 1.0))
        elif name[1] == "t":
            total = sums_over[name[0]].total(at["done"])
            at["done"] = grads[name[0]] = total.T if name[0] in "DO" else total
        else:
            at["done"] = sums_over[name[0]].step(COSTS.get(name, 1.0), at["done"])
    mine, others, layer_out, input_grad = (at[name] for name in ("mine", "others", "layer_out", "input_grad"))
    down_grad, gate_grad, up_grad, out_grad, x_grad, y_grad = (grads[letter] for letter in "DGUOXY")
    x_grad = x_grad[:block]
    low, high = jnp.where(first_place, mine, others), jnp.where(first_place, others, mine)
    both = jnp.stack([low[:-16], high[:-16]]).astype(F32).reshape(2, 2, -1, heads, gates.shape[-1])
    block_sums = jnp.transpose(both, (1, 0, 3, 2, 4)).reshape(2, 2 * heads, -1, gates.shape[-1])
    small = jnp.where(me < count // 2, low[-16:-8], high[-16:-8])[:, :each].astype(F32)

    return (
        layer_out[None],
        input_grad[None],
        at["gains"],
        x_grad,
        y_grad,
        small[0:4],
        small[4:7],
        small[7],
        block_sums,
        out_grad,
        gate_grad,
        up_grad,
        down_grad,
    )


def from_behind(value, axis, steps):
    count = lax.axis_size(axis)
    first, last = (max(0, -steps), min(count, count - steps))
    return lax.ppermute(value, axis, [(source, source + steps) for source in range(first, last)])


def rms_scale(values, gain_vec):
    return values * lax.rsqrt(jnp.mean(values * values, axis=-1, keepdims=True) + EPS) * gain_vec


def gelu_product(gate_val, up_val):
    return jax.nn.gelu(gate_val, approximate=True) * up_val


def lru_terms(conv_out, gate_in, gate_rate, a_param, starts):
    keep_mask = 1.0 - starts
    input_gate = jax.nn.sigmoid(gate_in)
    rate_gate = jax.nn.sigmoid(gate_rate)
    log_decay = -8.0 * rate_gate * jax.nn.softplus(a_param)
    scaling = starts + keep_mask * jnp.sqrt(-jnp.expm1(2.0 * log_decay))
    return (jnp.exp(log_decay) * keep_mask, conv_out * input_gate * scaling)


def matmul(first_mat, second_mat):
    return jnp.dot(first_mat, second_mat, preferred_element_type=jnp.float32)


def matmul_left(first_mat, second_mat):
    return lax.dot_general(
        first_mat, second_mat, (((0,), (0,)), ((), ())), preferred_element_type=jnp.float32
    )


def matmul_right(first_mat, second_mat):
    return lax.dot_general(
        first_mat, second_mat, (((1,), (1,)), ((), ())), preferred_element_type=jnp.float32
    )


def combine_state(first_item, second_item):
    return (first_item[0] * second_item[0], second_item[1] + second_item[0] * first_item[1])


def carry_across(coef_end, state_end, reverse):
    incoming = jnp.zeros_like(state_end)
    direction = -1 if reverse else 1
    for turn_index in range(lax.axis_size("tp") - 1):
        incoming = from_behind(state_end + coef_end * incoming, "tp", direction)
    return incoming


def local(
    layer_in,
    cotangent,
    resets,
    norm_gains,
    w_x,
    w_y,
    conv_w,
    lru_bias,
    a_param,
    gate_blocks,
    w_out,
    w_gate,
    w_up,
    w_down,
):
    inputs = layer_in[0].astype(jnp.float32)
    starts = resets[0].astype(jnp.float32)
    keep_mask = 1.0 - starts
    rim_size = conv_w.shape[0] - 1
    head_count = gate_blocks.shape[1]
    block_size = gate_blocks.shape[2]
    full_width = conv_w.shape[1]
    normed, norm_pull = jax.vjp(rms_scale, inputs, norm_gains[0])
    normed_low = normed.astype(jnp.bfloat16)
    proj_x, proj_y, proj_out = (
        lax.all_gather(w_x, "tp", axis=1, tiled=True),
        lax.all_gather(w_y, "tp", axis=1, tiled=True),
        lax.all_gather(w_out, "tp", axis=0, tiled=True),
    )
    rec_len = normed_low.shape[0]
    branch_x = matmul(normed_low, proj_x).astype(jnp.bfloat16)
    branch_y = matmul(normed_low, proj_y)
    rim_rows, rim_keep = from_behind(
        (branch_x[rec_len - rim_size :], keep_mask[rec_len - rim_size :].astype(jnp.bfloat16)),
        "tp",
        1,
    )
    padded_x = jnp.concatenate([rim_rows, branch_x], axis=0).astype(jnp.float32)
    padded_keep = jnp.concatenate([rim_keep.astype(jnp.float32), keep_mask])
    conv_sum = conv_w[0] * padded_x[rim_size:]
    valid_mask = keep_mask
    valid_list = []
    for offset in range(1, rim_size + 1):
        valid_list.append(valid_mask)
        conv_sum = (
            conv_sum
            + valid_mask[:, None]
            * conv_w[offset]
            * padded_x[rim_size - offset : rim_size - offset + rec_len]
        )
        valid_mask = valid_mask * padded_keep[rim_size - offset : rim_size - offset + rec_len]
    conv_out = (conv_sum + lru_bias[0]).astype(jnp.bfloat16)
    row_count = conv_out.shape[0]
    conv_blocks = conv_out.reshape(row_count, head_count, block_size)
    pre_rows = (
        jnp.einsum(
            "lhb,ghbc->glhc", conv_blocks, gate_blocks, preferred_element_type=jnp.float32
        ).reshape(2, row_count, full_width)
        + lru_bias[1:3][:, None, :]
    )
    gate_in = pre_rows[0]
    gate_rate = pre_rows[1]
    conv_float = conv_out.astype(jnp.float32)

    def lru_local(conv_in, in_pre, rate_pre, decay_in):
        return lru_terms(conv_in, in_pre, rate_pre, decay_in, starts[:, None])

    (decay_rate, pushed), lru_pull = jax.vjp(lru_local, conv_float, gate_in, gate_rate, a_param)
    decay_cum, local_states = lax.associative_scan(combine_state, (decay_rate, pushed), axis=0)
    incoming = carry_across(decay_cum[-1], local_states[-1], False)
    states = local_states + decay_cum * incoming
    gated_val, gated_pull = jax.vjp(gelu_product, branch_y, states)
    gated_low = gated_val.astype(jnp.bfloat16)
    recurrent = matmul(gated_low, proj_out)
    middle = inputs + recurrent
    normed_two, norm_two_pull = jax.vjp(rms_scale, middle, norm_gains[1])
    normed_two_low = normed_two.astype(jnp.bfloat16)
    group_rows = lax.all_gather(normed_two_low, "tp", axis=0, tiled=True)
    gate_val = matmul(group_rows, w_gate)
    up_val = matmul(group_rows, w_up)
    hidden_val, mlp_pull = jax.vjp(gelu_product, gate_val, up_val)
    hidden = hidden_val.astype(jnp.bfloat16)
    mlp_out = lax.psum_scatter(
        matmul(hidden, w_down).astype(jnp.bfloat16), "tp", scatter_dimension=0, tiled=True
    ).astype(jnp.float32)
    layer_out = (middle + mlp_out).astype(jnp.bfloat16)
    grad_out = cotangent[0].astype(jnp.float32)
    group_grad = lax.all_gather(cotangent[0], "tp", axis=0, tiled=True)
    w_down_grad = matmul_left(hidden, group_grad)
    grad_hidden = matmul_right(group_grad, w_down)
    grad_gate, grad_up = mlp_pull(grad_hidden)
    grad_gate = grad_gate.astype(jnp.bfloat16)
    grad_up = grad_up.astype(jnp.bfloat16)
    w_gate_grad = matmul_left(group_rows, grad_gate)
    w_up_grad = matmul_left(group_rows, grad_up)
    grad_normed_two = lax.psum_scatter(
        (matmul_right(grad_gate, w_gate) + matmul_right(grad_up, w_up)).astype(jnp.bfloat16),
        "tp",
        scatter_dimension=0,
        tiled=True,
    ).astype(jnp.float32)
    grad_middle, gain_two_grad = norm_two_pull(grad_normed_two)
    grad_middle = grad_middle + grad_out
    grad_rec = grad_middle.astype(jnp.bfloat16)
    grad_gated = matmul_right(grad_rec, proj_out)
    grad_branch_y, grad_direct = gated_pull(grad_gated)
    grad_branch_y = grad_branch_y.astype(jnp.bfloat16)
    decay_next = jnp.concatenate([decay_rate[1:], jnp.ones_like(decay_rate[:1])], axis=0)
    reach_back, local_grads = lax.associative_scan(
        combine_state, (decay_next, grad_direct), reverse=True, axis=0
    )
    outgoing = carry_across(decay_rate[0] * reach_back[0], decay_rate[0] * local_grads[0], True)
    state_grads = local_grads + reach_back * outgoing
    prior_states = jnp.concatenate([incoming[None], states[:-1]], axis=0)
    grad_conv, grad_in, grad_rate, a_local_grad = lru_pull(
        (state_grads * prior_states, state_grads)
    )
    grad_pre = jnp.stack([grad_in, grad_rate]).astype(jnp.bfloat16)
    pre_sums = jnp.sum(grad_pre.astype(jnp.float32), axis=1)
    pre_blocks = grad_pre.reshape(2, row_count, head_count, block_size)
    gate_blocks_grad = jnp.einsum(
        "lhb,glhc->ghbc", conv_blocks, pre_blocks, preferred_element_type=jnp.float32
    )
    gate_back = jnp.einsum(
        "glhc,ghbc->lhb", pre_blocks, gate_blocks, preferred_element_type=jnp.float32
    ).reshape(row_count, full_width)
    grad_conv = grad_conv + gate_back
    conv_w_rows = [jnp.sum(grad_conv * padded_x[rim_size:], axis=0)]
    grad_padded = (
        jnp.zeros((rec_len + rim_size, full_width), jnp.float32)
        .at[rim_size:]
        .add(conv_w[0] * grad_conv)
    )
    for offset in range(1, rim_size + 1):
        masked = valid_list[offset - 1][:, None] * grad_conv
        conv_w_rows.append(
            jnp.sum(masked * padded_x[rim_size - offset : rim_size - offset + rec_len], axis=0)
        )
        grad_padded = grad_padded.at[rim_size - offset : rim_size - offset + rec_len].add(
            conv_w[offset] * masked
        )
    returned = from_behind(grad_padded[:rim_size], "tp", -1)
    grad_x_branch = (
        grad_padded[rim_size:].at[rec_len - rim_size :].add(returned).astype(jnp.bfloat16)
    )
    conv_w_grad = jnp.stack(conv_w_rows)
    lru_bias_grad = jnp.concatenate([jnp.sum(grad_conv, axis=0)[None], pre_sums], axis=0)
    grad_normed = matmul_right(grad_x_branch, proj_x) + matmul_right(grad_branch_y, proj_y)
    grad_inputs, gain_one_grad = norm_pull(grad_normed)
    input_grad = grad_middle + grad_inputs
    w_x_grad, w_y_grad, w_out_grad = (
        lax.psum_scatter(
            matmul_left(normed_low, grad_x_branch).astype(jnp.bfloat16),
            "tp",
            scatter_dimension=1,
            tiled=True,
        ).astype(jnp.float32),
        lax.psum_scatter(
            matmul_left(normed_low, grad_branch_y).astype(jnp.bfloat16),
            "tp",
            scatter_dimension=1,
            tiled=True,
        ).astype(jnp.float32),
        lax.psum_scatter(
            matmul_left(gated_low, grad_rec).astype(jnp.bfloat16),
            "tp",
            scatter_dimension=0,
            tiled=True,
        ).astype(jnp.float32),
    )
    norm_gains_grad = jnp.stack([gain_one_grad, gain_two_grad])
    totals = (
        lax.psum_scatter(
            w_x_grad.astype(jnp.bfloat16), "dp", scatter_dimension=0, tiled=True
        ).astype(jnp.float32),
        lax.psum_scatter(
            w_y_grad.astype(jnp.bfloat16), "dp", scatter_dimension=0, tiled=True
        ).astype(jnp.float32),
        lax.psum_scatter(
            w_out_grad.astype(jnp.bfloat16), "dp", scatter_dimension=1, tiled=True
        ).astype(jnp.float32),
        lax.psum_scatter(
            w_gate_grad.astype(jnp.bfloat16), "dp", scatter_dimension=0, tiled=True
        ).astype(jnp.float32),
        lax.psum_scatter(
            w_up_grad.astype(jnp.bfloat16), "dp", scatter_dimension=0, tiled=True
        ).astype(jnp.float32),
        lax.psum_scatter(
            w_down_grad.astype(jnp.bfloat16), "dp", scatter_dimension=1, tiled=True
        ).astype(jnp.float32),
        lax.psum_scatter(
            norm_gains_grad.astype(jnp.bfloat16), "dp", scatter_dimension=1, tiled=True
        ).astype(jnp.float32),
        lax.psum_scatter(
            conv_w_grad.astype(jnp.bfloat16), "dp", scatter_dimension=1, tiled=True
        ).astype(jnp.float32),
        lax.psum_scatter(
            lru_bias_grad.astype(jnp.bfloat16), "dp", scatter_dimension=1, tiled=True
        ).astype(jnp.float32),
        lax.psum_scatter(
            a_local_grad.astype(jnp.bfloat16), "dp", scatter_dimension=0, tiled=True
        ).astype(jnp.float32),
        lax.psum_scatter(
            gate_blocks_grad.astype(jnp.bfloat16), "dp", scatter_dimension=2, tiled=True
        ).astype(jnp.float32),
    )
    reduced_small = (
        lax.psum(totals[6].astype(jnp.bfloat16), "tp").astype(jnp.float32),
        lax.psum(totals[7].astype(jnp.bfloat16), "tp").astype(jnp.float32),
        lax.psum(totals[8].astype(jnp.bfloat16), "tp").astype(jnp.float32),
        lax.psum(totals[9].astype(jnp.bfloat16), "tp").astype(jnp.float32),
        lax.psum(totals[10].astype(jnp.bfloat16), "tp").astype(jnp.float32),
    )
    return (
        layer_out[None],
        input_grad[None],
        reduced_small[0],
        totals[0],
        totals[1],
        reduced_small[1],
        reduced_small[2],
        reduced_small[3],
        reduced_small[4],
        totals[2],
        totals[3],
        totals[4],
        totals[5],
    )


def solution(mesh):
    rows, cols = mesh.shape["dp"], mesh.shape["tp"]
    by_channels = cols == 2 and rows >= 16 and rows & (rows - 1) == 0

    def step(*args):
        heads, model = args[9].shape[1], args[3].shape[1]
        fits = by_channels and heads % cols == 0 and model % (128 * rows) == 0
        return (local_channels if fits else local)(*args)

    return jax.shard_map(
        step,
        mesh=mesh,
        in_specs=(
            P("dp", "tp", None),
            P("dp", "tp", None),
            P("dp", "tp"),
            P(),
            P(None, "tp"),
            P(None, "tp"),
            P(),
            P(),
            P(),
            P(),
            P("tp", None),
            P(None, "tp"),
            P(None, "tp"),
            P("tp", None),
        ),
        out_specs=(
            P("dp", "tp", None),
            P("dp", "tp", None),
            P(None, "dp"),
            P("dp", "tp"),
            P("dp", "tp"),
            P(None, "dp"),
            P(None, "dp"),
            P("dp"),
            P(None, None, "dp", None),
            P("tp", "dp"),
            P("dp", "tp"),
            P("dp", "tp"),
            P("tp", "dp"),
        ),
        check_vma=False,
    )
```

```python
import functools

import jax
import jax.numpy as jnp
from jax import lax
from jax.experimental import pallas as pl
from jax.experimental.pallas import tpu as pltpu
from jax.sharding import PartitionSpec as P

EPS = 1e-06
F32, BF16 = jnp.float32, jnp.bfloat16
GELU_A, GELU_B = 0.7978845608028654, 0.044715
ORDER = (
    "DK", "GK", "UK", "B2", "P2", "D1", "G1", "P1", "OUT", "D2", "U1", "RB",
    "G2", "X", "Dt", "O1", "RS", "U2", "Gt", "Y", "O2", "X1", "OS", "RK",
    "IG", "Y1", "Ut", "Ot", "X2", "Y2", "OK", "LO", "Xt", "SW", "Yt", "GN",
)
CROSSED = "G"
COSTS = {"B2": 0.6, "GK": 0.6, "P2": 6, "UK": 0.6}
MESH = pl.DeviceIdType.MESH


AT_ONCE = 8
SEGMENTS = 8


def in_steps(own, other, into, first):
    steps = own.shape[0] // SEGMENTS
    for piece, spot in ((own, 0), (other, SEGMENTS)):
        rows = piece[...].astype(F32).reshape(SEGMENTS, steps, piece.shape[1])
        into[first : first + steps, spot : spot + SEGMENTS, :] = jnp.swapaxes(rows, 0, 1)


def in_rows(source, own, other):
    steps, _, lanes = source.shape
    for piece, spot in ((own, 0), (other, SEGMENTS)):
        rows = jnp.swapaxes(source[:, spot : spot + SEGMENTS, :], 0, 1)
        piece[...] = rows.reshape(SEGMENTS * steps, lanes).astype(piece.dtype)


def from_segment(value, place, later):
    segment = lax.broadcasted_iota(jnp.int32, value.shape, 1)
    if later:
        return jnp.where(segment == 2 * SEGMENTS - 1 - SEGMENTS * place, 0.0, pltpu.roll(value, 2 * SEGMENTS - 1, 1))
    return jnp.where(segment == SEGMENTS * place, 0.0, pltpu.roll(value, 1, 1))


def entering(added, factor, place, later):
    def turned(value):
        return jnp.where(place == 1, pltpu.roll(value, SEGMENTS, 0), value)

    added, factor = turned(added), turned(factor)
    state = jnp.zeros_like(added[0:1])
    rows = [None] * (2 * SEGMENTS)
    for index in reversed(range(2 * SEGMENTS)) if later else range(2 * SEGMENTS):
        rows[index] = state
        state = added[index : index + 1] + factor[index : index + 1] * state
    return turned(jnp.concatenate(rows, axis=0))


def wide_mask(mask_ref, index, first, count):
    mask = mask_ref[index, pl.ds(first, count)]
    return jnp.concatenate([mask, mask], axis=2)


def decay_terms(rate_gate, prm_ref):
    log_decay = prm_ref[7:8, :] * rate_gate
    decay = jnp.exp(log_decay)
    squared = decay * decay
    gap = jnp.maximum(-jnp.tanh(log_decay) * (1.0 + squared), 1e-37)
    return decay, squared, gap, lax.rsqrt(gap)


def rec_fwd_kernel(
    bx_own, bx_oth, by_own, by_oth, mask_ref, prm_ref, gate_ref,
    gated_own, gated_oth, state_ref, in_ref, rate_ref, conv_ref, xs, ys, pre, factor,
):
    place = lax.axis_index("tp")
    steps, both, lanes = state_ref.shape
    in_steps(bx_own, bx_oth, xs, 3)
    xs[0:3] = from_segment(xs[steps : steps + 3], place, False)
    in_steps(by_own, by_oth, ys, 0)
    taps = [prm_ref[k : k + 1, :] for k in range(4)]

    def conv_step(index, _):
        at = index * AT_ONCE
        total = taps[0] * xs[pl.ds(at + 3, AT_ONCE)] + prm_ref[4:5, :]
        for k in (1, 2, 3):
            total = total + taps[k] * (wide_mask(mask_ref, k - 1, at, AT_ONCE) * xs[pl.ds(at + 3 - k, AT_ONCE)])
        conv_ref[pl.ds(at, AT_ONCE)] = total.astype(BF16)
        return 0

    lax.fori_loop(0, steps // AT_ONCE, conv_step, 0)

    def gate_step(index, _):
        conv = conv_ref[pl.ds(index * 16, 16)].reshape(16 * both, lanes)
        rows = pl.ds(pl.multiple_of(index * 16 * both, 16 * both), 16 * both)
        pre[rows, 0:lanes] = jnp.dot(conv, gate_ref[0, 0], preferred_element_type=F32)
        pre[rows, lanes:] = jnp.dot(conv, gate_ref[1, 0], preferred_element_type=F32)
        return 0

    lax.fori_loop(0, steps // 16, gate_step, 0)

    def scan_step(index, carried):
        state, product = carried
        at = index * AT_ONCE
        block = pl.ds(at, AT_ONCE)
        rows = pl.ds(pl.multiple_of(at * both, AT_ONCE * both), AT_ONCE * both)
        shape = (AT_ONCE, both, lanes)
        in_gate = jax.nn.sigmoid(pre[rows, 0:lanes] + prm_ref[5:6, :]).reshape(shape)
        rate_gate = (1.0 / (1.0 + jnp.exp(-(pre[rows, lanes:] + prm_ref[6:7, :])))).reshape(shape)
        in_ref[block] = in_gate
        rate_ref[block] = rate_gate
        keep = wide_mask(mask_ref, 0, at, AT_ONCE)
        decay, _, gap, inverse = decay_terms(rate_gate, prm_ref)
        scaling = (1.0 - keep) + keep * (gap * inverse)
        pushed = conv_ref[block].astype(F32) * in_gate * scaling
        coef = decay * keep
        for one in range(AT_ONCE):
            state = coef[one] * state + pushed[one]
            product = coef[one] * product
            state_ref[at + one] = state
            factor[at + one] = product
        return state, product

    zero = jnp.zeros((both, lanes), F32)
    state, product = lax.fori_loop(0, steps // AT_ONCE, scan_step, (zero, zero + 1.0))
    enters = entering(state, product, place, False)

    def gated_step(index, _):
        block = pl.ds(index * AT_ONCE, AT_ONCE)
        state = state_ref[block] + factor[block] * enters
        state_ref[block] = state
        y = ys[block]
        tanh = jnp.tanh(GELU_A * y * (1.0 + GELU_B * (y * y)))
        ys[block] = state * (0.5 * y * (1.0 + tanh))
        return 0

    lax.fori_loop(0, steps // AT_ONCE, gated_step, 0)
    in_rows(ys, gated_own, gated_oth)


def fold(value):
    return jnp.sum(value, axis=0)


def rec_bwd_kernel(
    count, bits, bx_own, bx_oth, by_own, by_oth, state_ref, in_ref, rate_ref, conv_ref, up_own, up_oth, mask_ref, prm_ref, gate_ref,
    gx_own, gx_oth, gy_own, gy_oth, gw_ref, sum_ref, xs, ys, us, gs, factor, to_log, to_in, to_rate, to_conv, gc, dg, gw,
):
    place = lax.axis_index("tp")
    steps, both, lanes = state_ref.shape
    length = steps * both
    in_steps(bx_own, bx_oth, xs, 3)
    xs[0:3] = from_segment(xs[steps : steps + 3], place, False)
    in_steps(by_own, by_oth, ys, 0)
    in_steps(up_own, up_oth, us, 0)

    def scan_step(index, carried):
        sent, product = carried
        at = steps - AT_ONCE - index * AT_ONCE
        block = pl.ds(at, AT_ONCE)
        in_gate, rate_gate = in_ref[block], rate_ref[block]
        keep = wide_mask(mask_ref, 0, at, AT_ONCE)
        decay, squared, gap, inverse = decay_terms(rate_gate, prm_ref)
        scaling = (1.0 - keep) + keep * (gap * inverse)
        y = ys[block]
        y2 = y * y
        tanh = jnp.tanh(GELU_A * y * (1.0 + GELU_B * y2))
        lift = 0.5 + 0.5 * tanh
        slope = lift + y * (1.0 - tanh * tanh) * (0.5 * GELU_A + (1.5 * GELU_A * GELU_B) * y2)
        up = us[block]
        state = state_ref[block]
        ys[block] = up * state * slope
        direct = up * (y * lift)
        coef = decay * keep
        entered = conv_ref[block].astype(F32) * in_gate
        pushed = entered * scaling
        to_log[block] = ((state - pushed) - entered * (keep * squared * inverse)) * rate_gate
        to_in[block] = pushed * (1.0 - in_gate)
        to_rate[block] = (1.0 - rate_gate) * prm_ref[7:8, :]
        to_conv[block] = in_gate * scaling
        for one in reversed(range(AT_ONCE)):
            grad = direct[one] + sent
            gs[at + one] = grad
            factor[at + one] = product
            sent = coef[one] * grad
            product = coef[one] * product
        return sent, product

    zero = jnp.zeros((both, lanes), F32)
    sent, product = lax.fori_loop(0, steps // AT_ONCE, scan_step, (zero, zero + 1.0))
    enters = entering(sent, product, place, True)

    def grad_step(index, sum_log):
        at = index * AT_ONCE
        block = pl.ds(at, AT_ONCE)
        rows = pl.ds(pl.multiple_of(at * both, AT_ONCE * both), AT_ONCE * both)
        grad = gs[block] + factor[block] * enters
        through = grad * to_log[block]
        dg[rows, 0:lanes] = (grad * to_in[block]).astype(BF16).reshape(AT_ONCE * both, lanes)
        dg[rows, lanes:] = (through * to_rate[block]).astype(BF16).reshape(AT_ONCE * both, lanes)
        gc[block] = grad * to_conv[block]
        return sum_log + fold(through)

    sum_log = lax.fori_loop(0, steps // AT_ONCE, grad_step, zero)

    def back_step(index, _):
        rows = pl.ds(pl.multiple_of(index * 16 * both, 16 * both), 16 * both)
        more = matmul_right(dg[rows, 0:lanes], gate_ref[0, 0]) + matmul_right(dg[rows, lanes:], gate_ref[1, 0])
        gc[pl.ds(index * 16, 16)] += more.reshape(16, both, lanes)
        return 0

    lax.fori_loop(0, steps // 16, back_step, 0)
    conv = conv_ref[...].reshape(length, lanes)
    gw[0:lanes, :] = matmul_left(conv, dg[:, 0:lanes]).astype(BF16)
    gw[lanes:, :] = matmul_left(conv, dg[:, lanes:]).astype(BF16)
    gate_sums = jnp.dot(jnp.ones((8, length), BF16), dg[...], preferred_element_type=F32)
    rows_each = lanes // count
    me = lax.axis_index("dp")
    for spot in range(count):
        block = block_from(me, spot, bits)
        for gate in (0, 1):
            source = pl.ds(pl.multiple_of(gate * lanes + block * rows_each, rows_each), rows_each)
            gw_ref[spot, gate * rows_each : (gate + 1) * rows_each, :] = gw[source, :]
    gc[steps : steps + 3] = from_segment(gc[0:3], place, True)
    taps = [prm_ref[k : k + 1, :] for k in range(4)]

    def conv_step(index, sums):
        at = index * AT_ONCE
        here = gc[pl.ds(at, AT_ONCE)]
        total = taps[0] * here
        sums = [sums[0] + fold(here), sums[1] + fold(here * xs[pl.ds(at + 3, AT_ONCE)])] + list(sums[2:])
        for k in (1, 2, 3):
            total = total + taps[k] * (gc[pl.ds(at + k, AT_ONCE)] * wide_mask(mask_ref, k - 1, at + k, AT_ONCE))
            masked = here * wide_mask(mask_ref, k - 1, at, AT_ONCE)
            sums[k + 1] = sums[k + 1] + fold(masked * xs[pl.ds(at + 3 - k, AT_ONCE)])
        us[pl.ds(at, AT_ONCE)] = total
        return tuple(sums)

    sums = lax.fori_loop(0, steps // AT_ONCE, conv_step, (zero,) * 5)
    for index, value in ((0, sums[1]), (1, sums[2]), (2, sums[3]), (3, sums[4]), (4, sums[0]), (7, sum_log)):
        sum_ref[index : index + 1, :] = jnp.sum(value, axis=0, keepdims=True)
    sum_ref[5:6, :] = gate_sums[0:1, 0:lanes]
    sum_ref[6:7, :] = gate_sums[0:1, lanes:]
    in_rows(us, gx_own, gx_oth)
    in_rows(ys, gy_own, gy_oth)


def rec_specs(half, lanes):
    steps = half // SEGMENTS
    piece = pl.BlockSpec((half, lanes), lambda h: (0, h))
    stepped = pl.BlockSpec((steps, 2 * SEGMENTS, lanes), lambda h: (0, 0, h))
    mask = pl.BlockSpec((3, steps + 3, 2 * SEGMENTS, 128), lambda h: (0, 0, 0, 0))
    prm = pl.BlockSpec((8, lanes), lambda h: (0, h))
    gate = pl.BlockSpec((2, 1, lanes, lanes), lambda h: (0, h, 0, 0))
    return piece, stepped, mask, prm, gate


def rec_fwd(bx_own, bx_oth, by_own, by_oth, mask, prm, gates):
    half, width = bx_own.shape
    length, lanes, heads = 2 * half, gates.shape[2], gates.shape[1]
    steps, both = half // SEGMENTS, 2 * SEGMENTS
    piece, stepped, mask_spec, prm_spec, gate_spec = rec_specs(half, lanes)
    out = jax.ShapeDtypeStruct((half, width), BF16)
    kept = jax.ShapeDtypeStruct((steps, both, width), F32)
    return pl.pallas_call(
        rec_fwd_kernel,
        grid=(heads,),
        in_specs=[piece] * 4 + [mask_spec, prm_spec, gate_spec],
        out_specs=[piece] * 2 + [stepped] * 4,
        out_shape=[out, out, kept, kept, kept, jax.ShapeDtypeStruct((steps, both, width), BF16)],
        scratch_shapes=[
            pltpu.VMEM((steps + 3, both, lanes), F32),
            pltpu.VMEM((steps, both, lanes), F32),
            pltpu.VMEM((length, 2 * lanes), F32),
            pltpu.VMEM((steps, both, lanes), F32),
        ],
        compiler_params=pltpu.CompilerParams(vmem_limit_bytes=40 << 20),
        cost_estimate=pl.CostEstimate(
            flops=4 * length * width * lanes + 100 * length * width,
            bytes_accessed=26 * length * width,
            transcendentals=6 * length * width,
        ),
        name="rec_fwd",
    )(bx_own, bx_oth, by_own, by_oth, mask, prm, gates)


def rec_bwd(bx_own, bx_oth, by_own, by_oth, kept, up_own, up_oth, mask, prm, gates, count, cost):
    half, width = bx_own.shape
    length, lanes, heads = 2 * half, gates.shape[2], gates.shape[1]
    steps, both = half // SEGMENTS, 2 * SEGMENTS
    piece, stepped, mask_spec, prm_spec, gate_spec = rec_specs(half, lanes)
    block = pltpu.VMEM((steps, both, lanes), F32)
    padded = pltpu.VMEM((steps + 3, both, lanes), F32)
    return pl.pallas_call(
        functools.partial(rec_bwd_kernel, count, stage_bits(count, "X" in CROSSED)),
        grid=(heads,),
        in_specs=[piece] * 4 + [stepped] * 4 + [piece] * 2 + [mask_spec, prm_spec, gate_spec],
        out_specs=[piece] * 4 + [pl.BlockSpec((count, 2 * lanes // count, lanes), lambda h: (0, 0, h)), prm_spec],
        out_shape=[jax.ShapeDtypeStruct((half, width), BF16)] * 4
        + [
            jax.ShapeDtypeStruct((count, 2 * lanes // count, width), BF16),
            jax.ShapeDtypeStruct((8, width), F32),
        ],
        scratch_shapes=[padded]
        + [block] * 8
        + [padded, pltpu.VMEM((length, 2 * lanes), BF16), pltpu.VMEM((2 * lanes, lanes), BF16)],
        compiler_params=pltpu.CompilerParams(vmem_limit_bytes=52 << 20),
        cost_estimate=pl.CostEstimate(
            flops=int(cost * (8 * length * width * lanes + 150 * length * width)),
            bytes_accessed=int(cost * 34 * length * width),
            transcendentals=int(cost * 4 * length * width),
        ),
        name="rec_bwd",
    )(bx_own, bx_oth, by_own, by_oth, *kept, up_own, up_oth, mask, prm, gates)


def stage_bits(count, crossed=False):
    bits = [1 << bit for bit in range(count.bit_length() - 1)]
    return [bits[0], bits[2], bits[1]] + bits[3:] if crossed else bits


def block_at(place, bits):
    return sum(bit for step, bit in enumerate(bits) if (place >> (len(bits) - 1 - step)) & 1)


def block_from(me, place, bits):
    relative = block_at(place, bits)
    block = 0
    for bit in bits:
        mine = lax.rem(me // bit, 2)
        block = block + bit * (1 - mine if relative & bit else mine)
    return block


def arrange_kernel(bits, first, second, first_out, second_out):
    @pl.when(pl.program_id(0) == 0)
    def _():
        arranged(first, first_out, bits)

    @pl.when(pl.program_id(0) == 1)
    def _():
        arranged(second, second_out, bits)


def arrange(first, second, bits):
    whole = pl.BlockSpec(first.shape, lambda i: (0, 0))
    shape = jax.ShapeDtypeStruct(first.shape, first.dtype)
    return pl.pallas_call(
        functools.partial(arrange_kernel, bits),
        grid=(2,),
        in_specs=[whole, whole],
        out_specs=[whole, whole],
        out_shape=[shape, shape],
        compiler_params=pltpu.CompilerParams(vmem_limit_bytes=24 << 20),
        cost_estimate=pl.CostEstimate(flops=0, bytes_accessed=12 * first.size, transcendentals=0),
        name="arrange",
    )(first, second)


def weight_grad_kernel(more, own_a, own_b, oth_a, oth_b, right_own, right_oth, *rest):
    extra, (sent_next, kept, staged, landed, send_sem, recv_sem) = rest[:-6], rest[-6:]
    step = pl.program_id(0)
    me = lax.axis_index("dp")
    partner = {"dp": me + 1 - 2 * lax.rem(me, 2)}

    @pl.when(step == 0)
    def _():
        barrier = pltpu.get_barrier_semaphore()
        pl.semaphore_signal(barrier, inc=1, device_id=partner, device_id_type=MESH)
        pl.semaphore_wait(barrier, 1)

    def copy(tile):
        return pltpu.make_async_remote_copy(
            src_ref=staged.at[tile],
            dst_ref=landed.at[tile],
            send_sem=send_sem.at[tile],
            recv_sem=recv_sem.at[tile],
            device_id=partner,
            device_id_type=MESH,
        )

    left_own = jnp.concatenate([own_a[...], own_b[...]], axis=1)
    left_oth = jnp.concatenate([oth_a[...], oth_b[...]], axis=1)
    total = matmul_left(left_own, right_own[...]) + matmul_left(left_oth, right_oth[...])

    def pieces():
        if not more:
            return [(slice(0, total.shape[0]), total)]
        out = []
        for block in range(total.shape[0] // 128):
            first = block * (128 + more)
            out.append((slice(first, first + 128), total[block * 128 : (block + 1) * 128]))
            out.append((slice(first + 128, first + 128 + more), extra[0][block].astype(F32)))
        return out

    @pl.when(step < 2)
    def _():
        for rows, value in pieces():
            staged[step, rows, :] = value.astype(BF16)
        copy(step).start()

    def finish(tile, into):
        copy(tile).wait_recv()
        for rows, value in pieces():
            into[rows, :] = (value + landed[tile, rows, :].astype(F32)).astype(BF16)

    @pl.when(step == 2)
    def _():
        finish(0, sent_next)

    @pl.when(step == 3)
    def _():
        finish(1, kept)
        for tile in range(2):
            copy(tile).wait_send()


def weight_grad(left_own, left_oth, right_own, right_oth, crossed, cost, extra=None):
    half, cols = right_own.shape
    rows = left_own.shape[1] // 4
    more = 0 if extra is None else extra.shape[1]
    height = rows + rows // 128 * more
    out = pltpu.HBM((height, cols), BF16)

    def columns(part):
        def index(i):
            quarter = 3 - i
            return 0, (quarter // 2 * 4 + part * 2 + lax.rem(quarter, 2) if crossed else quarter * 2 + part)

        return pl.BlockSpec((half, rows // 2), index)

    right = pl.BlockSpec((half, cols), lambda i: (0, 0))
    whole = pl.BlockSpec((height, cols), lambda i: (0, 0))
    specs = [columns(0), columns(1), columns(0), columns(1), right, right]
    args = [left_own, left_own, left_oth, left_oth, right_own, right_oth]
    if more:
        specs.append(pl.BlockSpec((rows // 128, more, cols), lambda i: (3 - i, 0, 0)))
        args.append(extra)
    return pl.pallas_call(
        functools.partial(weight_grad_kernel, more),
        grid=(4,),
        in_specs=specs,
        out_specs=[whole, whole],
        out_shape=[out, out],
        scratch_shapes=[
            pltpu.VMEM((2, height, cols), BF16),
            pltpu.VMEM((2, height, cols), BF16),
            pltpu.SemaphoreType.DMA((2,)),
            pltpu.SemaphoreType.DMA((2,)),
        ],
        compiler_params=pltpu.CompilerParams(
            collective_id=4 * bool(more) + 2 * (cols > 2048) + crossed, has_side_effects=True, vmem_limit_bytes=60 << 20
        ),
        cost_estimate=pl.CostEstimate(
            flops=int(cost * 16 * half * rows * cols), bytes_accessed=int(cost * 16 * half * cols), transcendentals=0
        ),
        name="weight_grad",
    )(*args)


ROWS = 64


def arranged(source, into, bits):
    me = lax.axis_index("dp")
    count = 1 << len(bits)
    cols = source.shape[1] // count
    for place in range(count):
        block = pl.ds(pl.multiple_of(block_from(me, place, bits) * cols, cols), cols)
        into[:, place * cols : (place + 1) * cols] = source[:, block]


def feed_kernel(bits, sub, tokens, part, other, gain, grad_hidden, w_gate, w_up, middle, cols, hidden, grad_gate, grad_up, normed):
    @pl.when(pl.program_id(0) == 0)
    def _():
        def rows_step(index, _):
            rows = pl.ds(pl.multiple_of(index * ROWS, ROWS), ROWS)
            total = tokens[rows, :].astype(F32) + (part[rows, :].astype(F32) + other[rows, :].astype(F32))
            middle[rows, :] = total
            scale = lax.rsqrt(jnp.mean(total * total, axis=-1, keepdims=True) + EPS)
            normed[rows, :] = (total * scale * gain[...]).astype(BF16)
            return 0

        lax.fori_loop(0, tokens.shape[0] // ROWS, rows_step, 0)
        arranged(normed, cols, bits)

    for start in range(0, w_gate.shape[1], sub):
        part_cols = slice(start, start + sub)
        gate = jnp.dot(normed[...], w_gate[:, part_cols], preferred_element_type=F32)
        up = jnp.dot(normed[...], w_up[:, part_cols], preferred_element_type=F32)
        squared = gate * gate
        tanh = jnp.tanh(GELU_A * gate * (1.0 + GELU_B * squared))
        lift = 0.5 + 0.5 * tanh
        slope = lift + gate * (1.0 - tanh * tanh) * (0.5 * GELU_A + (1.5 * GELU_A * GELU_B) * squared)
        gelu = gate * lift
        back = grad_hidden[:, part_cols].astype(F32)
        hidden[:, part_cols] = (gelu * up).astype(BF16)
        grad_gate[:, part_cols] = (back * up * slope).astype(BF16)
        grad_up[:, part_cols] = (back * gelu).astype(BF16)


def feed(tokens, part, other, gain, grad_hidden, w_gate, w_up, bits, wide=768, sub=768):
    rows, model = tokens.shape
    cols = w_gate.shape[1]
    whole = pl.BlockSpec((rows, model), lambda n: (0, 0))
    piece = pl.BlockSpec((rows, wide), lambda n: (0, n))
    weight = pl.BlockSpec((model, wide), lambda n: (0, n))
    out = jax.ShapeDtypeStruct((rows, cols), BF16)
    return pl.pallas_call(
        functools.partial(feed_kernel, bits, sub),
        grid=(cols // wide,),
        in_specs=[whole] * 3 + [pl.BlockSpec((1, model), lambda n: (0, 0)), piece, weight, weight],
        out_specs=[whole, whole, piece, piece, piece],
        out_shape=[jax.ShapeDtypeStruct((rows, model), F32), jax.ShapeDtypeStruct((rows, model), BF16), out, out, out],
        scratch_shapes=[pltpu.VMEM((rows, model), BF16)],
        compiler_params=pltpu.CompilerParams(vmem_limit_bytes=56 << 20),
        cost_estimate=pl.CostEstimate(
            flops=4 * rows * model * cols, bytes_accessed=4 * model * cols + 12 * rows * cols, transcendentals=rows * cols
        ),
        name="feed",
    )(tokens, part, other, gain, grad_hidden, w_gate, w_up)


def pull_kernel(bits, middle, back, other, cot, gain, weight, grad, cols, into, rec):
    @pl.when(pl.program_id(0) == 0)
    def _():
        def rows_step(index, _):
            rows = pl.ds(pl.multiple_of(index * ROWS, ROWS), ROWS)
            values = middle[rows, :]
            scale = lax.rsqrt(jnp.mean(values * values, axis=-1, keepdims=True) + EPS)
            lifted = gain[...] * (back[rows, :].astype(F32) + other[rows, :].astype(F32))
            pulled = jnp.mean(values * lifted, axis=-1, keepdims=True)
            total = cot[rows, :].astype(F32) + (scale * lifted - values * (scale * scale * scale * pulled))
            grad[rows, :] = total
            rec[rows, :] = total.astype(BF16)
            return 0

        lax.fori_loop(0, middle.shape[0] // ROWS, rows_step, 0)
        arranged(rec, cols, bits)

    into[...] = matmul_right(rec[...], weight[...])


def pull(middle, back, other, cot, gain, weight, bits, cost, wide=640):
    rows, model = middle.shape
    cols = weight.shape[0]
    wide = wide if cols % wide == 0 else cols
    whole = pl.BlockSpec((rows, model), lambda n: (0, 0))
    return pl.pallas_call(
        functools.partial(pull_kernel, bits),
        grid=(cols // wide,),
        in_specs=[whole] * 4 + [pl.BlockSpec((1, model), lambda n: (0, 0)), pl.BlockSpec((wide, model), lambda n: (n, 0))],
        out_specs=[whole, whole, pl.BlockSpec((rows, wide), lambda n: (0, n))],
        out_shape=[
            jax.ShapeDtypeStruct((rows, model), F32),
            jax.ShapeDtypeStruct((rows, model), BF16),
            jax.ShapeDtypeStruct((rows, cols), F32),
        ],
        scratch_shapes=[pltpu.VMEM((rows, model), BF16)],
        compiler_params=pltpu.CompilerParams(vmem_limit_bytes=56 << 20),
        cost_estimate=pl.CostEstimate(
            flops=int(cost * 2 * rows * model * cols),
            bytes_accessed=int(cost * (16 * rows * model + 4 * rows * cols)),
            transcendentals=0,
        ),
        name="pull",
    )(middle, back, other, cot, gain, weight)


def two_back_kernel(first, first_w, second, second_w, out):
    out[...] = (matmul_right(first[...], first_w[...]) + matmul_right(second[...], second_w[...])).astype(BF16)


def two_back(first, first_w, second, second_w, cost=1.0):
    rows, depth = first.shape
    cols = first_w.shape[0]
    step = 512
    left = pl.BlockSpec((rows, depth), lambda n: (0, 0))
    right = pl.BlockSpec((step, depth), lambda n: (n, 0))
    return pl.pallas_call(
        two_back_kernel,
        grid=(cols // step,),
        in_specs=[left, right, left, right],
        out_specs=pl.BlockSpec((rows, step), lambda n: (0, n)),
        out_shape=jax.ShapeDtypeStruct((rows, cols), BF16),
        compiler_params=pltpu.CompilerParams(vmem_limit_bytes=48 << 20),
        cost_estimate=pl.CostEstimate(
            flops=int(cost * 4 * rows * depth * cols), bytes_accessed=int(cost * 4 * depth * (rows + cols)), transcendentals=0
        ),
        name="two_back",
    )(first, first_w, second, second_w)


def swap(value):
    return lax.ppermute(value, "tp", [(0, 1), (1, 0)])


def flip(value, bit):
    count = lax.axis_size("dp")
    return lax.ppermute(value, "dp", [(source, source ^ bit) for source in range(count)])


def halve_kernel(keep_low, keep_high, received_low, received_high, kept, sent):
    kept[...] = (keep_low[...].astype(F32) + received_low[...].astype(F32)).astype(BF16)
    sent[...] = (keep_high[...].astype(F32) + received_high[...].astype(F32)).astype(BF16)


def halve(keep, received, cost):
    rows, cols = keep.shape
    block = rows // 4 if rows > 512 else rows // 2
    steps = rows // 2 // block
    low = pl.BlockSpec((block, cols), lambda i: (i, 0))
    high = pl.BlockSpec((block, cols), lambda i: (i + steps, 0))
    return pl.pallas_call(
        halve_kernel,
        grid=(steps,),
        in_specs=[low, high, low, high],
        out_specs=[low, low],
        out_shape=[pltpu.HBM((rows // 2, cols), BF16)] * 2,
        compiler_params=pltpu.CompilerParams(vmem_limit_bytes=32 << 20),
        cost_estimate=pl.CostEstimate(flops=0, bytes_accessed=int(cost * 6 * rows * cols), transcendentals=0),
        name="halve",
    )(keep, keep, received, received)


class Reduction:
    def __init__(self, left, right, count, crossed, cost, extra=None):
        self.bits = stage_bits(count, crossed)[1:]
        sent, self.keep = weight_grad(*left, *right, crossed, cost, extra)
        self.pass_on(sent)

    def pass_on(self, sent):
        self.received = flip(sent, self.bits.pop(0))

    def step(self, cost, *others):
        self.keep, sent = halve(self.keep, after(self.received, *others), cost)
        self.pass_on(sent)
        return sent

    def total(self, *others):
        while self.bits:
            self.step(1.0, *others)
        return self.keep.astype(F32) + after(self.received, *others).astype(F32)


def after(value, *others):
    return lax.optimization_barrier((value, *others))[0]


def norm_back(values, gain, grad):
    scale = lax.rsqrt(jnp.mean(values * values, axis=-1, keepdims=True) + EPS)
    lifted = gain * grad
    pull = jnp.mean(values * lifted, axis=-1, keepdims=True)
    return scale * lifted - values * (scale * scale * scale * pull)


def local_channels(
    layer_in, cotangent, resets, norm_gains, w_x, w_y, conv_w, lru_bias, a_param, gate_blocks, w_out, w_gate, w_up, w_down,
):
    place = lax.axis_index("tp")
    me = lax.axis_index("dp")
    count = lax.axis_size("dp")
    bits = stage_bits(count)
    width = w_x.shape[1]
    full_width = conv_w.shape[1]
    heads = gate_blocks.shape[1] // 2
    model = norm_gains.shape[1]

    own_in, own_cot = layer_in[0], cotangent[0]
    oth_in = swap(own_in)
    oth_resets = swap(resets[0])
    oth_cot = swap(own_cot)
    normed_own = rms_scale(own_in.astype(F32), norm_gains[0]).astype(BF16)
    bx_own = matmul(normed_own, w_x).astype(BF16)
    by_own = matmul(normed_own, w_y)

    first_place = place == 0
    in_time = jnp.where(first_place, resets[0], oth_resets), jnp.where(first_place, oth_resets, resets[0])
    keep = 1.0 - jnp.concatenate(in_time).astype(F32)
    keep_1 = jnp.concatenate([jnp.ones((1,), F32), keep[:-1]])
    keep_2 = jnp.concatenate([jnp.ones((1,), F32), keep_1[:-1]])
    valid = jnp.stack([keep, keep * keep_1, keep * keep_1 * keep_2]).reshape(3, 2, SEGMENTS, -1)
    valid = jnp.where(first_place, valid, valid[:, ::-1]).reshape(3, 2 * SEGMENTS, -1)
    later = jnp.concatenate([valid[:, 1:, :3], valid[:, :1, :3]], axis=1)
    mask = jnp.swapaxes(jnp.concatenate([valid, later], axis=2), 1, 2)
    mask = jnp.broadcast_to(mask[..., None], mask.shape + (128,))
    table = jnp.concatenate([conv_w, lru_bias, -8.0 * jax.nn.softplus(a_param)[None]], axis=0)
    prm = lax.dynamic_slice(table, (0, place * width), (8, width))
    gates = lax.dynamic_slice_in_dim(gate_blocks, place * heads, heads, axis=1)

    gh_own = matmul_right(after(own_cot, bx_own, by_own), w_down)
    normed_oth = rms_scale(after(oth_in, gh_own).astype(F32), norm_gains[0]).astype(BF16)
    bx_oth = matmul(normed_oth, w_x).astype(BF16)
    by_oth = matmul(normed_oth, w_y)
    gated_own, gated_oth, *kept = rec_fwd(bx_own, bx_oth, by_own, by_oth, mask, prm, gates)

    part_oth = matmul(gated_oth, w_out).astype(BF16)
    swap_own = swap(part_oth)
    part_own = matmul(after(gated_own, part_oth), w_out).astype(BF16)
    swap_oth = swap(part_own)
    gh_oth = matmul_right(after(oth_cot, part_own), w_down)
    cot_cols = arrange(after(own_cot, gh_oth), oth_cot, bits)
    normed_cols = arrange(after(normed_own, cot_cols[0]), normed_oth, bits)
    gains = norm_gains[1:2]

    middle_own, two_own, hidden_own, gg_own, gu_own = feed(
        own_in, part_own, after(swap_own, normed_cols[0]), gains, gh_own, w_gate, w_up, bits
    )
    back_own = two_back(gg_own, w_gate, gu_own, w_up)
    back_own_swapped = swap(back_own)
    middle_oth, two_oth, hidden_oth, gg_oth, gu_oth = feed(
        oth_in, part_oth, after(swap_oth, back_own), gains, gh_oth, w_gate, w_up, bits
    )
    sums_over = {}
    at = {"done": hidden_oth}

    def reduce_kernel(name, letter, left, right, extra=None):
        left = (after(left[0], at["done"]), left[1])
        sums_over[letter] = Reduction(left, right, count, letter in CROSSED, COSTS.get(name, 1.0), extra)
        return sums_over[letter].keep

    def back_other(cost):
        at["back"] = two_back(after(gg_oth, at["done"]), w_gate, gu_oth, w_up, cost)
        at["back_swapped"] = swap(at["back"])
        return at["back"]

    def pull_other(cost):
        other = after(back_own_swapped, at["done"])
        _, at["rec_oth"], at["into_oth"] = pull(middle_oth, at["back"], other, oth_cot, gains, w_out, bits, cost)
        return at["into_oth"]

    def pull_own(cost):
        other = after(at["back_swapped"], at["done"])
        at["grad_own"], at["rec_own"], at["into_own"] = pull(middle_own, back_own, other, own_cot, gains, w_out, bits, cost)
        return at["into_own"]

    def recurrence(cost):
        into = after(at["into_own"], at["done"]), at["into_oth"]
        *grads, gate_sums, sums = rec_bwd(bx_own, bx_oth, by_own, by_oth, kept, *into, mask, prm, gates, count, cost)
        at["gx"], at["gy"] = grads[0:2], grads[2:4]
        row = jnp.arange(8)[:, None] == 7
        slopes = -8.0 * lax.dynamic_slice(jax.nn.sigmoid(a_param), (place * width,), (width,))
        sums = jnp.swapaxes(jnp.where(row, sums * slopes, sums).reshape(8, count // 2, each), 0, 1)
        order = [block_at(spot, stage_bits(count, "X" in CROSSED)) for spot in range(count)]
        chosen = jnp.bitwise_xor(jnp.array(order), me)[:, None] % (count // 2) == jnp.arange(count // 2)[None, :]
        sums = matmul(chosen.astype(BF16), sums.astype(BF16).reshape(count // 2, -1)).reshape(count, 8, each)
        sums = jnp.pad(sums.astype(BF16), ((0, 0), (0, 0), (0, width - each)))
        at["extra"] = jnp.concatenate([gate_sums, sums], axis=1)
        return grads[0]

    def rec_rows(index):
        def run(cost):
            name = ("rec_keep", "rec_send")[index]
            at[name] = two_back(after(at["gx"][index], at["done"]), w_x, at["gy"][index], w_y, cost)
            if index == 1:
                at["rec_swapped"] = swap(at[name])
            return at[name]

        return run

    def out_other(cost):
        sent = matmul(after(hidden_oth, at["done"]), w_down).astype(BF16)
        at["out_swapped"] = swap(sent)
        return sent

    def out_own(cost):
        at["out_keep"] = matmul(after(hidden_own, at["done"]), w_down).astype(BF16)
        return at["out_keep"]

    def to_inputs(cost):
        grad_normed = at["rec_keep"].astype(F32) + after(at["rec_swapped"], at["done"]).astype(F32)
        at["input_grad"] = at["grad_own"] + norm_back(own_in.astype(F32), norm_gains[0], grad_normed)
        return at["input_grad"]

    def to_outputs(cost):
        total = middle_own + at["out_keep"].astype(F32) + after(at["out_swapped"], at["done"]).astype(F32)
        at["layer_out"] = total.astype(BF16)
        return at["layer_out"]

    def swap_blocks(cost):
        at["mine"] = after(grads["X"][block:], at["done"]).astype(BF16)
        at["others"] = swap(at["mine"])
        return at["others"]

    each = full_width // count
    block = model // count

    def gain_grad(gain, *pairs):
        weights = sum(
            jnp.sum(lax.dynamic_slice_in_dim(weight, me * block, block, axis=0).astype(F32) * grad, axis=1)
            for weight, grad in pairs
        )
        return weights / lax.dynamic_slice_in_dim(gain, me * block, block, axis=0)

    def sum_gains(cost):
        first = gain_grad(norm_gains[0], (w_x, grads["X"][:block]), (w_y, grads["Y"]))
        second = gain_grad(norm_gains[1], (w_gate, grads["G"]), (w_up, grads["U"]))
        gains = after(jnp.stack([first, second]), at["done"])
        at["gains"] = gains + swap(gains)
        return gains

    steps = {
        "DK": lambda cost: reduce_kernel("DK", "D", cot_cols, (hidden_own, hidden_oth)),
        "GK": lambda cost: reduce_kernel("GK", "G", (two_own, two_oth), (gg_own, gg_oth)),
        "UK": lambda cost: reduce_kernel("UK", "U", (two_own, two_oth), (gu_own, gu_oth)),
        "OUT": lambda cost: reduce_kernel("OUT", "O", (at["rec_own"], at["rec_oth"]), (gated_own, gated_oth)),
        "X": lambda cost: reduce_kernel("X", "X", normed_cols, at["gx"], at["extra"]),
        "Y": lambda cost: reduce_kernel("Y", "Y", normed_cols, at["gy"]),
        "B2": back_other,
        "P2": pull_other,
        "P1": pull_own,
        "RB": recurrence,
        "RS": rec_rows(1),
        "RK": rec_rows(0),
        "OS": out_other,
        "OK": out_own,
        "IG": to_inputs,
        "LO": to_outputs,
        "SW": swap_blocks,
        "GN": sum_gains,
    }
    grads = {}
    for name in ORDER:
        if name in steps:
            at["done"] = steps[name](COSTS.get(name, 1.0))
        elif name[1] == "t":
            total = sums_over[name[0]].total(at["done"])
            at["done"] = grads[name[0]] = total.T if name[0] in "DO" else total
        else:
            at["done"] = sums_over[name[0]].step(COSTS.get(name, 1.0), at["done"])
    mine, others, layer_out, input_grad = (at[name] for name in ("mine", "others", "layer_out", "input_grad"))
    down_grad, gate_grad, up_grad, out_grad, x_grad, y_grad = (grads[letter] for letter in "DGUOXY")
    x_grad = x_grad[:block]
    low, high = jnp.where(first_place, mine, others), jnp.where(first_place, others, mine)
    both = jnp.stack([low[:-8], high[:-8]]).astype(F32).reshape(2, 2, -1, heads, gates.shape[-1])
    block_sums = jnp.transpose(both, (1, 0, 3, 2, 4)).reshape(2, 2 * heads, -1, gates.shape[-1])
    small = jnp.where(me < count // 2, low[-8:], high[-8:])[:, :each].astype(F32)

    return (
        layer_out[None],
        input_grad[None],
        at["gains"],
        x_grad,
        y_grad,
        small[0:4],
        small[4:7],
        small[7],
        block_sums,
        out_grad,
        gate_grad,
        up_grad,
        down_grad,
    )


def from_behind(value, axis, steps):
    count = lax.axis_size(axis)
    first, last = (max(0, -steps), min(count, count - steps))
    return lax.ppermute(value, axis, [(source, source + steps) for source in range(first, last)])


def rms_scale(values, gain_vec):
    return values * lax.rsqrt(jnp.mean(values * values, axis=-1, keepdims=True) + EPS) * gain_vec


def gelu_product(gate_val, up_val):
    return jax.nn.gelu(gate_val, approximate=True) * up_val


def lru_terms(conv_out, gate_in, gate_rate, a_param, starts):
    keep_mask = 1.0 - starts
    input_gate = jax.nn.sigmoid(gate_in)
    rate_gate = jax.nn.sigmoid(gate_rate)
    log_decay = -8.0 * rate_gate * jax.nn.softplus(a_param)
    scaling = starts + keep_mask * jnp.sqrt(-jnp.expm1(2.0 * log_decay))
    return (jnp.exp(log_decay) * keep_mask, conv_out * input_gate * scaling)


def matmul(first_mat, second_mat):
    return jnp.dot(first_mat, second_mat, preferred_element_type=jnp.float32)


def matmul_left(first_mat, second_mat):
    return lax.dot_general(
        first_mat, second_mat, (((0,), (0,)), ((), ())), preferred_element_type=jnp.float32
    )


def matmul_right(first_mat, second_mat):
    return lax.dot_general(
        first_mat, second_mat, (((1,), (1,)), ((), ())), preferred_element_type=jnp.float32
    )


def combine_state(first_item, second_item):
    return (first_item[0] * second_item[0], second_item[1] + second_item[0] * first_item[1])


def carry_across(coef_end, state_end, reverse):
    incoming = jnp.zeros_like(state_end)
    direction = -1 if reverse else 1
    for turn_index in range(lax.axis_size("tp") - 1):
        incoming = from_behind(state_end + coef_end * incoming, "tp", direction)
    return incoming


def local(
    layer_in,
    cotangent,
    resets,
    norm_gains,
    w_x,
    w_y,
    conv_w,
    lru_bias,
    a_param,
    gate_blocks,
    w_out,
    w_gate,
    w_up,
    w_down,
):
    inputs = layer_in[0].astype(jnp.float32)
    starts = resets[0].astype(jnp.float32)
    keep_mask = 1.0 - starts
    rim_size = conv_w.shape[0] - 1
    head_count = gate_blocks.shape[1]
    block_size = gate_blocks.shape[2]
    full_width = conv_w.shape[1]
    normed, norm_pull = jax.vjp(rms_scale, inputs, norm_gains[0])
    normed_low = normed.astype(jnp.bfloat16)
    proj_x, proj_y, proj_out = (
        lax.all_gather(w_x, "tp", axis=1, tiled=True),
        lax.all_gather(w_y, "tp", axis=1, tiled=True),
        lax.all_gather(w_out, "tp", axis=0, tiled=True),
    )
    rec_len = normed_low.shape[0]
    branch_x = matmul(normed_low, proj_x).astype(jnp.bfloat16)
    branch_y = matmul(normed_low, proj_y)
    rim_rows, rim_keep = from_behind(
        (branch_x[rec_len - rim_size :], keep_mask[rec_len - rim_size :].astype(jnp.bfloat16)),
        "tp",
        1,
    )
    padded_x = jnp.concatenate([rim_rows, branch_x], axis=0).astype(jnp.float32)
    padded_keep = jnp.concatenate([rim_keep.astype(jnp.float32), keep_mask])
    conv_sum = conv_w[0] * padded_x[rim_size:]
    valid_mask = keep_mask
    valid_list = []
    for offset in range(1, rim_size + 1):
        valid_list.append(valid_mask)
        conv_sum = (
            conv_sum
            + valid_mask[:, None]
            * conv_w[offset]
            * padded_x[rim_size - offset : rim_size - offset + rec_len]
        )
        valid_mask = valid_mask * padded_keep[rim_size - offset : rim_size - offset + rec_len]
    conv_out = (conv_sum + lru_bias[0]).astype(jnp.bfloat16)
    row_count = conv_out.shape[0]
    conv_blocks = conv_out.reshape(row_count, head_count, block_size)
    pre_rows = (
        jnp.einsum(
            "lhb,ghbc->glhc", conv_blocks, gate_blocks, preferred_element_type=jnp.float32
        ).reshape(2, row_count, full_width)
        + lru_bias[1:3][:, None, :]
    )
    gate_in = pre_rows[0]
    gate_rate = pre_rows[1]
    conv_float = conv_out.astype(jnp.float32)

    def lru_local(conv_in, in_pre, rate_pre, decay_in):
        return lru_terms(conv_in, in_pre, rate_pre, decay_in, starts[:, None])

    (decay_rate, pushed), lru_pull = jax.vjp(lru_local, conv_float, gate_in, gate_rate, a_param)
    decay_cum, local_states = lax.associative_scan(combine_state, (decay_rate, pushed), axis=0)
    incoming = carry_across(decay_cum[-1], local_states[-1], False)
    states = local_states + decay_cum * incoming
    gated_val, gated_pull = jax.vjp(gelu_product, branch_y, states)
    gated_low = gated_val.astype(jnp.bfloat16)
    recurrent = matmul(gated_low, proj_out)
    middle = inputs + recurrent
    normed_two, norm_two_pull = jax.vjp(rms_scale, middle, norm_gains[1])
    normed_two_low = normed_two.astype(jnp.bfloat16)
    group_rows = lax.all_gather(normed_two_low, "tp", axis=0, tiled=True)
    gate_val = matmul(group_rows, w_gate)
    up_val = matmul(group_rows, w_up)
    hidden_val, mlp_pull = jax.vjp(gelu_product, gate_val, up_val)
    hidden = hidden_val.astype(jnp.bfloat16)
    mlp_out = lax.psum_scatter(
        matmul(hidden, w_down).astype(jnp.bfloat16), "tp", scatter_dimension=0, tiled=True
    ).astype(jnp.float32)
    layer_out = (middle + mlp_out).astype(jnp.bfloat16)
    grad_out = cotangent[0].astype(jnp.float32)
    group_grad = lax.all_gather(cotangent[0], "tp", axis=0, tiled=True)
    w_down_grad = matmul_left(hidden, group_grad)
    grad_hidden = matmul_right(group_grad, w_down)
    grad_gate, grad_up = mlp_pull(grad_hidden)
    grad_gate = grad_gate.astype(jnp.bfloat16)
    grad_up = grad_up.astype(jnp.bfloat16)
    w_gate_grad = matmul_left(group_rows, grad_gate)
    w_up_grad = matmul_left(group_rows, grad_up)
    grad_normed_two = lax.psum_scatter(
        (matmul_right(grad_gate, w_gate) + matmul_right(grad_up, w_up)).astype(jnp.bfloat16),
        "tp",
        scatter_dimension=0,
        tiled=True,
    ).astype(jnp.float32)
    grad_middle, gain_two_grad = norm_two_pull(grad_normed_two)
    grad_middle = grad_middle + grad_out
    grad_rec = grad_middle.astype(jnp.bfloat16)
    grad_gated = matmul_right(grad_rec, proj_out)
    grad_branch_y, grad_direct = gated_pull(grad_gated)
    grad_branch_y = grad_branch_y.astype(jnp.bfloat16)
    decay_next = jnp.concatenate([decay_rate[1:], jnp.ones_like(decay_rate[:1])], axis=0)
    reach_back, local_grads = lax.associative_scan(
        combine_state, (decay_next, grad_direct), reverse=True, axis=0
    )
    outgoing = carry_across(decay_rate[0] * reach_back[0], decay_rate[0] * local_grads[0], True)
    state_grads = local_grads + reach_back * outgoing
    prior_states = jnp.concatenate([incoming[None], states[:-1]], axis=0)
    grad_conv, grad_in, grad_rate, a_local_grad = lru_pull(
        (state_grads * prior_states, state_grads)
    )
    grad_pre = jnp.stack([grad_in, grad_rate]).astype(jnp.bfloat16)
    pre_sums = jnp.sum(grad_pre.astype(jnp.float32), axis=1)
    pre_blocks = grad_pre.reshape(2, row_count, head_count, block_size)
    gate_blocks_grad = jnp.einsum(
        "lhb,glhc->ghbc", conv_blocks, pre_blocks, preferred_element_type=jnp.float32
    )
    gate_back = jnp.einsum(
        "glhc,ghbc->lhb", pre_blocks, gate_blocks, preferred_element_type=jnp.float32
    ).reshape(row_count, full_width)
    grad_conv = grad_conv + gate_back
    conv_w_rows = [jnp.sum(grad_conv * padded_x[rim_size:], axis=0)]
    grad_padded = (
        jnp.zeros((rec_len + rim_size, full_width), jnp.float32)
        .at[rim_size:]
        .add(conv_w[0] * grad_conv)
    )
    for offset in range(1, rim_size + 1):
        masked = valid_list[offset - 1][:, None] * grad_conv
        conv_w_rows.append(
            jnp.sum(masked * padded_x[rim_size - offset : rim_size - offset + rec_len], axis=0)
        )
        grad_padded = grad_padded.at[rim_size - offset : rim_size - offset + rec_len].add(
            conv_w[offset] * masked
        )
    returned = from_behind(grad_padded[:rim_size], "tp", -1)
    grad_x_branch = (
        grad_padded[rim_size:].at[rec_len - rim_size :].add(returned).astype(jnp.bfloat16)
    )
    conv_w_grad = jnp.stack(conv_w_rows)
    lru_bias_grad = jnp.concatenate([jnp.sum(grad_conv, axis=0)[None], pre_sums], axis=0)
    grad_normed = matmul_right(grad_x_branch, proj_x) + matmul_right(grad_branch_y, proj_y)
    grad_inputs, gain_one_grad = norm_pull(grad_normed)
    input_grad = grad_middle + grad_inputs
    w_x_grad, w_y_grad, w_out_grad = (
        lax.psum_scatter(
            matmul_left(normed_low, grad_x_branch).astype(jnp.bfloat16),
            "tp",
            scatter_dimension=1,
            tiled=True,
        ).astype(jnp.float32),
        lax.psum_scatter(
            matmul_left(normed_low, grad_branch_y).astype(jnp.bfloat16),
            "tp",
            scatter_dimension=1,
            tiled=True,
        ).astype(jnp.float32),
        lax.psum_scatter(
            matmul_left(gated_low, grad_rec).astype(jnp.bfloat16),
            "tp",
            scatter_dimension=0,
            tiled=True,
        ).astype(jnp.float32),
    )
    norm_gains_grad = jnp.stack([gain_one_grad, gain_two_grad])
    totals = (
        lax.psum_scatter(
            w_x_grad.astype(jnp.bfloat16), "dp", scatter_dimension=0, tiled=True
        ).astype(jnp.float32),
        lax.psum_scatter(
            w_y_grad.astype(jnp.bfloat16), "dp", scatter_dimension=0, tiled=True
        ).astype(jnp.float32),
        lax.psum_scatter(
            w_out_grad.astype(jnp.bfloat16), "dp", scatter_dimension=1, tiled=True
        ).astype(jnp.float32),
        lax.psum_scatter(
            w_gate_grad.astype(jnp.bfloat16), "dp", scatter_dimension=0, tiled=True
        ).astype(jnp.float32),
        lax.psum_scatter(
            w_up_grad.astype(jnp.bfloat16), "dp", scatter_dimension=0, tiled=True
        ).astype(jnp.float32),
        lax.psum_scatter(
            w_down_grad.astype(jnp.bfloat16), "dp", scatter_dimension=1, tiled=True
        ).astype(jnp.float32),
        lax.psum_scatter(
            norm_gains_grad.astype(jnp.bfloat16), "dp", scatter_dimension=1, tiled=True
        ).astype(jnp.float32),
        lax.psum_scatter(
            conv_w_grad.astype(jnp.bfloat16), "dp", scatter_dimension=1, tiled=True
        ).astype(jnp.float32),
        lax.psum_scatter(
            lru_bias_grad.astype(jnp.bfloat16), "dp", scatter_dimension=1, tiled=True
        ).astype(jnp.float32),
        lax.psum_scatter(
            a_local_grad.astype(jnp.bfloat16), "dp", scatter_dimension=0, tiled=True
        ).astype(jnp.float32),
        lax.psum_scatter(
            gate_blocks_grad.astype(jnp.bfloat16), "dp", scatter_dimension=2, tiled=True
        ).astype(jnp.float32),
    )
    reduced_small = (
        lax.psum(totals[6].astype(jnp.bfloat16), "tp").astype(jnp.float32),
        lax.psum(totals[7].astype(jnp.bfloat16), "tp").astype(jnp.float32),
        lax.psum(totals[8].astype(jnp.bfloat16), "tp").astype(jnp.float32),
        lax.psum(totals[9].astype(jnp.bfloat16), "tp").astype(jnp.float32),
        lax.psum(totals[10].astype(jnp.bfloat16), "tp").astype(jnp.float32),
    )
    return (
        layer_out[None],
        input_grad[None],
        reduced_small[0],
        totals[0],
        totals[1],
        reduced_small[1],
        reduced_small[2],
        reduced_small[3],
        reduced_small[4],
        totals[2],
        totals[3],
        totals[4],
        totals[5],
    )


def solution(mesh):
    rows, cols = mesh.shape["dp"], mesh.shape["tp"]
    by_channels = cols == 2 and rows >= 16 and rows & (rows - 1) == 0

    def step(*args):
        heads, model = args[9].shape[1], args[3].shape[1]
        fits = by_channels and heads % cols == 0 and model % (128 * rows) == 0
        return (local_channels if fits else local)(*args)

    return jax.shard_map(
        step,
        mesh=mesh,
        in_specs=(
            P("dp", "tp", None),
            P("dp", "tp", None),
            P("dp", "tp"),
            P(),
            P(None, "tp"),
            P(None, "tp"),
            P(),
            P(),
            P(),
            P(),
            P("tp", None),
            P(None, "tp"),
            P(None, "tp"),
            P("tp", None),
        ),
        out_specs=(
            P("dp", "tp", None),
            P("dp", "tp", None),
            P(None, "dp"),
            P("dp", "tp"),
            P("dp", "tp"),
            P(None, "dp"),
            P(None, "dp"),
            P("dp"),
            P(None, None, "dp", None),
            P("tp", "dp"),
            P("dp", "tp"),
            P("dp", "tp"),
            P("tp", "dp"),
        ),
        check_vma=False,
    )
```
